32 devices in a mesh: dp: 8 (over y, x, core), mp: 4 (over z).
Axes of the slice: x: 2, y: 2, z: 4, core: 2. Of those that a mesh axis runs over, the one named last changes fastest.
Arguments:
- frames: bfloat16 [4096, 1024], P(('dp', 'mp')), may hold values from -6 to 6
- codes_embed: bfloat16 [12288, 1024], P(('dp', 'mp')), may hold values from -6 to 6
- lengths: int32 [8, 8], P('dp'), may hold values from 1 to 384, 448 in all within a row
- cotangent: bfloat16 [12288, 1024], P(('dp', 'mp')), may hold values from -6 to 6
- frame_gain_a: bfloat16 [1024], replicated, may hold values from 0.099609375 to 1.8984375
- frame_qkv: bfloat16 [3, 1024, 1024], P(None, None, 'mp'), may hold values from -0.1875 to 0.1875
- frame_wout: bfloat16 [1024, 1024], P('mp'), may hold values from -1.5 to 1.5
- frame_gain_b: bfloat16 [1024], replicated, may hold values from 0.099609375 to 1.8984375
- frame_wup: bfloat16 [1024, 4096], P(None, 'mp'), may hold values from -0.1875 to 0.1875
- frame_bup: bfloat16 [4096], P('mp'), may hold values from -3 to 3
- frame_wdown: bfloat16 [4096, 1024], P('mp'), may hold values from -0.09375 to 0.09375
- frame_bdown: bfloat16 [1024], replicated, may hold values from -3 to 3
- token_gain_a: bfloat16 [1024], replicated, may hold values from 0.099609375 to 1.8984375
- token_qkv: bfloat16 [3, 1024, 1024], P(None, None, 'mp'), may hold values from -0.1875 to 0.1875
- token_wout: bfloat16 [1024, 1024], P('mp'), may hold values from -0.25 to 0.25
- token_gain_b: bfloat16 [1024], replicated, may hold values from 0.099609375 to 1.8984375
- token_wup: bfloat16 [1024, 4096], P(None, 'mp'), may hold values from -0.1875 to 0.1875
- token_bup: bfloat16 [4096], P('mp'), may hold values from -3 to 3
- token_wdown: bfloat16 [4096, 1024], P('mp'), may hold values from -0.09375 to 0.09375
- token_bdown: bfloat16 [1024], replicated, may hold values from -3 to 3
Outputs:
- output: bfloat16 [12288, 1024], P(('dp', 'mp'))
- frames_grad: float32 [4096, 1024], P(('dp', 'mp'))
- frame_gain_a_grad: float32 [1024], P(('dp', 'mp'))
- frame_qkv_grad: float32 [3, 1024, 1024], P(None, 'dp', 'mp')
- frame_wout_grad: float32 [1024, 1024], P('mp', 'dp')
- frame_gain_b_grad: float32 [1024], P(('dp', 'mp'))
- frame_wup_grad: float32 [1024, 4096], P('dp', 'mp')
- frame_bup_grad: float32 [4096], P(('dp', 'mp'))
- frame_wdown_grad: float32 [4096, 1024], P('mp', 'dp')
- frame_bdown_grad: float32 [1024], P(('dp', 'mp'))
- token_gain_a_grad: float32 [1024], P(('dp', 'mp'))
- token_qkv_grad: float32 [3, 1024, 1024], P(None, 'dp', 'mp')
- token_wout_grad: float32 [1024, 1024], P('mp', 'dp')
- token_gain_b_grad: float32 [1024], P(('dp', 'mp'))
- token_wup_grad: float32 [1024, 4096], P('dp', 'mp')
- token_bup_grad: float32 [4096], P(('dp', 'mp'))
- token_wdown_grad: float32 [4096, 1024], P('mp', 'dp')
- token_bdown_grad: float32 [1024], P(('dp', 'mp'))
The draws below stay inside these ranges and needn't reach their ends.
Inputs may be any that keep to these rules, and one draw needn't show every extreme that they name: Each row of lengths gives the frames of the items packed one after another into one group of 512 frames; frames after the row's total are padding.
All inputs are finite; a program needn't handle non-finite values.
Results may differ from the reference program's by a relative error of at most 0.023.
Values may be sent and summed in bfloat16 or wider, within the bound.
No kernel may reach another device: no remote copies, remote signals or barrier semaphores. Data moves between devices by JAX's collectives and lax.ppermute only.
A program may use at most 192 MiB of HBM per device.

```python
import math
import jax
import jax.numpy as jnp
import numpy as np
from jax import lax

D = 1024
HD = 64
FF = 4096
F_DEV = 512
ITEMS = 8
FRAMES = 4096
TOKENS = 12288
N_DP = 8


def shard_levels(stream_key, dims, split, low, top_value):
    def one(axis_at, parts):
        heights = jax.random.uniform(jax.random.fold_in(jax.random.fold_in(stream_key, 6), axis_at), (parts,), jnp.float32, low / len(split), top_value / len(split))
        return jnp.repeat(jnp.exp(heights), dims[axis_at] // parts).reshape((-1,) + (1,) * (len(dims) - axis_at - 1))

    gain = one(*split[0])
    for cut in split[1:]:
        gain = gain * one(*cut)
    return gain


def split_up(number_of, total, most, slope):
    portions = [(1 << 20) // math.isqrt(standing ** slope) + 1 for standing in range(2, number_of + 1)]
    rest, given = total - most - (number_of - 1), [1] * (number_of - 1)
    while rest > 0:
        movable = [i for i in range(number_of - 1) if given[i] < most]
        mass, budget = sum([portions[i] for i in movable]), rest
        for i in movable:
            addition = min(most - given[i], max(1, budget * portions[i] // mass), rest)
            given[i] = given[i] + addition
            rest = rest - addition
    return np.array([most] + given)


def ragged_sizes(key, count, total, most, skew):
    if count == 2:
        one = jax.random.randint(key, (), max(1, total - most), min(most, total - 1) + 1)
        return jnp.stack([one, total - one])
    sizes = jnp.asarray(split_up(count, total, most, skew), jnp.int32)
    pairs = (count - 1) // 2
    source_of, sink = sizes[1:1 + 2 * pairs:2], sizes[2:2 + 2 * pairs:2]
    margin = jnp.minimum(source_of - 1, most - sink)
    moved = jax.random.randint(jax.random.fold_in(key, 1), (pairs,), 0, 1 << 20) % (margin + 1)
    sizes = sizes.at[1:1 + 2 * pairs:2].set(source_of - moved).at[2:2 + 2 * pairs:2].set(sink + moved)
    return sizes[jax.random.permutation(jax.random.fold_in(key, 2), count)]


def noise(key, shape, width, reach, shards=(), kind=jnp.bfloat16):
    loudness = shard_levels(key, shape, shards, -0.22, 0.18) if shards else 1.0
    entries = jax.random.normal(key, shape, jnp.float32) * width * loudness
    return jnp.minimum(jnp.maximum(entries, -reach), reach).astype(kind)


def setup_inputs(seed: int = 0) -> dict:
    arg_keys = jax.random.split(jax.random.key(seed), 21)
    frames = noise(arg_keys[0], (FRAMES, D), 1.0, 6.0, ((0, 32),))
    codes_embed = noise(arg_keys[1], (TOKENS, D), 1.0, 6.0, ((0, 32),))
    lengths = jax.vmap(lambda own: ragged_sizes(own, ITEMS, F_DEV - F_DEV // 8, 3 * F_DEV // 4, 2))(jax.random.split(arg_keys[2], N_DP)).reshape((N_DP, ITEMS)).astype(jnp.int32)
    cotangent = noise(arg_keys[3], (TOKENS, D), 1.0, 6.0, ((0, 32),))
    frame_gain_a = jnp.clip(1.0 + 0.18 * jax.random.normal(arg_keys[4], (D,), jnp.float32), 0.099609375, 1.8984375).astype(jnp.bfloat16)
    frame_qkv = noise(arg_keys[5], (3, D, D), D ** -0.5, 0.1875, ((2, 4),))
    frame_wout = noise(arg_keys[6], (D, D), (HD // 4) ** -0.5, 1.5, ((0, 4),))
    frame_gain_b = jnp.clip(1.0 + 0.18 * jax.random.normal(arg_keys[7], (D,), jnp.float32), 0.099609375, 1.8984375).astype(jnp.bfloat16)
    frame_wup = noise(arg_keys[8], (D, FF), D ** -0.5, 0.1875, ((1, 4),))
    frame_bup = noise(arg_keys[9], (FF,), 0.5, 3.0, ((0, 4),))
    frame_wdown = noise(arg_keys[10], (FF, D), FF ** -0.5, 0.09375, ((0, 4),))
    frame_bdown = noise(arg_keys[11], (D,), 0.5, 3.0)
    token_gain_a = jnp.clip(1.0 + 0.18 * jax.random.normal(arg_keys[12], (D,), jnp.float32), 0.099609375, 1.8984375).astype(jnp.bfloat16)
    token_qkv = noise(arg_keys[13], (3, D, D), D ** -0.5, 0.1875, ((2, 4),))
    token_wout = noise(arg_keys[14], (D, D), (D // 2) ** -0.5, 0.25, ((0, 4),))
    token_gain_b = jnp.clip(1.0 + 0.18 * jax.random.normal(arg_keys[15], (D,), jnp.float32), 0.099609375, 1.8984375).astype(jnp.bfloat16)
    token_wup = noise(arg_keys[16], (D, FF), D ** -0.5, 0.1875, ((1, 4),))
    token_bup = noise(arg_keys[17], (FF,), 0.5, 3.0, ((0, 4),))
    token_wdown = noise(arg_keys[18], (FF, D), FF ** -0.5, 0.09375, ((0, 4),))
    token_bdown = noise(arg_keys[19], (D,), 0.5, 3.0)
    return dict(frames=frames, codes_embed=codes_embed, lengths=lengths, cotangent=cotangent, frame_gain_a=frame_gain_a, frame_qkv=frame_qkv, frame_wout=frame_wout, frame_gain_b=frame_gain_b, frame_wup=frame_wup, frame_bup=frame_bup, frame_wdown=frame_wdown, frame_bdown=frame_bdown, token_gain_a=token_gain_a, token_qkv=token_qkv, token_wout=token_wout, token_gain_b=token_gain_b, token_wup=token_wup, token_bup=token_bup, token_wdown=token_wdown, token_bdown=token_bdown)


@jax.custom_vjp
def low(v):
    return lax.optimization_barrier(v.astype(jnp.bfloat16)).astype(jnp.float32)

@jax.custom_vjp
def low_back(v):
    return v

def low_keep(v):
    return (low(v), None)

def low_pass(kept, grad):
    return (grad,)

def back_keep(v):
    return (v, None)

def back_low(kept, grad):
    return (low(grad),)
low.defvjp(low_keep, low_pass)
low_back.defvjp(back_keep, back_low)
eps = 1e-05
highest = lax.Precision.HIGHEST

def normalize(stream, gain_vec):
    return stream * lax.rsqrt(lax.optimization_barrier(jnp.mean(stream * stream, axis=-1, keepdims=True)) + eps) * gain_vec

def segments(length_row, whole_rows):
    item_ends = jnp.cumsum(length_row, dtype=jnp.int32)
    positions = jnp.arange(whole_rows, dtype=jnp.int32)
    segment = lax.optimization_barrier(jnp.sum((positions[:, None] >= item_ends[None, :]).astype(jnp.int32), axis=1, dtype=jnp.int32))
    is_valid = positions < item_ends[-1]
    segment = jnp.where(is_valid, segment, positions + length_row.shape[0])
    return (segment, is_valid)

def frame_attention(qkv_rows, segment):
    whole_rows = qkv_rows.shape[1]
    head_count = qkv_rows.shape[2] // HD
    queries = qkv_rows[0].reshape(whole_rows, head_count, HD)
    key_rows = qkv_rows[1].reshape(whole_rows, head_count, HD)
    value_rows = qkv_rows[2].reshape(whole_rows, head_count, HD)
    block_rows = min(512, whole_rows)
    score_scale = 1.0 / math.sqrt(HD)
    positions = jnp.arange(whole_rows, dtype=jnp.int32)

    def one_block(first_row):
        query_block = lax.dynamic_slice_in_dim(queries, first_row, block_rows, 0)
        raw_scores = jnp.einsum('qhe,khe->hqk', query_block, key_rows, precision=highest) * score_scale
        query_pos = first_row + jnp.arange(block_rows, dtype=jnp.int32)
        query_seg = lax.dynamic_slice_in_dim(segment, first_row, block_rows, 0)
        allowed = (positions[None, :] <= query_pos[:, None]) & (segment[None, :] == query_seg[:, None])
        scores = jnp.where(allowed[None], low_back(raw_scores), -1e+30)
        attn_probs = low(jax.nn.softmax(scores, axis=-1))
        return low(low_back(jnp.einsum('hqk,khe->qhe', attn_probs, value_rows, precision=highest)))
    firsts = jnp.arange(whole_rows // block_rows, dtype=jnp.int32) * block_rows
    mixed_blocks = lax.map(jax.checkpoint(one_block), firsts)
    return mixed_blocks.reshape(whole_rows, head_count * HD)

def token_attention(qkv_rows):
    all_rows = qkv_rows.shape[1]
    frame_count = all_rows // 3
    head_count = qkv_rows.shape[2] // HD
    queries = qkv_rows[0].reshape(frame_count, 3, head_count, HD)
    key_rows = qkv_rows[1].reshape(frame_count, 3, head_count, HD)
    value_rows = qkv_rows[2].reshape(frame_count, 3, head_count, HD)
    score_scale = 1.0 / math.sqrt(HD)
    raw_scores = jnp.einsum('fphe,fqhe->fhpq', queries, key_rows, precision=highest) * score_scale
    places = jnp.arange(3, dtype=jnp.int32)
    allowed = places[None, :] <= places[:, None]
    scores = jnp.where(allowed, low_back(raw_scores), -1e+30)
    attn_probs = low(jax.nn.softmax(scores, axis=-1))
    mixed_rows = low(low_back(jnp.einsum('fhpq,fqhe->fphe', attn_probs, value_rows, precision=highest)))
    return mixed_rows.reshape(all_rows, head_count * HD)

def block(stream, params, attend):
    gain_a, w_qkv, w_out, gain_b, w_up, b_up, w_down, b_down = params
    normed_a = low(normalize(stream, gain_a))
    qkv_rows = low(low_back(jnp.einsum('rd,tde->tre', normed_a, w_qkv, precision=highest)))
    mixed_rows = attend(qkv_rows)
    middle = stream + low_back(jnp.dot(mixed_rows, w_out, precision=highest, preferred_element_type=jnp.float32))
    normed_b = low(normalize(middle, gain_b))
    hidden_pre = low_back(jnp.dot(normed_b, w_up, precision=highest, preferred_element_type=jnp.float32) + b_up)
    hidden = low(jax.nn.gelu(hidden_pre, approximate=True))
    return middle + low_back(jnp.dot(hidden, w_down, precision=highest, preferred_element_type=jnp.float32)) + b_down

def group_forward(frame_rows, embed_rows, length_row, frame_params, token_params):
    whole_rows = frame_rows.shape[0]
    segment, is_valid = segments(length_row, whole_rows)

    def frame_attend(qkv_rows):
        return frame_attention(qkv_rows, segment)
    frame_out = block(frame_rows, frame_params, frame_attend)
    token_in = jnp.repeat(frame_out, 3, axis=0) + embed_rows
    token_out = block(token_in, token_params, token_attention)
    return token_out * jnp.repeat(is_valid, 3).astype(jnp.float32)[:, None]

def reference(frames, codes_embed, lengths, cotangent, frame_gain_a, frame_qkv, frame_wout, frame_gain_b, frame_wup, frame_bup, frame_wdown, frame_bdown, token_gain_a, token_qkv, token_wout, token_gain_b, token_wup, token_bup, token_wdown, token_bdown):
    weights = (frame_gain_a, frame_qkv, frame_wout, frame_gain_b, frame_wup, frame_bup, frame_wdown, frame_bdown, token_gain_a, token_qkv, token_wout, token_gain_b, token_wup, token_bup, token_wdown, token_bdown)
    params32 = tuple((weight.astype(jnp.float32) for weight in weights))
    frames32 = frames.astype(jnp.float32).reshape(N_DP, F_DEV, D)
    embed32 = codes_embed.astype(jnp.float32).reshape(N_DP, 3 * F_DEV, D)

    def forward(frame_all, params):

        def one_group(inputs):
            return group_forward(inputs[0], inputs[1], inputs[2], params[:8], params[8:])
        return lax.map(jax.checkpoint(one_group), (frame_all, embed32, lengths))
    result, pull = jax.vjp(forward, frames32, params32)
    grad_frames, grads = pull(cotangent.astype(jnp.float32).reshape(N_DP, 3 * F_DEV, D))
    return (result.reshape(TOKENS, D).astype(jnp.bfloat16), grad_frames.reshape(FRAMES, D), grads[0], grads[1], grads[2], grads[3], grads[4], grads[5], grads[6], grads[7], grads[8], grads[9], grads[10], grads[11], grads[12], grads[13], grads[14], grads[15])
```

```python
import math

import jax
import jax.numpy as jnp
from jax import lax
from jax.sharding import PartitionSpec as P

HD = 64
eps = 1e-05
BF = jnp.bfloat16
F32 = jnp.float32


def normalize(stream, gain_vec):
    return stream * lax.rsqrt(jnp.mean(stream * stream, axis=-1, keepdims=True) + eps) * gain_vec


def activate(values):
    return jax.nn.gelu(values, approximate=True)


def dot_nt(a, b):
    return lax.dot_general(a, b, (((1,), (1,)), ((), ())), preferred_element_type=F32)


def dot_nn(a, b):
    return lax.dot_general(a, b, (((1,), (0,)), ((), ())), preferred_element_type=F32)


def dot_tn(a, b):
    return lax.dot_general(a, b, (((0,), (0,)), ((), ())), preferred_element_type=F32)


def gather_rows(rows):
    return lax.all_gather(rows, "mp", axis=0, tiled=True)


def scatter_rows(partial):
    return lax.psum_scatter(
        partial.astype(BF), "mp", scatter_dimension=0, tiled=True
    ).astype(F32)


def swap_dp(value, bit):
    size = lax.axis_size("dp")
    return lax.ppermute(value, "dp", [(i, i ^ bit) for i in range(size)])


def swap_mp(value, mask):
    size = lax.axis_size("mp")
    return lax.ppermute(value, "mp", [(i, i ^ mask) for i in range(size)])


def plane_bits():
    size = lax.axis_size("dp")
    bits = []
    bit = 2
    while bit < size:
        bits.append(bit)
        bit *= 2
    return bits


def gather_shards(piece):
    z = lax.axis_index("mp")
    near = swap_mp(piece, 1)
    far = swap_mp(piece, 2)
    inner = lax.ppermute(piece, "mp", [(1, 2), (2, 1)])
    outer = lax.ppermute(far, "mp", [(2, 3), (1, 0)])
    middle = (z == 1) | (z == 2)
    last = jnp.where(middle, inner, outer)
    return jnp.concatenate([near, far, last], axis=1)


def gather_plane(block, order):
    masks = [0]
    parts = [block]
    whole = block
    for bit in order:
        got = swap_dp(whole, bit)
        k = block.shape[1]
        parts = parts + [got[:, i * k : (i + 1) * k] for i in range(len(masks))]
        masks = masks + [m ^ bit for m in masks]
        if bit == order[-1]:
            ranked = sorted(range(len(masks)), key=lambda i: masks[i])
            whole = jnp.concatenate([parts[i] for i in ranked], axis=1)
        else:
            whole = jnp.concatenate(parts, axis=1)
    return whole


def own_piece(shard_rows):
    dp = lax.axis_size("dp")
    k = shard_rows.shape[1] // dp
    return lax.dynamic_slice_in_dim(shard_rows, lax.axis_index("dp") * k, k, 1)


def gather_weight(shard_rows, order):
    mine = gather_plane(gather_shards(own_piece(shard_rows)), order)
    other = swap_dp(mine, 1)
    return jnp.concatenate([shard_rows, mine, other], axis=1)


def by_xor(slots):
    me = lax.axis_index("dp")
    for bit in [1] + plane_bits():
        on = (me & bit) != 0
        slots = [jnp.where(on, slots[i ^ bit], slots[i]) for i in range(len(slots))]
    return slots


def gather_bias(bias):
    dp = lax.axis_size("dp")
    n = bias.shape[0]
    k = n // dp
    row = bias.reshape(1, 1, n)
    rest = gather_shards(row).reshape(3, dp, k)
    slots = by_xor([rest[:, i] for i in range(dp)])
    rest = jnp.stack(slots[0::2] + slots[1::2])
    return jnp.concatenate([bias, rest.reshape(3 * n)])


def d_blocks(rows):
    dp = lax.axis_size("dp")
    block = rows.shape[1] // dp
    view = by_xor([rows[:, i * block : (i + 1) * block] for i in range(dp)])
    return view[0::2], view[1::2]


def swap_masks(value, bit, segs):
    own, per, count = segs
    pieces = [value[:own]] if own else []
    shift = bit // 2
    for core in range(2):
        base = own + core * per * count
        for m in range(count):
            at = base + (m ^ shift) * per
            pieces.append(value[at : at + per])
    return jnp.concatenate(pieces, axis=0)


def scatter_plane(make, order, segs):
    bits = list(order)
    count = 1 << len(bits)
    masks = list(range(count))
    first = bits[0] // 2
    keep_masks = [m for m in masks if not m & first]
    send_masks = [m for m in masks if m & first]
    if len(bits) > 1:
        nxt = bits[1] // 2
        keep_masks = sorted(keep_masks, key=lambda m: (bool(m & nxt), m))
    send_masks = [m ^ first for m in keep_masks]
    send_masks = [m | first for m in send_masks]
    block_send = make(send_masks)
    block_keep = make(keep_masks)
    held = keep_masks
    got = swap_dp(block_send, bits[0])
    if segs is not None:
        got = swap_masks(got, bits[0], segs)
    total = block_keep.astype(F32) + got.astype(F32)
    for i, bit in enumerate(bits[1:], start=1):
        b = bit // 2
        width = total.shape[1] // len(held)
        low = [j for j, m in enumerate(held) if not m & b]
        high = [j for j, m in enumerate(held) if m & b]
        high = [next(j for j in high if held[j] == held[q] | b) for q in low]
        pick = lambda js: jnp.concatenate([total[:, j * width : (j + 1) * width] for j in js], axis=1)
        got = swap_dp(pick(high).astype(BF), bit)
        if segs is not None:
            got = swap_masks(got, bit, segs)
        total = pick(low) + got.astype(F32)
        held = [held[j] for j in low]
    return total


def scatter_shards(total, n):
    dp = lax.axis_size("dp")
    per = n // dp
    block = total.shape[1]
    rest = total[n:].reshape(2, dp // 2, 3, per, block).astype(BF)
    got = sum(
        swap_mp(rest[:, :, r - 1], r).astype(F32) for r in (1, 2, 3)
    )
    slots = by_xor([got[i & 1, i >> 1] for i in range(dp)])
    return total[:n] + jnp.concatenate(slots, axis=0)


def segments(lengths, whole_rows):
    count = lengths.shape[1]
    order = jnp.arange(count, dtype=jnp.int32)
    item_ends = jnp.sum(
        jnp.where(order[None, :] <= order[:, None], lengths[0][None, :], 0), axis=1, dtype=jnp.int32
    )
    positions = jnp.arange(whole_rows, dtype=jnp.int32)
    segment = jnp.sum(
        (positions[:, None] >= item_ends[None, :]).astype(jnp.int32), axis=1, dtype=jnp.int32
    )
    is_valid = positions < jnp.sum(lengths[0], dtype=jnp.int32)
    segment = jnp.where(is_valid, segment, positions + count)
    return (segment, is_valid)


def frame_allowed(segment):
    positions = jnp.arange(segment.shape[0], dtype=jnp.int32)
    return (positions[None, :] <= positions[:, None]) & (segment[None, :] == segment[:, None])


def split_heads(rows):
    return rows.reshape(rows.shape[0], rows.shape[1] // HD, HD)


def frame_forward(qkv_rows, segment):
    queries, key_rows, value_rows = (split_heads(qkv_rows[t]) for t in range(3))
    raw_scores = jnp.einsum("qhe,khe->hqk", queries, key_rows, preferred_element_type=F32) * (
        1.0 / math.sqrt(HD)
    )
    scores = jnp.where(frame_allowed(segment)[None], raw_scores, -1e30)
    top_score = jnp.max(scores, axis=-1, keepdims=True)
    exp_scores = jnp.exp(scores - top_score)
    exp_total = jnp.sum(exp_scores, axis=-1, keepdims=True)
    attn_probs = (exp_scores / exp_total).astype(BF)
    mixed = jnp.einsum("hqk,khe->qhe", attn_probs, value_rows, preferred_element_type=F32)
    log_total = top_score[:, :, 0] + jnp.log(exp_total[:, :, 0])
    return (mixed.astype(BF).reshape(qkv_rows.shape[1], -1), log_total)


def frame_backward(qkv_rows, log_total, grad_mixed, segment):
    queries, key_rows, value_rows = (split_heads(qkv_rows[t]) for t in range(3))
    grad_heads = split_heads(grad_mixed)
    scale = 1.0 / math.sqrt(HD)
    raw_scores = jnp.einsum("qhe,khe->hqk", queries, key_rows, preferred_element_type=F32) * scale
    scores = jnp.where(frame_allowed(segment)[None], raw_scores, -1e30)
    attn_probs = jnp.exp(scores - log_total[:, :, None])
    value_grad = jnp.einsum(
        "hqk,qhe->khe", attn_probs.astype(BF), grad_heads, preferred_element_type=F32
    )
    grad_probs = jnp.einsum("qhe,khe->hqk", grad_heads, value_rows, preferred_element_type=F32)
    row_delta = jnp.sum(attn_probs * grad_probs, axis=-1, keepdims=True)
    grad_scores = (attn_probs * (grad_probs - row_delta)).astype(BF)
    query_grad = jnp.einsum("hqk,khe->qhe", grad_scores, key_rows, preferred_element_type=F32) * scale
    key_grad = jnp.einsum("hqk,qhe->khe", grad_scores, queries, preferred_element_type=F32) * scale
    rows = qkv_rows.shape[1]
    return [g.reshape(rows, -1).astype(BF) for g in (query_grad, key_grad, value_grad)]


def frame_block_forward(stream, params, segment):
    gain_a, w_qkv, w_out, gain_b, w_up, b_up, w_down, b_down = params
    normed_a = normalize(stream, gain_a.astype(F32)).astype(BF)
    gathered_a = gather_rows(normed_a)
    qkv_rows = jnp.einsum(
        "rd,tde->tre", gathered_a, w_qkv, preferred_element_type=F32
    ).astype(BF)
    mixed_rows, log_total = frame_forward(qkv_rows, segment)
    middle = stream + scatter_rows(dot_nn(mixed_rows, w_out))
    normed_b = normalize(middle, gain_b.astype(F32)).astype(BF)
    gathered_b = gather_rows(normed_b)
    hidden_pre = dot_nn(gathered_b, w_up) + b_up.astype(F32)
    hidden = activate(hidden_pre).astype(BF)
    result = middle + scatter_rows(dot_nn(hidden, w_down)) + b_down.astype(F32)
    saved = (stream, gathered_a, qkv_rows, mixed_rows, log_total, middle, gathered_b, hidden_pre, hidden)
    return (result, saved)


def frame_scatter(left, right, order):
    same, cross = d_blocks(right)
    units = left.shape[1]
    give = dot_tn(left, jnp.concatenate(cross, axis=1)).astype(BF)
    hold = dot_tn(left, jnp.concatenate(same, axis=1))
    total = hold + swap_dp(give, 1).astype(F32)
    width = right.shape[1] // lax.axis_size("dp")

    def make(masks):
        return jnp.concatenate([total[:, m * width : (m + 1) * width] for m in masks], axis=1).astype(BF)

    return scatter_plane(make, order, None)


def frame_block_backward(grad_out, saved, params, segment):
    gain_a, w_qkv, w_out, gain_b, w_up, b_up, w_down, b_down = params
    stream, gathered_a, qkv_rows, mixed_rows, log_total, middle, gathered_b, hidden_pre, hidden = saved
    up_order = plane_bits()
    down_order = up_order[::-1]
    bias_down_grad = jnp.sum(grad_out, axis=0)
    gathered_down = gather_rows(grad_out.astype(BF))
    grad_hidden = dot_nt(gathered_down, w_down)
    grad_pre = jax.vjp(activate, hidden_pre)[1](grad_hidden)[0].astype(BF)
    bias_up_grad = jnp.sum(grad_pre.astype(F32), axis=0)
    grad_normed_b = scatter_rows(dot_nt(grad_pre, w_up))
    down_grad = frame_scatter(hidden, gathered_down, down_order)
    up_grad = frame_scatter(grad_pre, gathered_b, up_order)
    second_norm = jax.vjp(normalize, middle, gain_b.astype(F32))[1](grad_normed_b)
    grad_middle = grad_out + second_norm[0]
    gathered_mid = gather_rows(grad_middle.astype(BF))
    grad_mixed = dot_nt(gathered_mid, w_out).astype(BF)
    out_grad = frame_scatter(mixed_rows, gathered_mid, down_order)
    grad_qkv = frame_backward(qkv_rows, log_total, grad_mixed, segment)
    grad_all = jnp.concatenate(grad_qkv, axis=1)
    w_all = jnp.concatenate([w_qkv[0], w_qkv[1], w_qkv[2]], axis=1)
    grad_normed_a = scatter_rows(dot_nt(grad_all, w_all))
    qkv_grad = frame_scatter(grad_all, gathered_a, up_order)
    first_norm = jax.vjp(normalize, stream, gain_a.astype(F32))[1](grad_normed_a)
    grad_stream = grad_middle + first_norm[0]
    return (
        grad_stream,
        (qkv_grad, out_grad, up_grad, down_grad),
        (first_norm[1], second_norm[1], bias_up_grad, bias_down_grad),
    )


def head_table(features, own):
    at = jnp.arange(features, dtype=jnp.int32)
    shards = lax.axis_size("mp")
    own_heads = own // HD
    rest = (features - own) // 2
    piece = rest // (features // HD - own_heads)
    head = jnp.where(at < own, at // HD, own_heads + ((at - own) % rest) // piece)
    return (head[:, None] == jnp.arange(128, dtype=jnp.int32)[None, :]).astype(F32)


def token_pairs():
    return [(p, q) for p in range(3) for q in range(p + 1)]


def token_forward(q, k, v, table):
    q32, k32, v32 = (a.astype(F32) for a in (q, k, v))
    scale = 1.0 / math.sqrt(HD)
    pairs = token_pairs()
    prods = jnp.concatenate([q32[p] * k32[s] for p, s in pairs], axis=0)
    scores = jnp.dot(prods, table, precision=lax.Precision.HIGHEST) * scale
    frames = q.shape[1]
    score = {pair: scores[i * frames : (i + 1) * frames] for i, pair in enumerate(pairs)}
    probs = {}
    for p in range(3):
        row = [score[(p, s)] for s in range(p + 1)]
        top = row[0]
        for r in row[1:]:
            top = jnp.maximum(top, r)
        ex = [jnp.exp(r - top) for r in row]
        tot = sum(ex[1:], ex[0])
        for s in range(p + 1):
            probs[(p, s)] = ex[s] / tot
    low = jnp.concatenate([probs[pair] for pair in pairs], axis=0).astype(BF)
    wide = dot_nt(low, table.astype(BF))
    wide = {pair: wide[i * frames : (i + 1) * frames] for i, pair in enumerate(pairs)}
    mixed = jnp.stack(
        [sum(wide[(p, s)] * v32[s] for s in range(p + 1)) for p in range(3)]
    ).astype(BF)
    return mixed, (probs, low)


def token_backward(q, k, v, kept, grad_mixed, table):
    probs, low = kept
    q32, k32, v32, g32 = (a.astype(F32) for a in (q, k, v, grad_mixed))
    scale = 1.0 / math.sqrt(HD)
    pairs = token_pairs()
    frames = q.shape[1]
    cut = lambda a: {pair: a[i * frames : (i + 1) * frames] for i, pair in enumerate(pairs)}
    prods = jnp.concatenate([g32[p] * v32[s] for p, s in pairs], axis=0)
    gp = cut(jnp.dot(prods, table, precision=lax.Precision.HIGHEST))
    gs = []
    for p in range(3):
        delta = sum(probs[(p, s)] * gp[(p, s)] for s in range(p + 1))
        for s in range(p + 1):
            gs.append((probs[(p, s)] * (gp[(p, s)] - delta)).astype(BF))
    both = dot_nt(jnp.concatenate(gs + [low], axis=0), table.astype(BF))
    gw = cut(both[: 6 * frames])
    pw = cut(both[6 * frames :])
    gq = [sum(gw[(p, s)] * k32[s] for s in range(p + 1)) * scale for p in range(3)]
    gk = [sum(gw[(p, s)] * q32[p] for p in range(s, 3)) * scale for s in range(3)]
    gv = [sum(pw[(p, s)] * g32[p] for p in range(s, 3)) for s in range(3)]
    return [jnp.concatenate(a, axis=0).astype(BF) for a in (gq, gk, gv)]


def token_scatter(left, right, order, n):
    same, cross = d_blocks(right)
    from_right = swap_dp(jnp.concatenate(cross, axis=1), 1)
    from_left = swap_dp(left, 1)
    half = 3 * n // 2
    from_left = jnp.concatenate(
        [from_left[:, :n], from_left[:, n + half :], from_left[:, n : n + half]], axis=1
    )
    lefts = jnp.concatenate([left, from_left], axis=0)
    width = right.shape[1] // lax.axis_size("dp")

    def make(masks):
        mine = jnp.concatenate([same[m] for m in masks], axis=1)
        theirs = jnp.concatenate([from_right[:, m * width : (m + 1) * width] for m in masks], axis=1)
        return dot_tn(lefts, jnp.concatenate([mine, theirs], axis=0)).astype(BF)

    dp = lax.axis_size("dp")
    total = scatter_plane(make, order, (n, 3 * (n // dp), dp // 2))
    return scatter_shards(total, n)


def token_block(frame_out, embed, cotangent, row_valid, params, weights):
    gain_a, gain_b, b_down = (params[i].astype(F32) for i in (0, 3, 7))
    n_attn = params[2].shape[0]
    n_ff = params[6].shape[0]
    w_q, w_k, w_v, w_o, w_u, w_d, b_u = weights
    frames, d = frame_out.shape
    rows = 3 * frames
    table = head_table(w_o.shape[0], n_attn)

    stream = (frame_out[None] + embed.astype(F32)).reshape(rows, d)
    normed_a = normalize(stream, gain_a).astype(BF)
    q, k, v = (dot_nt(normed_a, w).astype(BF).reshape(3, frames, -1) for w in (w_q, w_k, w_v))
    mixed, kept = token_forward(q, k, v, table)
    mixed = mixed.reshape(rows, -1)
    middle = stream + dot_nn(mixed, w_o)
    normed_b = normalize(middle, gain_b).astype(BF)
    hidden_pre = dot_nt(normed_b, w_u) + b_u.astype(F32)
    hidden = activate(hidden_pre).astype(BF)
    token_out = middle + dot_nn(hidden, w_d) + b_down
    output = jnp.where(row_valid, token_out.reshape(3, frames, d), 0.0).astype(BF)

    up_order = plane_bits()
    down_order = up_order[::-1]
    grad_out = jnp.where(row_valid, cotangent.astype(F32), 0.0).reshape(rows, d)
    bias_down_grad = jnp.sum(grad_out, axis=0)
    g_low = grad_out.astype(BF)
    grad_hidden = dot_nt(g_low, w_d)
    grad_pre = jax.vjp(activate, hidden_pre)[1](grad_hidden)[0].astype(BF)
    bias_up_grad = jnp.sum(grad_pre.astype(F32), axis=0)
    down_grad = token_scatter(hidden, g_low, down_order, n_ff)
    up_grad = token_scatter(grad_pre, normed_b, up_order, n_ff)
    grad_normed_b = dot_nn(grad_pre, w_u)
    second_norm = jax.vjp(normalize, middle, gain_b)[1](grad_normed_b)
    grad_middle = grad_out + second_norm[0]
    m_low = grad_middle.astype(BF)
    grad_mixed = dot_nt(m_low, w_o).astype(BF)
    gq, gk, gv = token_backward(q, k, v, kept, grad_mixed.reshape(3, frames, -1), table)
    out_grad = token_scatter(mixed, m_low, down_order, n_attn)
    q_grad = token_scatter(gq, normed_a, up_order, n_attn)
    k_grad = token_scatter(gk, normed_a, up_order, n_attn)
    v_grad = token_scatter(gv, normed_a, down_order, n_attn)
    grad_normed_a = dot_nn(gq, w_q) + dot_nn(gk, w_k) + dot_nn(gv, w_v)
    first_norm = jax.vjp(normalize, stream, gain_a)[1](grad_normed_a)
    grad_stream = grad_middle + first_norm[0]
    return (
        output,
        jnp.sum(grad_stream.reshape(3, frames, d), axis=0),
        (jnp.concatenate([q_grad, k_grad, v_grad], axis=0), out_grad, up_grad, down_grad),
        (first_norm[1], second_norm[1], bias_up_grad, bias_down_grad),
    )


def place_bias(grad, n):
    dp = lax.axis_size("dp")
    z = lax.axis_index("mp")
    k = n // dp
    rest = grad[n:].reshape(2, dp // 2, 3, k)
    slots = by_xor([rest[i & 1, i >> 1] for i in range(dp)])
    shards = [grad[:n]] + [jnp.concatenate([s[r] for s in slots]) for r in range(3)]
    for bit in (1, 2):
        on = (z & bit) != 0
        shards = [jnp.where(on, shards[i ^ bit], shards[i]) for i in range(4)]
    return jnp.stack(shards)


def shards(
    frames,
    codes_embed,
    lengths,
    cotangent,
    *params,
):
    frame_params = params[:8]
    token_params = params[8:]
    parts = lax.axis_size("mp")
    z = lax.axis_index("mp")
    local_frames, d = frames.shape
    segment, is_valid = segments(lengths, local_frames * parts)
    mine_valid = lax.dynamic_slice_in_dim(is_valid, z * local_frames, local_frames, 0)
    row_valid = mine_valid[None, :, None]

    def by_place(rows):
        return jnp.transpose(rows.reshape(local_frames, 3, d), (1, 0, 2))

    up_order = plane_bits()
    down_order = up_order[::-1]
    qkv_t = jnp.transpose(token_params[1], (0, 2, 1))
    qk = gather_weight(qkv_t[:2], up_order)
    vo = gather_weight(jnp.stack([qkv_t[2], token_params[2]]), down_order)
    up = gather_weight(token_params[4].T[None], up_order)
    down = gather_weight(token_params[6][None], down_order)
    b_u = gather_bias(token_params[5])
    weights = (qk[0], qk[1], vo[0], vo[1], up[0], down[0], b_u)

    frame_out, frame_saved = frame_block_forward(frames.astype(F32), frame_params, segment)
    output, grad_frame_out, token_mats, token_vecs = token_block(
        frame_out, by_place(codes_embed), by_place(cotangent), row_valid, token_params, weights
    )
    output = jnp.transpose(output, (1, 0, 2)).reshape(3 * local_frames, d)
    frames_grad, frame_mats, frame_vecs = frame_block_backward(
        grad_frame_out, frame_saved, frame_params, segment
    )

    n_ff = frame_params[4].shape[1]
    devices = lax.axis_size("dp") * parts
    wide = jnp.zeros((parts, n_ff), F32)
    frame_up = lax.dynamic_update_slice_in_dim(wide, frame_vecs[2][None], z, 0)
    token_up = place_bias(token_vecs[2], n_ff)
    packed = jnp.concatenate(
        [
            v.reshape(devices, -1)
            for v in (
                frame_vecs[0],
                frame_vecs[1],
                frame_up,
                frame_vecs[3],
                token_vecs[0],
                token_vecs[1],
                token_up,
                token_vecs[3],
            )
        ],
        axis=1,
    )
    summed = lax.psum_scatter(packed, ("dp", "mp"), scatter_dimension=0, tiled=False)
    vectors = []
    at = 0
    for width in (d, d, n_ff * parts, d) * 2:
        size = width // devices
        vectors.append(summed[at : at + size])
        at += size

    def finish(mats):
        qkv, out, up_, down_ = mats
        width = qkv.shape[1]
        return (jnp.transpose(qkv.reshape(3, -1, width), (0, 2, 1)), out, up_.T, down_)

    f = finish(frame_mats)
    t = finish(token_mats)
    return (
        output,
        frames_grad,
        vectors[0],
        f[0],
        f[1],
        vectors[1],
        f[2],
        vectors[2],
        f[3],
        vectors[3],
        vectors[4],
        t[0],
        t[1],
        vectors[5],
        t[2],
        vectors[6],
        t[3],
        vectors[7],
    )


def solution(mesh):
    rows = P(("dp", "mp"), None)
    block = (
        P(),
        P(None, None, "mp"),
        P("mp", None),
        P(),
        P(None, "mp"),
        P("mp"),
        P("mp", None),
        P(),
    )
    vec = P(("dp", "mp"))
    block_out = (
        vec,
        P(None, "dp", "mp"),
        P("mp", "dp"),
        vec,
        P("dp", "mp"),
        vec,
        P("mp", "dp"),
        vec,
    )
    return jax.shard_map(
        shards,
        mesh=mesh,
        in_specs=(rows, rows, P("dp", None), rows) + block + block,
        out_specs=(rows, rows) + block_out + block_out,
        check_vma=False,
    )
```

```python
import functools
import math

import jax
import jax.numpy as jnp
from jax import lax
from jax.experimental import pallas as pl
from jax.experimental.pallas import tpu as pltpu
from jax.sharding import PartitionSpec as P

HD = 64
eps = 1e-05
BF = jnp.bfloat16
F32 = jnp.float32


def normalize(stream, gain_vec):
    return stream * lax.rsqrt(jnp.mean(stream * stream, axis=-1, keepdims=True) + eps) * gain_vec


def activate(values):
    return jax.nn.gelu(values, approximate=True)


def dot_nt(a, b):
    return lax.dot_general(a, b, (((1,), (1,)), ((), ())), preferred_element_type=F32)


def dot_nn(a, b):
    return lax.dot_general(a, b, (((1,), (0,)), ((), ())), preferred_element_type=F32)


def dot_tn(a, b):
    return lax.dot_general(a, b, (((0,), (0,)), ((), ())), preferred_element_type=F32)


def gather_rows(rows):
    return lax.all_gather(rows, "mp", axis=0, tiled=True)


def scatter_rows(partial):
    return lax.psum_scatter(
        partial.astype(BF), "mp", scatter_dimension=0, tiled=True
    ).astype(F32)


INNER = 8


def swap_dp(value, bit):
    size = lax.axis_size("dp")
    return lax.ppermute(value, "dp", [(i, i ^ bit) for i in range(size)])


def swap_mp(value, mask):
    size = lax.axis_size("mp")
    return lax.ppermute(value, "mp", [(i, i ^ mask) for i in range(size)])


def my_place():
    return lax.axis_index("dp") % INNER


BITS = [2, 4]
SIDES = [BITS, BITS[::-1]]


def after(value, *marks):
    return lax.optimization_barrier((value,) + tuple(marks))[0]


def all_after(values, *marks):
    return lax.optimization_barrier(tuple(values) + tuple(marks))[: len(values)]


class Gather:
    def __init__(self, piece):
        self.k = piece.shape[1]
        self.piece = piece

    def shards(self, *marks):
        piece = after(self.piece, *marks) if marks else self.piece
        near = swap_mp(piece, 1)
        far = swap_mp(piece, 2)
        inner = lax.ppermute(piece, "mp", [(1, 2), (2, 1)])
        outer = lax.ppermute(far, "mp", [(2, 3), (1, 0)])
        self.held = (near, far, inner, outer)

    def plane_first(self, *marks):
        near, far, inner, outer = all_after(self.held, *marks)
        z = lax.axis_index("mp")
        last = jnp.where((z == 1) | (z == 2), inner, outer)
        half = near.shape[2] // 2
        self.held = []
        for h, side in enumerate(SIDES):
            lanes = slice(h * half, (h + 1) * half)
            whole = jnp.concatenate([near[..., lanes], far[..., lanes], last[..., lanes]], axis=1)
            self.held.append((whole, swap_dp(whole, side[0])))

    def marks(self):
        return [got for _, got in self.held]

    def plane_last(self, *marks):
        held = []
        for (whole, got), side in zip(self.held, SIDES):
            whole, got = all_after((whole, got), *marks)
            low = jnp.concatenate([whole, got], axis=1)
            held.append((low, swap_dp(low, side[1])))
        self.held = held

    def cores(self, *marks):
        held = []
        for low, high in self.held:
            low, high = all_after((low, high), *marks)
            held += [low, high, swap_dp(low, 1), swap_dp(high, 1)]
        self.held = held

    def runs(self):
        out = []
        k = self.k
        for h, side in enumerate(SIDES):
            first, last = side[0] // 2, side[1] // 2
            for core in range(2):
                for high in range(2):
                    for i in range(2):
                        mask = i * first + high * last
                        for r in range(3):
                            out.append(
                                (core, h, 4 * h + 2 * core + high, (3 * i + r) * k, (4 * r + mask) * k, k)
                            )
        return out


def own_rows(shard_rows):
    k = shard_rows.shape[0] // INNER
    return lax.dynamic_slice_in_dim(shard_rows, my_place() * k, k, 0)


def own_cols(shard_cols):
    k = shard_cols.shape[-1] // INNER
    piece = lax.dynamic_slice_in_dim(shard_cols, my_place() * k, k, shard_cols.ndim - 1)
    return jnp.swapaxes(piece, -1, -2)


def by_xor(slots):
    me = my_place()
    for bit in [1] + BITS:
        on = (me & bit) != 0
        slots = [jnp.where(on, slots[i ^ bit], slots[i]) for i in range(len(slots))]
    return slots


def by_xor_mp(slots):
    z = lax.axis_index("mp")
    for bit in (1, 2):
        on = (z & bit) != 0
        slots = [jnp.where(on, slots[i ^ bit], slots[i]) for i in range(len(slots))]
    return slots


def gather_bias(bias):
    n = bias.shape[0]
    row = bias.reshape(1, n)
    rest = jnp.concatenate([swap_mp(row, r) for r in (1, 2, 3)], axis=0).reshape(3, INNER, n // INNER)
    slots = by_xor([rest[:, i] for i in range(INNER)])
    cores = [jnp.stack(slots[c::2], axis=1).reshape(-1) for c in range(2)]
    return jnp.concatenate([bias] + cores)


def place_bias(grad, n):
    rest = grad[n:].reshape(2, 3, INNER // 2, n // INNER)
    slots = by_xor([rest[i & 1, :, i >> 1] for i in range(INNER)])
    return [grad[:n]] + [jnp.concatenate([s[r] for s in slots]) for r in range(3)]


def d_order(rows):
    outer = lax.axis_size("dp") // INNER
    if outer == 1:
        return rows
    view = rows.reshape(rows.shape[0], outer, INNER, -1)
    return jnp.transpose(view, (0, 2, 1, 3)).reshape(rows.shape)


def outer_sum(value, axis):
    size = lax.axis_size("dp")
    if size == INNER:
        return value
    groups = [[o * INNER + i for o in range(size // INNER)] for i in range(INNER)]
    return lax.psum_scatter(
        value, "dp", scatter_dimension=axis, axis_index_groups=groups, tiled=True
    )


def rsq(x):
    return lax.rsqrt(jnp.mean(x * x, axis=-1, keepdims=True) + eps)


def norm_back(grad, x, gain):
    r = rsq(x)
    xr = x * r
    gg = grad * gain
    return r * (gg - xr * jnp.mean(gg * xr, axis=-1, keepdims=True)), grad * xr


def split_dot(x, table):
    hi = x.astype(BF)
    lo = (x - hi.astype(F32)).astype(BF)
    return dot_nn(hi, table) + dot_nn(lo, table)


PAIRS = [(p, s) for p in range(3) for s in range(p + 1)]


def weight_copies(runs, bufs, own_rows, dst, sem, first):
    lead = (slice(None),) * (len(dst.shape) - 2)
    rest = (dst.shape[-2] - own_rows) // 2
    half = dst.shape[-1] // 2
    copies = []
    for i, (core, h, buf, row, at, rows) in enumerate(runs):
        copies.append(
            pltpu.make_async_copy(
                bufs[buf].at[lead + (pl.ds(row, rows),)],
                dst.at[lead + (pl.ds(own_rows + core * rest + at, rows), pl.ds(h * half, half))],
                sem.at[first + i],
            )
        )
    return copies


def attn_weight_copies(runs, own_qkv, own_out, bufs, w, sem):
    n = own_out.shape[0]
    copies = [
        pltpu.make_async_copy(own_qkv, w.at[pl.ds(0, 3), pl.ds(0, n)], sem.at[0]),
        pltpu.make_async_copy(own_out, w.at[3, pl.ds(0, n)], sem.at[1]),
    ]
    return copies + weight_copies(runs, bufs, n, w, sem, 2)


def place_pick(p, frames):
    col = lax.broadcasted_iota(jnp.int32, (frames, 3 * frames), 1)
    row = lax.broadcasted_iota(jnp.int32, (frames, 3 * frames), 0)
    return (col == 3 * row + p).astype(BF)


def place_put(p, frames):
    row = lax.broadcasted_iota(jnp.int32, (3 * frames, frames), 0)
    col = lax.broadcasted_iota(jnp.int32, (3 * frames, frames), 1)
    return (row == 3 * col + p).astype(BF)


def token_attn_kernel(runs, fo, emb, cot, valid, ga, gb, table, own_qkv, own_out, *rest):
    bufs, (s_o, g_o, na_o, q_o, k_o, v_o, mix_o, mid_o, nb_o, pr_o, w, sem) = rest[:8], rest[8:]
    copies = attn_weight_copies(runs, own_qkv, own_out, bufs, w, sem)
    for c in copies:
        c.start()
    frames = fo.shape[0]
    places = [pl.ds(p * frames, frames) for p in range(3)]
    for p in range(3):
        pick = place_pick(p, frames)
        g = dot_nn(pick, cot[...])
        g_o[places[p]] = jnp.where(valid[...] > 0.0, g, 0.0).astype(BF)
        s = fo[...] + dot_nn(pick, emb[...])
        s_o[places[p]] = s
        na_o[places[p]] = (s * rsq(s) * ga[...]).astype(BF)
    for c in copies:
        c.wait()
    for t, out in enumerate((q_o, k_o, v_o)):
        out[...] = dot_nt(na_o[...], w[t]).astype(BF)
    scale = 1.0 / math.sqrt(HD)
    for p in range(3):
        scores = [
            split_dot(q_o[places[p]].astype(F32) * k_o[places[s]].astype(F32), table[...]) * scale
            for s in range(p + 1)
        ]
        top = scores[0]
        for x in scores[1:]:
            top = jnp.maximum(top, x)
        ex = [jnp.exp(x - top) for x in scores]
        total = ex[0]
        for x in ex[1:]:
            total = total + x
        mixed = None
        for s in range(p + 1):
            prob = ex[s] / total
            pr_o[PAIRS.index((p, s))] = prob
            term = dot_nt(prob.astype(BF), table[...]) * v_o[places[s]].astype(F32)
            mixed = term if mixed is None else mixed + term
        mix_o[places[p]] = mixed.astype(BF)
    for p in places:
        mid = s_o[p] + dot_nn(mix_o[p], w[3])
        mid_o[p] = mid
        nb_o[p] = (mid * rsq(mid) * gb[...]).astype(BF)


def token_back_kernel(runs, g, gnb, mid, s_in, ga, gb, q, k, v, mix, pr, table, own_qkv, own_out, *rest):
    bufs, (ml_o, left_o, gf_o, da_o, db_o, w, gm, gx, sem) = rest[:8], rest[8:]
    copies = attn_weight_copies(runs, own_qkv, own_out, bufs, w, sem)
    for c in copies:
        c.start()
    frames, feats = gf_o.shape[0], q.shape[1]
    places = [pl.ds(p * frames, frames) for p in range(3)]
    lanes = [pl.ds(t * feats, feats) for t in range(4)]
    total = None
    for p in places:
        dx, dg = norm_back(gnb[p], mid[p], gb[...])
        grad = g[p].astype(F32) + dx
        gm[p] = grad
        ml_o[p] = grad.astype(BF)
        row = jnp.sum(dg, axis=0, keepdims=True)
        total = row if total is None else total + row
    db_o[...] = total
    left_o[:, lanes[3]] = mix[...]
    for c in copies:
        c.wait()
    gx[...] = dot_nt(ml_o[...], w[3]).astype(BF)
    scale = 1.0 / math.sqrt(HD)
    kg, vg = {}, {}
    for p in range(3):
        gp = [
            split_dot(gx[places[p]].astype(F32) * v[places[s]].astype(F32), table[...])
            for s in range(p + 1)
        ]
        probs = [pr[PAIRS.index((p, s))] for s in range(p + 1)]
        delta = probs[0] * gp[0]
        for s in range(1, p + 1):
            delta = delta + probs[s] * gp[s]
        query = None
        for s in range(p + 1):
            wide = dot_nt((probs[s] * (gp[s] - delta)).astype(BF), table[...])
            term = wide * k[places[s]].astype(F32)
            query = term if query is None else query + term
            key = wide * q[places[p]].astype(F32) * scale
            value = dot_nt(probs[s].astype(BF), table[...]) * gx[places[p]].astype(F32)
            if p == s:
                kg[s], vg[s] = key, value
            else:
                kg[s], vg[s] = kg[s] + key, vg[s] + value
        left_o[places[p], lanes[0]] = (query * scale).astype(BF)
    for s in range(3):
        left_o[places[s], lanes[1]] = kg[s].astype(BF)
        left_o[places[s], lanes[2]] = vg[s].astype(BF)
    gna = dot_nn(left_o[:, lanes[0]], w[0]) + dot_nn(left_o[:, lanes[1]], w[1]) + dot_nn(left_o[:, lanes[2]], w[2])
    total = out = None
    for i, p in enumerate(places):
        dx, dg = norm_back(gna[i * frames : (i + 1) * frames], s_in[p], ga[...])
        grad = gm[p] + dx
        row = jnp.sum(dg, axis=0, keepdims=True)
        total = row if total is None else total + row
        out = grad if out is None else out + grad
    da_o[...] = total
    gf_o[...] = out


GELU_S = math.sqrt(2.0 / math.pi)


def gelu_both(u):
    u2 = u * u
    t = jnp.tanh(GELU_S * (u + 0.044715 * (u2 * u)))
    h = 0.5 * (1.0 + t)
    return u * h, h + 0.5 * u * (1.0 - t * t) * (GELU_S * (1.0 + 3.0 * 0.044715 * u2))


def token_ff_kernel(runs, step, nb, g, mid, valid, bias, bdown, own_up, own_down, *rest):
    bufs, (out_o, gnb_o, left_o, gb_o, wuo, wdo, w, acc, sem) = rest[:8], rest[8:]
    n, frames = own_down.shape[0], valid.shape[0]
    own = [
        pltpu.make_async_copy(own_up, wuo, sem.at[0]),
        pltpu.make_async_copy(own_down, wdo, sem.at[1]),
    ]
    copies = weight_copies(runs, bufs, 0, w, sem, 2)
    for c in own + copies:
        c.start()
    acc[...] = jnp.zeros_like(acc)
    gnb_o[...] = jnp.zeros_like(gnb_o)

    def middle(at, size, pre, back):
        cols = pl.ds(at, size)
        h, dh = gelu_both(pre + bias[:, cols])
        h = h.astype(BF)
        gp = (dh * back).astype(BF)
        left_o[:, cols] = h
        left_o[:, pl.ds(pl.multiple_of(4 * n + at, 128), size)] = gp
        gb_o[:, cols] = jnp.sum(gp.astype(F32), axis=0, keepdims=True)
        return h, gp

    for c in own:
        c.wait()
    own_step = n // 2

    def own_block(j, carry):
        at = pl.multiple_of(j * own_step, own_step)
        cols = pl.ds(at, own_step)
        pre = dot_nn(nb[...], wuo[:, cols])
        back = dot_nt(g[...], wdo[cols, :])
        h, gp = middle(at, own_step, pre, back)
        acc[...] += dot_nn(h, wdo[cols, :])
        gnb_o[...] += dot_nt(gp, wuo[:, cols])
        return carry

    lax.fori_loop(0, n // own_step, own_block, 0)
    for c in copies:
        c.wait()

    def block(j, carry):
        rows = pl.ds(pl.multiple_of(j * step, step), step)
        pre = dot_nt(nb[...], w[0, rows, :])
        back = dot_nt(g[...], w[1, rows, :])
        h, gp = middle(pl.multiple_of(n + j * step, 128), step, pre, back)
        acc[...] += dot_nn(h, w[1, rows, :])
        gnb_o[...] += dot_nn(gp, w[0, rows, :])
        return carry

    lax.fori_loop(0, w.shape[1] // step, block, 0)
    out = None
    for p in range(3):
        rows = pl.ds(p * frames, frames)
        val = jnp.where(valid[...] > 0.0, acc[rows] + mid[rows] + bdown[...], 0.0).astype(BF)
        term = dot_nn(place_put(p, frames), val)
        out = term if out is None else out + term
    out_o[...] = out.astype(BF)


def stage_masks(side):
    first, last = side[0] // 2, side[1] // 2
    return [0, last], [first, first | last]


def right_rows(me, core):
    order = []
    for h, side in enumerate(SIDES):
        keep, give = stage_masks(side)
        for m in keep + give:
            order.append(((me ^ (2 * m + core)), h))
    return order


def lay_right(dst, at, right, me, core, block):
    half = block // 2
    for i, (place, h) in enumerate(right_rows(me, core)):
        dst[pl.ds(at + i * half, half), :] = right[
            pl.ds(pl.multiple_of(place * block + h * half, half), half), :
        ]


def pair_grad_kernel(new, swap, me_ref, lm, lt, rm, rt, *rest):
    outs, (tmp, am, at) = rest[:4], rest[4:]
    j = pl.program_id(0)
    me = me_ref[0]
    block = rm.shape[2] // INNER

    @pl.when(new(j))
    def _():
        for src, dst in ((rm, am), (rt, at)):
            tmp[...] = jnp.transpose(src[0])
            lay_right(dst, 0, tmp, me, 0, block)

    other = lt[...]
    if swap is not None:
        a, b = swap
        other = jnp.concatenate([other[:, :a], other[:, a + b :], other[:, a : a + b]], axis=1)
    total = dot_nn(am[...], lm[...]) + dot_nn(at[...], other)
    size = total.shape[0] // 4
    for i, out in enumerate(outs):
        out[...] = total[i * size : (i + 1) * size].astype(BF)


def frame_grad_kernel(new, me_ref, left, right, *rest):
    outs, (tmp, am) = rest[:5], rest[5:]
    j = pl.program_id(0)
    me = me_ref[0]
    d = right.shape[2]
    block = d // INNER

    @pl.when(new(j))
    def _():
        tmp[...] = jnp.transpose(right[0])
        lay_right(am, 0, tmp, me, 0, block)
        lay_right(am, d // 2, tmp, me, 1, block)

    total = dot_nn(am[...], left[...])
    size = d // 8
    for i in range(4):
        outs[i][...] = total[i * size : (i + 1) * size].astype(BF)
    outs[4][...] = total[d // 2 :].astype(BF)


def lane_swap(x, bit, k, own):
    parts = [x[:, :own]] if own else []
    lanes = 4 * k
    for at in range(own, x.shape[1], lanes):
        group = x[:, at : at + lanes]
        if k % 128 == 0:
            parts += [group[:, (m ^ bit) * k : (m ^ bit) * k + k] for m in range(4)]
        elif bit == 2:
            parts.append(pltpu.roll(group, lanes // 2, 1))
        else:
            lane = lax.broadcasted_iota(jnp.int32, group.shape, 1)
            parts.append(
                jnp.where((lane & k) == 0, pltpu.roll(group, lanes - k, 1), pltpu.roll(group, k, 1))
            )
    return jnp.concatenate(parts, axis=1) if len(parts) > 1 else parts[0]


def add_kernel(k, own_of, *refs):
    ins, outs = refs[:4], refs[4:]
    j = pl.program_id(0)
    for h, side in enumerate(SIDES):
        keep, got, low, high = ins[2 * h], ins[2 * h + 1], outs[2 * h], outs[2 * h + 1]
        half = keep.shape[0] // 2

        def put(value):
            total = keep[...].astype(F32) + value
            low[...] = total[:half]
            high[...] = total[half:].astype(BF)

        def plain():
            put(got[...].astype(F32))

        def moved(own=0):
            put(lane_swap(got[...].astype(F32), side[0] // 2, k, own))

        if k is None:
            plain()
        elif isinstance(own_of, int):
            moved(own_of)
        else:
            pl.when(own_of(j))(plain)
            pl.when(jnp.logical_not(own_of(j)))(moved)


def split_kernel(k, own, *refs):
    ins, (own_o, *sent) = refs[:4], refs[4:]
    for h, side in enumerate(SIDES):
        keep, got = ins[2 * h], ins[2 * h + 1]
        half = keep.shape[0]
        rows = pl.ds(h * half, half)
        total = keep[...] + lane_swap(got[...].astype(F32), side[1] // 2, k, own)
        own_o[rows, :] = total[:, :own]
        for core in range(2):
            for r in range(3):
                at = own + (3 * core + r) * 4 * k
                sent[r][rows, pl.ds(core * 4 * k, 4 * k)] = total[:, at : at + 4 * k].astype(BF)


def ff_final_kernel(me_ref, own, g1, g2, g3, down, up):
    me = me_ref[0]
    n = own.shape[1] // 2
    k = n // INNER
    for m in range(2):
        for i in range(INNER):
            slot = me ^ i
            at = pl.multiple_of(m * n + (slot & 1) * (n // 2) + (slot >> 1) * k, k)
            lanes = pl.ds(at, k)
            total = own[:, m * n + i * k : m * n + (i + 1) * k]
            for g in (g1, g2, g3):
                total = total + g[:, lanes].astype(F32)
            if m == 0:
                down[i * k : (i + 1) * k, :] = jnp.transpose(total)
            else:
                up[:, i * k : (i + 1) * k] = total


def attn_final_kernel(me_ref, own, g1, g2, g3, qkv, out):
    me = me_ref[0]
    n = own.shape[1] // 4
    k = n // INNER
    row = lax.broadcasted_iota(jnp.int32, (n, n), 0)
    col = lax.broadcasted_iota(jnp.int32, (n, n), 1)
    half = n // 2
    inside = row & (half - 1)
    place = (2 * (inside // k) + (row // half)) ^ me
    perm = (col == place * k + (row & (k - 1))).astype(BF)
    for t in range(4):
        lanes = slice(t * n, (t + 1) * n)
        total = own[:, lanes]
        for g in (g1, g2, g3):
            total = total + dot_nn(g[:, lanes], perm)
        if t < 3:
            qkv[t] = total
        else:
            out[...] = jnp.transpose(total)


def frame_core_kernel(*refs):
    keeps, got, outs = refs[:4], refs[4], refs[5:]
    size = outs[0].shape[0]
    for i in range(4):
        outs[i][...] = (
            keeps[i][...].astype(F32) + got[i * size : (i + 1) * size, :].astype(F32)
        ).astype(BF)


def frame_final_kernel(kind, ka, ga, kb, gb, *outs):
    half = ka.shape[0]

    def put(at, size):
        return jnp.concatenate(
            [
                ka[:, at : at + size] + ga[:, at : at + size].astype(F32),
                kb[:, at : at + size] + gb[:, at : at + size].astype(F32),
            ],
            axis=0,
        )

    units = ka.shape[1]
    if kind == "ff":
        n = units // 2
        step = n // 8
        for i in range(8):
            outs[0][i * step : (i + 1) * step, :] = jnp.transpose(put(i * step, step))
        outs[1][...] = put(n, n)
    else:
        n = units // 4
        for t in range(3):
            outs[0][t] = put(t * n, n)
        outs[1][...] = jnp.transpose(put(3 * n, n))


VMEM_LIMIT = 60 * 1024 * 1024


def arr(shape, dtype):
    return jax.ShapeDtypeStruct(shape, dtype)


def cost(flops, ins, outs):
    size = sum(a.size * a.dtype.itemsize for a in ins) + sum(
        math.prod(o.shape) * o.dtype.itemsize for o in outs
    )
    return pl.CostEstimate(flops=flops, bytes_accessed=size, transcendentals=0)


def call(kernel, outs, ins, scratch, any_from, flops, smem=0):
    def space(i):
        return pltpu.SMEM if i < smem else pltpu.VMEM if i < any_from else pl.ANY

    return pl.pallas_call(
        kernel,
        out_shape=outs,
        in_specs=[pl.BlockSpec(memory_space=space(i)) for i in range(len(ins))],
        out_specs=[pl.BlockSpec(memory_space=pltpu.VMEM)] * len(outs),
        scratch_shapes=scratch,
        compiler_params=pltpu.CompilerParams(vmem_limit_bytes=VMEM_LIMIT),
        cost_estimate=cost(flops, ins, outs),
    )(*ins)


def token_attn(fo, emb, cot, valid, ga, gb, table, own_qkv, own_out, gather, bufs):
    frames, d = fo.shape
    rows, feats = 3 * frames, table.shape[0]
    runs = gather.runs()
    outs = (
        [arr((rows, d), F32), arr((rows, d), BF), arr((rows, d), BF)]
        + [arr((rows, feats), BF)] * 4
        + [arr((rows, d), F32), arr((rows, d), BF), arr((len(PAIRS), frames, table.shape[1]), F32)]
    )
    return call(
        functools.partial(token_attn_kernel, runs),
        outs,
        [fo, emb, cot, valid, ga, gb, table, own_qkv, own_out, *bufs],
        [pltpu.VMEM((4, feats, d), BF), pltpu.SemaphoreType.DMA((2 + len(runs),))],
        7,
        8 * rows * feats * d,
    )


def token_back(g, gnb, mid, s, ga, gb, q, k, v, mix, pr, table, own_qkv, own_out, gather, bufs):
    rows, d = s.shape
    frames, feats = rows // 3, table.shape[0]
    runs = gather.runs()
    outs = [
        arr((rows, d), BF),
        arr((rows, 4 * feats), BF),
        arr((frames, d), F32),
        arr((1, d), F32),
        arr((1, d), F32),
    ]
    return call(
        functools.partial(token_back_kernel, runs),
        outs,
        [g, gnb, mid, s, ga, gb, q, k, v, mix, pr, table, own_qkv, own_out, *bufs],
        [
            pltpu.VMEM((4, feats, d), BF),
            pltpu.VMEM((rows, d), F32),
            pltpu.VMEM((rows, feats), BF),
            pltpu.SemaphoreType.DMA((2 + len(runs),)),
        ],
        12,
        8 * rows * feats * d,
    )


def token_ff(nb, g, mid, valid, bias, bdown, own_up, own_down, gather, bufs):
    rows, d = nb.shape
    n = own_down.shape[0]
    runs = gather.runs()
    outs = [
        arr((rows, d), BF),
        arr((rows, d), F32),
        arr((rows, 8 * n), BF),
        arr((1, 4 * n), F32),
    ]
    return call(
        functools.partial(token_ff_kernel, runs, 384),
        outs,
        [nb, g, mid, valid, bias, bdown, own_up, own_down, *bufs],
        [
            pltpu.VMEM((d, n), BF),
            pltpu.VMEM((n, d), BF),
            pltpu.VMEM((2, 3 * n, d), BF),
            pltpu.VMEM((rows, d), F32),
            pltpu.SemaphoreType.DMA((2 + len(runs),)),
        ],
        6,
        32 * rows * n * d,
    )


def smem_spec():
    return pl.BlockSpec(memory_space=pltpu.SMEM)


def pair_grad(me, left, left_other, rights, rights_other, step, pick, partner, new, swap):
    rows, units = left.shape
    d = rights.shape[2]
    outs = [arr((d // 8, units), BF)] * 4
    return pl.pallas_call(
        functools.partial(pair_grad_kernel, new, swap),
        grid=(units // step,),
        in_specs=[
            smem_spec(),
            pl.BlockSpec((rows, step), lambda j: (0, j)),
            pl.BlockSpec((rows, step), lambda j: (0, partner(j))),
            pl.BlockSpec((1, rows, d), lambda j: (pick(j), 0, 0)),
            pl.BlockSpec((1, rows, d), lambda j: (pick(j), 0, 0)),
        ],
        out_specs=[pl.BlockSpec((d // 8, step), lambda j: (0, j))] * 4,
        out_shape=outs,
        scratch_shapes=[pltpu.VMEM((d, rows), BF)] + [pltpu.VMEM((d // 2, rows), BF)] * 2,
        compiler_params=pltpu.CompilerParams(vmem_limit_bytes=VMEM_LIMIT),
        cost_estimate=cost(2 * rows * units * d, [left, left_other, rights, rights_other], outs),
    )(me, left, left_other, rights, rights_other)


def ff_pair_grad(me, left, other, rights, rights_other, n):
    step = n // 2

    def partner(j):
        b = j % 8
        return j - b + jnp.where(b < 2, b, jnp.where(b < 5, b + 3, b - 3))

    return pair_grad(
        me, left, other, rights, rights_other, step,
        lambda j: j // 8, partner, lambda j: j % 8 == 0, None,
    )


def attn_pair_grad(me, left, other, rights, rights_other, n):
    return pair_grad(
        me, left, other, rights, rights_other, 4 * n,
        lambda j: j // 3, lambda j: j, lambda j: (j == 0) | (j == 3), (n, 3 * n // 2),
    )


def frame_grad(me, left, rights, split):
    rows, units = left.shape
    d = rights.shape[2]
    step = units // 4 if split * 4 % units else units // 4
    at = split // step
    outs = [arr((d // 8, units), BF)] * 4 + [arr((d // 2, units), BF)]
    return pl.pallas_call(
        functools.partial(frame_grad_kernel, lambda j: (j == 0) | (j == at)),
        grid=(4,),
        in_specs=[
            smem_spec(),
            pl.BlockSpec((rows, step), lambda j: (0, j)),
            pl.BlockSpec((1, rows, d), lambda j: (jnp.where(j < at, 0, 1), 0, 0)),
        ],
        out_specs=[pl.BlockSpec((d // 8, step), lambda j: (0, j))] * 4
        + [pl.BlockSpec((d // 2, step), lambda j: (0, j))],
        out_shape=outs,
        scratch_shapes=[pltpu.VMEM((d, rows), BF)] * 2,
        compiler_params=pltpu.CompilerParams(vmem_limit_bytes=VMEM_LIMIT),
        cost_estimate=cost(2 * rows * units * d, [left, rights], outs),
    )(me, left, rights)


def add_halves(keep_a, got_a, keep_b, got_b, step, k, own_of):
    rows, units = keep_a.shape
    outs = [arr((rows // 2, units), F32), arr((rows // 2, units), BF)] * 2
    ins = [keep_a, got_a, keep_b, got_b]
    return pl.pallas_call(
        functools.partial(add_kernel, k, own_of),
        grid=(units // step,),
        in_specs=[pl.BlockSpec((rows, step), lambda j: (0, j))] * 4,
        out_specs=[pl.BlockSpec((rows // 2, step), lambda j: (0, j))] * 4,
        out_shape=outs,
        compiler_params=pltpu.CompilerParams(vmem_limit_bytes=VMEM_LIMIT),
        cost_estimate=cost(0, ins, outs),
    )(*ins)


def split_shards(keep_a, got_a, keep_b, got_b, n, k):
    rows, units = keep_a.shape
    count = units // (4 * n)
    outs = [arr((2 * rows, count * n), F32)] + [arr((2 * rows, count * n), BF)] * 3
    ins = [keep_a, got_a, keep_b, got_b]
    return pl.pallas_call(
        functools.partial(split_kernel, k, n),
        grid=(count,),
        in_specs=[pl.BlockSpec((rows, 4 * n), lambda j: (0, j))] * 4,
        out_specs=[pl.BlockSpec((2 * rows, n), lambda j: (0, j))] * 4,
        out_shape=outs,
        compiler_params=pltpu.CompilerParams(vmem_limit_bytes=VMEM_LIMIT),
        cost_estimate=cost(0, ins, outs),
    )(*ins)


class TokenGrads:
    def __init__(self, quarters, n, k, step, own_of):
        self.n, self.k, self.step, self.own_of = n, k, step, own_of
        keep_a, give_a, keep_b, give_b = quarters
        self.hold = keep_a
        self.held = (keep_a, swap_dp(give_a, SIDES[0][0]), keep_b, swap_dp(give_b, SIDES[1][0]))

    def middle(self, *marks):
        keep_a, give_a, keep_b, give_b = add_halves(
            *all_after(self.held, *marks), self.step, self.k, self.own_of
        )
        self.hold = keep_a
        self.held = (keep_a, swap_dp(give_a, SIDES[0][1]), keep_b, swap_dp(give_b, SIDES[1][1]))

    def shards(self, *marks):
        own, *sent = split_shards(*all_after(self.held, *marks), self.n, self.k)
        self.own = own
        self.held = tuple(swap_mp(sent[r - 1], r) for r in (1, 2, 3))
        return own

    def last(self, kernel, outs, me, *marks):
        ins = [me, self.own, *all_after(self.held, *marks)]
        return call(kernel, outs, ins, [], len(ins), 0, smem=1)


class FrameGrads:
    def __init__(self, parts):
        self.hold = parts[0]
        self.held = tuple(parts[:4]) + (swap_dp(parts[4], 1),)

    def first(self, *marks):
        ins = all_after(self.held, *marks)
        rows, units = ins[0].shape
        step = units // 4
        outs = [arr((rows, units), BF)] * 4
        keep_a, give_a, keep_b, give_b = pl.pallas_call(
            frame_core_kernel,
            grid=(4,),
            in_specs=[pl.BlockSpec((rows, step), lambda j: (0, j))] * 4
            + [pl.BlockSpec((4 * rows, step), lambda j: (0, j))],
            out_specs=[pl.BlockSpec((rows, step), lambda j: (0, j))] * 4,
            out_shape=outs,
            compiler_params=pltpu.CompilerParams(vmem_limit_bytes=VMEM_LIMIT),
            cost_estimate=cost(0, ins, outs),
        )(*ins)
        self.hold = keep_a
        self.held = (keep_a, swap_dp(give_a, SIDES[0][0]), keep_b, swap_dp(give_b, SIDES[1][0]))

    def middle(self, *marks):
        ins = all_after(self.held, *marks)
        keep_a, give_a, keep_b, give_b = add_halves(*ins, ins[0].shape[1] // 2, None, None)
        self.hold = keep_a
        self.held = (keep_a, swap_dp(give_a, SIDES[0][1]), keep_b, swap_dp(give_b, SIDES[1][1]))

    def last(self, kind, outs, *marks):
        ins = all_after(self.held, *marks)
        return call(functools.partial(frame_final_kernel, kind), outs, list(ins), [], 4, 0)


def segments(lengths, whole_rows):
    count = lengths.shape[1]
    order = jnp.arange(count, dtype=jnp.int32)
    item_ends = jnp.sum(
        jnp.where(order[None, :] <= order[:, None], lengths[0][None, :], 0), axis=1, dtype=jnp.int32
    )
    positions = jnp.arange(whole_rows, dtype=jnp.int32)
    segment = jnp.sum(
        (positions[:, None] >= item_ends[None, :]).astype(jnp.int32), axis=1, dtype=jnp.int32
    )
    is_valid = positions < jnp.sum(lengths[0], dtype=jnp.int32)
    segment = jnp.where(is_valid, segment, positions + count)
    return (segment, is_valid)


def frame_allowed(segment):
    positions = jnp.arange(segment.shape[0], dtype=jnp.int32)
    return (positions[None, :] <= positions[:, None]) & (segment[None, :] == segment[:, None])


def split_heads(rows):
    return rows.reshape(rows.shape[0], rows.shape[1] // HD, HD)


def frame_forward(qkv_rows, segment):
    queries, key_rows, value_rows = (split_heads(qkv_rows[t]) for t in range(3))
    raw_scores = jnp.einsum("qhe,khe->hqk", queries, key_rows, preferred_element_type=F32) * (
        1.0 / math.sqrt(HD)
    )
    scores = jnp.where(frame_allowed(segment)[None], raw_scores, -1e30)
    top_score = jnp.max(scores, axis=-1, keepdims=True)
    exp_scores = jnp.exp(scores - top_score)
    exp_total = jnp.sum(exp_scores, axis=-1, keepdims=True)
    attn_probs = (exp_scores / exp_total).astype(BF)
    mixed = jnp.einsum("hqk,khe->qhe", attn_probs, value_rows, preferred_element_type=F32)
    log_total = top_score[:, :, 0] + jnp.log(exp_total[:, :, 0])
    return (mixed.astype(BF).reshape(qkv_rows.shape[1], -1), log_total)


def frame_backward(qkv_rows, log_total, grad_mixed, segment):
    queries, key_rows, value_rows = (split_heads(qkv_rows[t]) for t in range(3))
    grad_heads = split_heads(grad_mixed)
    scale = 1.0 / math.sqrt(HD)
    raw_scores = jnp.einsum("qhe,khe->hqk", queries, key_rows, preferred_element_type=F32) * scale
    scores = jnp.where(frame_allowed(segment)[None], raw_scores, -1e30)
    attn_probs = jnp.exp(scores - log_total[:, :, None])
    value_grad = jnp.einsum(
        "hqk,qhe->khe", attn_probs.astype(BF), grad_heads, preferred_element_type=F32
    )
    grad_probs = jnp.einsum("qhe,khe->hqk", grad_heads, value_rows, preferred_element_type=F32)
    row_delta = jnp.sum(attn_probs * grad_probs, axis=-1, keepdims=True)
    grad_scores = (attn_probs * (grad_probs - row_delta)).astype(BF)
    query_grad = jnp.einsum("hqk,khe->qhe", grad_scores, key_rows, preferred_element_type=F32) * scale
    key_grad = jnp.einsum("hqk,qhe->khe", grad_scores, queries, preferred_element_type=F32) * scale
    rows = qkv_rows.shape[1]
    return [g.reshape(rows, -1).astype(BF) for g in (query_grad, key_grad, value_grad)]


def head_table(features, own):
    at = jnp.arange(features, dtype=jnp.int32)
    own_heads = own // HD
    rest = (features - own) // 2
    piece = rest // (features // HD - own_heads)
    head = jnp.where(at < own, at // HD, own_heads + ((at - own) % rest) // piece)
    return (head[:, None] == jnp.arange(128, dtype=jnp.int32)[None, :]).astype(BF)


def shards(frames, codes_embed, lengths, cotangent, *params):
    gain_a, w_qkv, w_out, gain_b, w_up, b_up, w_down, b_down = params[:8]
    t_gain_a, t_qkv, t_out, t_gain_b, t_up, t_bup, t_down, t_bdown = params[8:]
    dp, parts = lax.axis_size("dp"), lax.axis_size("mp")
    z = lax.axis_index("mp")
    me = my_place().astype(jnp.int32).reshape(1)
    local, d = frames.shape
    n_attn, n_ff = w_out.shape[0], w_down.shape[0]
    block = d // INNER
    segment, is_valid = segments(lengths, local * parts)
    valid = lax.dynamic_slice_in_dim(is_valid, z * local, local, 0).astype(F32)[:, None]

    stream = frames.astype(F32)
    gain_a32, gain_b32 = gain_a.astype(F32), gain_b.astype(F32)
    normed_a = normalize(stream, gain_a32).astype(BF)
    gathered_a = gather_rows(normed_a)

    attn_w = Gather(jnp.concatenate([own_cols(t_qkv), own_rows(t_out)[None]], axis=0))
    ff_w = Gather(jnp.stack([own_cols(t_up), own_rows(t_down)]))
    attn_w.shards()
    gathered_a = after(gathered_a, *attn_w.held)

    qkv_rows = jnp.einsum("rd,tde->tre", gathered_a, w_qkv, preferred_element_type=F32).astype(BF)
    mixed_rows, log_total = frame_forward(qkv_rows, segment)
    part_a = dot_nn(mixed_rows, w_out).astype(BF)
    branch_a = scatter_rows(part_a)

    ff_w.shards(part_a)
    attn_w.plane_first(part_a)
    middle = stream + after(branch_a, *ff_w.held, *attn_w.marks())

    normed_b = normalize(middle, gain_b32).astype(BF)
    gathered_b = gather_rows(normed_b)

    attn_w.plane_last(normed_b)
    ff_w.plane_first(normed_b)
    gathered_b = after(gathered_b, *attn_w.marks(), *ff_w.marks())

    hidden_pre = dot_nn(gathered_b, w_up) + b_up.astype(F32)
    hidden = activate(hidden_pre).astype(BF)
    part_b = dot_nn(hidden, w_down).astype(BF)
    branch_b = scatter_rows(part_b)

    attn_w.cores(part_b)
    ff_w.plane_last(part_b)
    frame_out = middle + after(branch_b, *attn_w.held, *ff_w.marks()) + b_down.astype(F32)

    t_bias = gather_bias(t_bup).astype(F32)[None]
    own_qkv = jnp.transpose(t_qkv, (0, 2, 1))
    table = head_table(n_attn * parts, n_attn)
    tga, tgb = t_gain_a.astype(F32)[None], t_gain_b.astype(F32)[None]

    attn_bufs = attn_w.held
    t_stream, g_low, t_na, q, k, v, mixed, t_middle, t_nb, probs = token_attn(
        frame_out, codes_embed, cotangent, valid, tga, tgb, table, own_qkv, t_out, attn_w, attn_bufs
    )
    ff_w.cores()
    output, t_gnb, t_left, t_gbup = token_ff(
        t_nb, g_low, t_middle, valid, t_bias, t_bdown.astype(F32)[None], t_up, t_down, ff_w, ff_w.held
    )
    rights = jnp.stack([d_order(g_low), d_order(t_nb)])
    rights_other = swap_dp(rights, 1)
    left_other = swap_dp(t_left, 1)
    m_low, a_left, grad_frame, t_da, t_db = token_back(
        g_low, t_gnb, t_middle, t_stream, tga, tgb, q, k, v, mixed, probs, table, own_qkv, t_out, attn_w, attn_bufs
    )
    t_dbd = jnp.sum(g_low.astype(F32), axis=0)

    grad_low = grad_frame.astype(BF)
    gathered_down = gather_rows(grad_low)

    ff_s = TokenGrads(
        ff_pair_grad(me, after(t_left, grad_low), left_other, rights, rights_other, n_ff),
        n_ff, n_ff // INNER, n_ff, lambda j: j % 4 == 0,
    )
    a_left = after(a_left, grad_low)
    a_rights = jnp.stack([d_order(t_na), d_order(m_low)])
    a_rights_other = swap_dp(a_rights, 1)
    a_other = swap_dp(a_left, 1)

    gathered_down = after(gathered_down, ff_s.hold)
    grad_hidden = dot_nt(gathered_down, w_down)
    grad_pre = jax.vjp(activate, hidden_pre)[1](grad_hidden)[0].astype(BF)
    part_c = dot_nt(grad_pre, w_up).astype(BF)
    grad_nb = scatter_rows(part_c)

    attn_s = TokenGrads(
        attn_pair_grad(me, after(a_left, part_c), a_other, a_rights, a_rights_other, n_attn),
        n_attn, n_attn // INNER, 4 * n_attn, n_attn,
    )
    f_left = jnp.concatenate([hidden, grad_pre], axis=1)
    f_ff = FrameGrads(
        frame_grad(me, after(f_left, part_c), jnp.stack([d_order(gathered_down), d_order(gathered_b)]), n_ff)
    )

    grad_nb = after(grad_nb, attn_s.hold, f_ff.hold)
    second = jax.vjp(normalize, middle, gain_b32)[1](grad_nb)
    grad_middle = grad_frame + second[0]
    mid_low = grad_middle.astype(BF)
    gathered_mid = gather_rows(mid_low)

    ff_s.middle(mid_low)
    f_ff.first(mid_low)

    grad_mixed = dot_nt(after(gathered_mid, ff_s.hold, f_ff.hold), w_out).astype(BF)
    grad_qkv = jnp.concatenate(frame_backward(qkv_rows, log_total, grad_mixed, segment), axis=1)
    w_all = jnp.concatenate([w_qkv[0], w_qkv[1], w_qkv[2]], axis=1)
    part_d32 = dot_nt(grad_qkv, w_all)
    part_d = part_d32.astype(BF)
    grad_na = scatter_rows(part_d)
    f_da = jnp.sum(part_d32 * gathered_a.astype(F32), axis=0) / gain_a32

    ff_s.shards(part_d)
    attn_s.middle(part_d)
    f_ff.middle(part_d)
    f_attn = FrameGrads(
        frame_grad(
            me,
            after(jnp.concatenate([grad_qkv, mixed_rows], axis=1), part_d),
            jnp.stack([d_order(gathered_a), d_order(gathered_mid)]),
            3 * n_attn,
        )
    )

    wide = lax.dynamic_update_slice_in_dim(
        jnp.zeros((parts, n_ff), F32), jnp.sum(grad_pre.astype(F32), axis=0)[None], z, 0
    )
    t_wide = jnp.stack(by_xor_mp(place_bias(t_gbup[0], n_ff)))

    def by_owner(full):
        return jnp.transpose(full.reshape(dp, parts, -1), (1, 0, 2)).reshape(parts, -1)

    vec = jnp.concatenate(
        [
            jnp.stack([f_da, second[1], jnp.sum(grad_frame, axis=0), t_da[0], t_db[0], t_dbd]),
            by_owner(wide),
            by_owner(t_wide),
        ],
        axis=0,
    )
    vec = d_order(vec)
    vec = jnp.concatenate(by_xor([vec[:, i * block : (i + 1) * block] for i in range(INNER)]), axis=1)
    for bit in (4, 2, 1):
        half = vec.shape[1] // 2
        vec = vec[:, :half] + swap_dp(vec[:, half:], bit)
    vec = outer_sum(vec, 1)
    width = vec.shape[1]
    quarter = width // parts
    rows = by_xor_mp(
        [
            jnp.concatenate(
                [vec[:6, i * quarter : (i + 1) * quarter].reshape(-1), vec[6 + i], vec[6 + parts + i]]
            )
            for i in range(parts)
        ]
    )
    mine = rows[0] + sum(swap_mp(rows[r], r) for r in (1, 2, 3))
    vectors = [mine[i * quarter : (i + 1) * quarter] for i in range(6)]
    f_bup, t_bup_grad = mine[6 * quarter : 6 * quarter + width], mine[6 * quarter + width :]

    ff_outs = [arr((n_ff, block), F32), arr((block, n_ff), F32)]
    attn_outs = [arr((3, block, n_attn), F32), arr((n_attn, block), F32)]
    attn_s.shards()
    f_attn.first()
    grad_na = after(grad_na, attn_s.hold, f_ff.hold, f_attn.hold)
    first = jax.vjp(normalize, stream, gain_a32)[1](grad_na)
    frames_grad = grad_middle + first[0]
    f_attn.middle()
    t_down_grad, t_up_grad = ff_s.last(ff_final_kernel, ff_outs, me)
    f_down_grad, f_up_grad = f_ff.last("ff", ff_outs)
    t_qkv_grad, t_out_grad = attn_s.last(attn_final_kernel, attn_outs, me)
    f_qkv_grad, f_out_grad = f_attn.last("attn", attn_outs)

    def owned(qkv_grad, out_grad, up_grad, down_grad):
        return (
            outer_sum(qkv_grad, 1),
            outer_sum(out_grad, 1),
            outer_sum(up_grad, 0),
            outer_sum(down_grad, 1),
        )

    f = owned(f_qkv_grad, f_out_grad, f_up_grad, f_down_grad)
    t = owned(t_qkv_grad, t_out_grad, t_up_grad, t_down_grad)
    return (
        output,
        frames_grad,
        vectors[0],
        f[0],
        f[1],
        vectors[1],
        f[2],
        f_bup,
        f[3],
        vectors[2],
        vectors[3],
        t[0],
        t[1],
        vectors[4],
        t[2],
        t_bup_grad,
        t[3],
        vectors[5],
    )


def solution(mesh):
    rows = P(("dp", "mp"), None)
    block = (
        P(),
        P(None, None, "mp"),
        P("mp", None),
        P(),
        P(None, "mp"),
        P("mp"),
        P("mp", None),
        P(),
    )
    vec = P(("dp", "mp"))
    block_out = (
        vec,
        P(None, "dp", "mp"),
        P("mp", "dp"),
        vec,
        P("dp", "mp"),
        vec,
        P("mp", "dp"),
        vec,
    )
    return jax.shard_map(
        shards,
        mesh=mesh,
        in_specs=(rows, rows, P("dp", None), rows) + block + block,
        out_specs=(rows, rows) + block_out + block_out,
        check_vma=False,
    )
```

```python
import functools
import math

import jax
import jax.numpy as jnp
from jax import lax
from jax.experimental import pallas as pl
from jax.experimental.pallas import tpu as pltpu
from jax.sharding import PartitionSpec as P

HD = 64
eps = 1e-05
BF = jnp.bfloat16
F32 = jnp.float32


def normalize(stream, gain_vec):
    return stream * lax.rsqrt(jnp.mean(stream * stream, axis=-1, keepdims=True) + eps) * gain_vec


def activate(values):
    return jax.nn.gelu(values, approximate=True)


def dot_nt(a, b):
    return lax.dot_general(a, b, (((1,), (1,)), ((), ())), preferred_element_type=F32)


def dot_nn(a, b):
    return lax.dot_general(a, b, (((1,), (0,)), ((), ())), preferred_element_type=F32)


def dot_tn(a, b):
    return lax.dot_general(a, b, (((0,), (0,)), ((), ())), preferred_element_type=F32)


def gather_rows(rows):
    return lax.all_gather(rows, "mp", axis=0, tiled=True)


def scatter_rows(partial):
    return lax.psum_scatter(
        partial.astype(BF), "mp", scatter_dimension=0, tiled=True
    ).astype(F32)


INNER = 8


def swap_dp(value, bit):
    size = lax.axis_size("dp")
    return lax.ppermute(value, "dp", [(i, i ^ bit) for i in range(size)])


def swap_mp(value, mask):
    size = lax.axis_size("mp")
    return lax.ppermute(value, "mp", [(i, i ^ mask) for i in range(size)])


def my_place():
    return lax.axis_index("dp") % INNER


BITS = [2, 4]
SIDES = [BITS, BITS[::-1]]


def after(value, *marks):
    return lax.optimization_barrier((value,) + tuple(marks))[0]


def all_after(values, *marks):
    return lax.optimization_barrier(tuple(values) + tuple(marks))[: len(values)]


class Gather:
    def __init__(self, piece):
        self.k = piece.shape[1]
        self.piece = piece

    def shards(self, *marks, then=()):
        piece = after(self.piece, *marks) if marks else self.piece
        near = swap_mp(piece, 1)
        far = swap_mp(piece, 2)
        inner = lax.ppermute(piece, "mp", [(1, 2), (2, 1)])
        outer = lax.ppermute(after(far, *then), "mp", [(2, 3), (1, 0)])
        self.held = (near, far, inner, outer)

    def plane_first(self, *marks):
        near, far, inner, outer = all_after(self.held, *marks)
        z = lax.axis_index("mp")
        last = jnp.where((z == 1) | (z == 2), inner, outer)
        half = near.shape[2] // 2
        self.held = []
        for h, side in enumerate(SIDES):
            lanes = slice(h * half, (h + 1) * half)
            whole = jnp.concatenate([near[..., lanes], far[..., lanes], last[..., lanes]], axis=1)
            self.held.append((whole, swap_dp(whole, side[0])))

    def marks(self):
        return [got for _, got in self.held]

    def plane_last(self, *marks):
        held = []
        for (whole, got), side in zip(self.held, SIDES):
            whole, got = all_after((whole, got), *marks)
            low = jnp.concatenate([whole, got], axis=1)
            held.append((low, swap_dp(low, side[1])))
        self.held = held

    def cores(self, *marks):
        held = []
        for low, high in self.held:
            low, high = all_after((low, high), *marks)
            held += [low, high, swap_dp(low, 1), swap_dp(high, 1)]
        self.held = held


def buffer_rows(k):
    out = []
    for h, side in enumerate(SIDES):
        first, last = side[0] // 2, side[1] // 2
        for core in range(2):
            for high in range(2):
                for i in range(2):
                    place = 2 * (i * first + high * last) + core
                    for r in range(3):
                        out.append((h, 4 * h + 2 * core + high, (3 * i + r) * k, place, r + 1))
    return out


def own_rows(shard_rows):
    k = shard_rows.shape[0] // INNER
    return lax.dynamic_slice_in_dim(shard_rows, my_place() * k, k, 0)


def own_cols(shard_cols):
    k = shard_cols.shape[-1] // INNER
    piece = lax.dynamic_slice_in_dim(shard_cols, my_place() * k, k, shard_cols.ndim - 1)
    return jnp.swapaxes(piece, -1, -2)


def by_xor(slots):
    me = my_place()
    for bit in [1] + BITS:
        on = (me & bit) != 0
        slots = [jnp.where(on, slots[i ^ bit], slots[i]) for i in range(len(slots))]
    return slots


def by_xor_mp(slots):
    z = lax.axis_index("mp")
    for bit in (1, 2):
        on = (z & bit) != 0
        slots = [jnp.where(on, slots[i ^ bit], slots[i]) for i in range(len(slots))]
    return slots


def gather_all(value):
    return by_xor_mp([value] + [swap_mp(value, r) for r in (1, 2, 3)])


def gather_rows_p(rows):
    return jnp.concatenate(gather_all(rows), axis=0)


def scatter_rows_p(partial):
    low = partial.astype(BF)
    local = low.shape[0] // 4
    z = lax.axis_index("mp")
    cut = lambda at: lax.dynamic_slice_in_dim(low, at * local, local, 0)
    return cut(z), [swap_mp(cut(z ^ r), r) for r in (1, 2, 3)]


def scatter_plane(value):
    size = lax.axis_size("dp")
    groups = [
        [o + 2 * i + c for i in range(4)] for o in range(0, size, INNER) for c in range(2)
    ]
    return lax.psum_scatter(value, "dp", scatter_dimension=0, axis_index_groups=groups, tiled=True)


def plane_parts(value, *marks):
    if marks:
        value = after(value, *marks)
    block = value.shape[0] // 4
    at = my_place() // 2
    cut = lambda i: lax.dynamic_slice_in_dim(value, i * block, block, 0)
    return cut(at), [swap_dp(cut(at ^ m), 2 * m) for m in (1, 2, 3)]


def scatter_shards(value, n, *marks):
    z = lax.axis_index("mp")
    if marks:
        value = after(value, *marks)
    count = value.shape[1] // (4 * n)

    def cut(at):
        return jnp.concatenate(
            [lax.dynamic_slice_in_dim(value, (4 * i + at) * n, n, 1) for i in range(count)], axis=1
        )

    return cut(z), [swap_mp(cut(z ^ r), r) for r in (1, 2, 3)]


def shards_total(own, sent, *marks):
    sent = all_after(sent, *marks)
    return own.astype(F32) + sent[0].astype(F32) + sent[1].astype(F32) + sent[2].astype(F32)


def d_order(rows):
    outer = lax.axis_size("dp") // INNER
    if outer == 1:
        return rows
    view = rows.reshape(rows.shape[0], outer, INNER, -1)
    return jnp.transpose(view, (0, 2, 1, 3)).reshape(rows.shape)


def outer_sum(value, axis):
    size = lax.axis_size("dp")
    if size == INNER:
        return value
    groups = [[o * INNER + i for o in range(size // INNER)] for i in range(INNER)]
    return lax.psum_scatter(
        value, "dp", scatter_dimension=axis, axis_index_groups=groups, tiled=True
    )


def rsq(x):
    return lax.rsqrt(jnp.mean(x * x, axis=-1, keepdims=True) + eps)


def norm_back(grad, x, gain):
    r = rsq(x)
    xr = x * r
    gg = grad * gain
    return r * (gg - xr * jnp.mean(gg * xr, axis=-1, keepdims=True)), grad * xr


def split_dot(x, table):
    hi = x.astype(BF)
    lo = (x - hi.astype(F32)).astype(BF)
    return dot_nn(hi, table) + dot_nn(lo, table)


PAIRS = [(p, s) for p in range(3) for s in range(p + 1)]


def weight_copies(ids, k, bufs, dst, sem, first):
    half, n = dst.shape[2] // 2, dst.shape[1] // 4
    copies = []
    for i, (h, buf, row, place, hop) in enumerate(buffer_rows(k)):
        at = pl.multiple_of((ids[1] ^ hop) * n + (ids[0] ^ place) * k, k)
        copies.append(
            pltpu.make_async_copy(
                bufs[buf].at[:, pl.ds(row, k)],
                dst.at[:, pl.ds(at, k), pl.ds(h * half, half)],
                sem.at[first + i],
            )
        )
    return copies


COPIES = 48


def attn_weight_copies(ids, own_qkv, own_out, bufs, w, sem):
    n = own_out.shape[0]
    own = pl.ds(pl.multiple_of(ids[1] * n, n), n)
    copies = [
        pltpu.make_async_copy(own_qkv, w.at[pl.ds(0, 3), own], sem.at[0]),
        pltpu.make_async_copy(own_out, w.at[3, own], sem.at[1]),
    ]
    return copies + weight_copies(ids, n // INNER, bufs, w, sem, 2)


def place_pick(p, frames):
    col = lax.broadcasted_iota(jnp.int32, (frames, 3 * frames), 1)
    row = lax.broadcasted_iota(jnp.int32, (frames, 3 * frames), 0)
    return (col == 3 * row + p).astype(BF)


def place_put(p, frames):
    row = lax.broadcasted_iota(jnp.int32, (3 * frames, frames), 0)
    col = lax.broadcasted_iota(jnp.int32, (3 * frames, frames), 1)
    return (row == 3 * col + p).astype(BF)


def frame_out_copies(ids, own, bufs, w, sem):
    n, d = own.shape
    k, half = n // INNER, d // 2
    copies = [pltpu.make_async_copy(own, w.at[0], sem.at[0])]
    for h, buf, row, place, hop in buffer_rows(k):
        at = pl.multiple_of((ids[0] ^ place) * k, k)
        copies.append(
            pltpu.make_async_copy(
                bufs[buf].at[0, pl.ds(row, k)],
                w.at[hop, pl.ds(at, k), pl.ds(h * half, half)],
                sem.at[len(copies)],
            )
        )
    return copies


FRAME_OUT_COPIES = 1 + 48


def frame_out_kernel(ids, m0, m1, m2, m3, frames, gain, own, *rest):
    bufs, (mid_o, nb_o, w, sem) = rest[:8], rest[8:]
    copies = frame_out_copies(ids, own, bufs, w, sem)
    for c in copies:
        c.start()
    for c in copies:
        c.wait()
    mid = frames[...].astype(F32)
    for r, m in enumerate((m0, m1, m2, m3)):
        mid = mid + dot_nn(m[...], w[r])
    mid_o[...] = mid
    nb_o[...] = (mid * rsq(mid) * gain[...]).astype(BF)


def frame_mid_kernel(ids, gnb, mid, grad_out, gain, own, *rest):
    bufs, (gm_o, low_o, dg_o, gx_o, w, sem) = rest[:8], rest[8:]
    copies = frame_out_copies(ids, own, bufs, w, sem)
    for c in copies:
        c.start()
    dx, dg = norm_back(gnb[...], mid[...], gain[...])
    grad = grad_out[...] + dx
    gm_o[...] = grad
    low_o[...] = grad.astype(BF)
    dg_o[...] = jnp.sum(dg, axis=0, keepdims=True)
    for c in copies:
        c.wait()
    for r in range(4):
        gx_o[r] = dot_nt(low_o[...], w[r]).astype(BF)


def token_attn_kernel(ids, fo, emb, cot, valid, ga, gb, table, own_qkv, own_out, *rest):
    bufs, (s_o, g_o, na_o, q_o, k_o, v_o, mix_o, mid_o, nb_o, pr_o, w, sem) = rest[:8], rest[8:]
    copies = attn_weight_copies(ids, own_qkv, own_out, bufs, w, sem)
    for c in copies:
        c.start()
    frames = fo.shape[0]
    places = [pl.ds(p * frames, frames) for p in range(3)]
    for p in range(3):
        pick = place_pick(p, frames)
        g = dot_nn(pick, cot[...])
        g_o[places[p]] = jnp.where(valid[...] > 0.0, g, 0.0).astype(BF)
        s = fo[...] + dot_nn(pick, emb[...])
        s_o[places[p]] = s
        na_o[places[p]] = (s * rsq(s) * ga[...]).astype(BF)
    for c in copies:
        c.wait()
    for t, out in enumerate((q_o, k_o, v_o)):
        out[...] = dot_nt(na_o[...], w[t]).astype(BF)
    scale = 1.0 / math.sqrt(HD)
    for p in range(3):
        scores = [
            split_dot(q_o[places[p]].astype(F32) * k_o[places[s]].astype(F32), table[...]) * scale
            for s in range(p + 1)
        ]
        top = scores[0]
        for x in scores[1:]:
            top = jnp.maximum(top, x)
        ex = [jnp.exp(x - top) for x in scores]
        total = ex[0]
        for x in ex[1:]:
            total = total + x
        mixed = None
        for s in range(p + 1):
            prob = ex[s] / total
            pr_o[PAIRS.index((p, s))] = prob
            term = dot_nt(prob.astype(BF), table[...]) * v_o[places[s]].astype(F32)
            mixed = term if mixed is None else mixed + term
        mix_o[places[p]] = mixed.astype(BF)
    for p in places:
        mid = s_o[p] + dot_nn(mix_o[p], w[3])
        mid_o[p] = mid
        nb_o[p] = (mid * rsq(mid) * gb[...]).astype(BF)


def token_back_kernel(ids, g, gnb, mid, s_in, ga, gb, q, k, v, mix, pr, table, own_qkv, own_out, *rest):
    bufs, (ml_o, left_o, gf_o, da_o, db_o, w, gm, gx, sem) = rest[:8], rest[8:]
    copies = attn_weight_copies(ids, own_qkv, own_out, bufs, w, sem)
    for c in copies:
        c.start()
    frames, feats = gf_o.shape[0], q.shape[1]
    places = [pl.ds(p * frames, frames) for p in range(3)]
    lanes = [pl.ds(t * feats, feats) for t in range(4)]
    total = None
    for p in places:
        dx, dg = norm_back(gnb[p], mid[p], gb[...])
        grad = g[p].astype(F32) + dx
        gm[p] = grad
        ml_o[p] = grad.astype(BF)
        row = jnp.sum(dg, axis=0, keepdims=True)
        total = row if total is None else total + row
    db_o[...] = total
    left_o[:, lanes[3]] = mix[...]
    for c in copies:
        c.wait()
    gx[...] = dot_nt(ml_o[...], w[3]).astype(BF)
    scale = 1.0 / math.sqrt(HD)
    kg, vg = {}, {}
    for p in range(3):
        gp = [
            split_dot(gx[places[p]].astype(F32) * v[places[s]].astype(F32), table[...])
            for s in range(p + 1)
        ]
        probs = [pr[PAIRS.index((p, s))] for s in range(p + 1)]
        delta = probs[0] * gp[0]
        for s in range(1, p + 1):
            delta = delta + probs[s] * gp[s]
        query = None
        for s in range(p + 1):
            wide = dot_nt((probs[s] * (gp[s] - delta)).astype(BF), table[...])
            term = wide * k[places[s]].astype(F32)
            query = term if query is None else query + term
            key = wide * q[places[p]].astype(F32) * scale
            value = dot_nt(probs[s].astype(BF), table[...]) * gx[places[p]].astype(F32)
            if p == s:
                kg[s], vg[s] = key, value
            else:
                kg[s], vg[s] = kg[s] + key, vg[s] + value
        left_o[places[p], lanes[0]] = (query * scale).astype(BF)
    for s in range(3):
        left_o[places[s], lanes[1]] = kg[s].astype(BF)
        left_o[places[s], lanes[2]] = vg[s].astype(BF)
    gna = dot_nn(left_o[:, lanes[0]], w[0]) + dot_nn(left_o[:, lanes[1]], w[1]) + dot_nn(left_o[:, lanes[2]], w[2])
    total = out = None
    for i, p in enumerate(places):
        dx, dg = norm_back(gna[i * frames : (i + 1) * frames], s_in[p], ga[...])
        grad = gm[p] + dx
        row = jnp.sum(dg, axis=0, keepdims=True)
        total = row if total is None else total + row
        out = grad if out is None else out + grad
    da_o[...] = total
    gf_o[...] = out


GELU_S = math.sqrt(2.0 / math.pi)


def gelu_both(u):
    u2 = u * u
    t = jnp.tanh(GELU_S * (u + 0.044715 * (u2 * u)))
    h = 0.5 * (1.0 + t)
    return u * h, h + 0.5 * u * (1.0 - t * t) * (GELU_S * (1.0 + 3.0 * 0.044715 * u2))


def token_ff_kernel(step, ids, nb, g, mid, valid, bias, bdown, own_up, own_down, *rest):
    bufs, (out_o, gnb_o, left_o, gb_o, wuo, wdo, w, acc, sem) = rest[:8], rest[8:]
    n, frames = own_down.shape[0], valid.shape[0]
    own = [
        pltpu.make_async_copy(own_up, wuo, sem.at[0]),
        pltpu.make_async_copy(own_down, wdo, sem.at[1]),
    ]
    copies = weight_copies(ids, n // INNER, bufs, w, sem, 2)
    z = ids[1]
    for c in own + copies:
        c.start()
    acc[...] = jnp.zeros_like(acc)
    gnb_o[...] = jnp.zeros_like(gnb_o)

    def middle(at, size, pre, back):
        cols = pl.ds(at, size)
        h, dh = gelu_both(pre + bias[:, cols])
        h = h.astype(BF)
        gp = (dh * back).astype(BF)
        left_o[:, cols] = h
        left_o[:, pl.ds(pl.multiple_of(4 * n + at, 128), size)] = gp
        gb_o[:, cols] = jnp.sum(gp.astype(F32), axis=0, keepdims=True)
        return h, gp

    for c in own:
        c.wait()
    own_step = n // 2

    def own_block(j, carry):
        cols = pl.ds(pl.multiple_of(j * own_step, own_step), own_step)
        pre = dot_nn(nb[...], wuo[:, cols])
        back = dot_nt(g[...], wdo[cols, :])
        h, gp = middle(pl.multiple_of(z * n + j * own_step, own_step), own_step, pre, back)
        acc[...] += dot_nn(h, wdo[cols, :])
        gnb_o[...] += dot_nt(gp, wuo[:, cols])
        return carry

    lax.fori_loop(0, n // own_step, own_block, 0)
    for c in copies:
        c.wait()

    def block(j, carry):
        at = pl.multiple_of(j * step + jnp.where(j * step >= z * n, n, 0), step)
        rows = pl.ds(at, step)
        pre = dot_nt(nb[...], w[0, rows, :])
        back = dot_nt(g[...], w[1, rows, :])
        h, gp = middle(at, step, pre, back)
        acc[...] += dot_nn(h, w[1, rows, :])
        gnb_o[...] += dot_nn(gp, w[0, rows, :])
        return carry

    lax.fori_loop(0, 3 * n // step, block, 0)
    out = None
    for p in range(3):
        rows = pl.ds(p * frames, frames)
        val = jnp.where(valid[...] > 0.0, acc[rows] + mid[rows] + bdown[...], 0.0).astype(BF)
        term = dot_nn(place_put(p, frames), val)
        out = term if out is None else out + term
    out_o[...] = out.astype(BF)


def lay_right(dst, row, col, right, core, block):
    for i in range(INNER // 2):
        at = pl.multiple_of((2 * i + core) * block, block)
        dst[pl.ds(row + i * block, block), pl.ds(col, right.shape[1])] = right[pl.ds(at, block), :]


def pair_grad_kernel(new, ids, lm, lt, rm, rt, out, tmp, am):
    @pl.when(new(pl.program_id(0)))
    def _():
        for i, src in enumerate((rm, rt)):
            tmp[...] = jnp.transpose(src[0])
            lay_right(am, 0, i * src.shape[1], tmp, ids[0] & 1, src.shape[2] // INNER)

    out[...] = dot_nn(am[...], jnp.concatenate([lm[...], lt[...]], axis=0)).astype(BF)


def frame_grad_kernel(new, ids, left, right, same, cross, tmp, am):
    d = right.shape[2]

    @pl.when(new(pl.program_id(0)))
    def _():
        tmp[...] = jnp.transpose(right[0])
        for i in range(2):
            lay_right(am, i * (d // 2), 0, tmp, (ids[0] & 1) ^ i, d // INNER)

    total = dot_nn(am[...], left[...])
    same[...] = total[: d // 2].astype(BF)
    cross[...] = total[d // 2 :].astype(BF)


VMEM_LIMIT = 60 * 1024 * 1024


def arr(shape, dtype):
    return jax.ShapeDtypeStruct(shape, dtype)


def cost(flops, ins, outs):
    size = sum(a.size * a.dtype.itemsize for a in ins) + sum(
        math.prod(o.shape) * o.dtype.itemsize for o in outs
    )
    return pl.CostEstimate(flops=flops, bytes_accessed=size, transcendentals=0)


def call(kernel, outs, ins, scratch, any_from, flops, smem=0):
    def space(i):
        return pltpu.SMEM if i < smem else pltpu.VMEM if i < any_from else pl.ANY

    return pl.pallas_call(
        kernel,
        out_shape=outs,
        in_specs=[pl.BlockSpec(memory_space=space(i)) for i in range(len(ins))],
        out_specs=[pl.BlockSpec(memory_space=pltpu.VMEM)] * len(outs),
        scratch_shapes=scratch,
        compiler_params=pltpu.CompilerParams(vmem_limit_bytes=VMEM_LIMIT),
        cost_estimate=cost(flops, ins, outs),
    )(*ins)


def frame_out(ids, mixed, frames, gain, own, bufs):
    rows, d = frames.shape
    ins = [ids, *mixed, frames, gain, own, *bufs]
    scratch = [pltpu.VMEM((4, *own.shape), BF), pltpu.SemaphoreType.DMA((FRAME_OUT_COPIES,))]
    outs = [arr((rows, d), F32), arr((rows, d), BF)]
    return call(frame_out_kernel, outs, ins, scratch, 7, 8 * rows * own.size, smem=1)


def frame_mid(ids, gnb, mid, grad_out, gain, own, bufs):
    rows, d = mid.shape
    ins = [ids, gnb, mid, grad_out, gain, own, *bufs]
    scratch = [pltpu.VMEM((4, *own.shape), BF), pltpu.SemaphoreType.DMA((FRAME_OUT_COPIES,))]
    outs = [arr((rows, d), F32), arr((rows, d), BF), arr((1, d), F32), arr((4, rows, own.shape[0]), BF)]
    return call(frame_mid_kernel, outs, ins, scratch, 5, 8 * rows * own.size, smem=1)


def token_attn(ids, fo, emb, cot, valid, ga, gb, table, own_qkv, own_out, bufs):
    frames, d = fo.shape
    rows, feats = 3 * frames, table.shape[0]
    outs = (
        [arr((rows, d), F32), arr((rows, d), BF), arr((rows, d), BF)]
        + [arr((rows, feats), BF)] * 4
        + [arr((rows, d), F32), arr((rows, d), BF), arr((len(PAIRS), frames, table.shape[1]), F32)]
    )
    return call(
        token_attn_kernel,
        outs,
        [ids, fo, emb, cot, valid, ga, gb, table, own_qkv, own_out, *bufs],
        [pltpu.VMEM((4, feats, d), BF), pltpu.SemaphoreType.DMA((2 + COPIES,))],
        8,
        8 * rows * feats * d,
        smem=1,
    )


def token_back(ids, g, gnb, mid, s, ga, gb, q, k, v, mix, pr, table, own_qkv, own_out, bufs):
    rows, d = s.shape
    frames, feats = rows // 3, table.shape[0]
    outs = [
        arr((rows, d), BF),
        arr((rows, 4 * feats), BF),
        arr((frames, d), F32),
        arr((1, d), F32),
        arr((1, d), F32),
    ]
    return call(
        token_back_kernel,
        outs,
        [ids, g, gnb, mid, s, ga, gb, q, k, v, mix, pr, table, own_qkv, own_out, *bufs],
        [
            pltpu.VMEM((4, feats, d), BF),
            pltpu.VMEM((rows, d), F32),
            pltpu.VMEM((rows, feats), BF),
            pltpu.SemaphoreType.DMA((2 + COPIES,)),
        ],
        13,
        8 * rows * feats * d,
        smem=1,
    )


def token_ff(ids, nb, g, mid, valid, bias, bdown, own_up, own_down, bufs):
    rows, d = nb.shape
    n = own_down.shape[0]
    outs = [
        arr((rows, d), BF),
        arr((rows, d), F32),
        arr((rows, 8 * n), BF),
        arr((1, 4 * n), F32),
    ]
    return call(
        functools.partial(token_ff_kernel, 512),
        outs,
        [ids, nb, g, mid, valid, bias, bdown, own_up, own_down, *bufs],
        [
            pltpu.VMEM((d, n), BF),
            pltpu.VMEM((n, d), BF),
            pltpu.VMEM((2, 4 * n, d), BF),
            pltpu.VMEM((rows, d), F32),
            pltpu.SemaphoreType.DMA((2 + COPIES,)),
        ],
        7,
        32 * rows * n * d,
        smem=1,
    )


def smem_spec():
    return pl.BlockSpec(memory_space=pltpu.SMEM)


def pair_grad(ids, left, left_other, rights, rights_other, split):
    rows, units = left.shape
    d = rights.shape[2]
    step = d
    at = split // step
    pick = lambda j: jnp.where(j < at, 0, 1)
    outs = [arr((d // 2, units), BF)]
    [out] = pl.pallas_call(
        functools.partial(pair_grad_kernel, lambda j: (j == 0) | (j == at)),
        grid=(units // step,),
        in_specs=[smem_spec()]
        + [pl.BlockSpec((rows, step), lambda j: (0, j))] * 2
        + [pl.BlockSpec((1, rows, d), lambda j: (pick(j), 0, 0))] * 2,
        out_specs=[pl.BlockSpec((d // 2, step), lambda j: (0, j))],
        out_shape=outs,
        scratch_shapes=[pltpu.VMEM((d, rows), BF), pltpu.VMEM((d // 2, 2 * rows), BF)],
        compiler_params=pltpu.CompilerParams(vmem_limit_bytes=VMEM_LIMIT),
        cost_estimate=cost(2 * rows * units * d, [left, left_other, rights, rights_other], outs),
    )(ids, left, left_other, rights, rights_other)
    return out


def frame_grad(ids, left, rights, split):
    rows, units = left.shape
    d = rights.shape[2]
    step = units // 4
    at = split // step
    outs = [arr((d // 2, units), BF)] * 2
    return pl.pallas_call(
        functools.partial(frame_grad_kernel, lambda j: (j == 0) | (j == at)),
        grid=(4,),
        in_specs=[
            smem_spec(),
            pl.BlockSpec((rows, step), lambda j: (0, j)),
            pl.BlockSpec((1, rows, d), lambda j: (jnp.where(j < at, 0, 1), 0, 0)),
        ],
        out_specs=[pl.BlockSpec((d // 2, step), lambda j: (0, j))] * 2,
        out_shape=outs,
        scratch_shapes=[pltpu.VMEM((d, rows), BF)] * 2,
        compiler_params=pltpu.CompilerParams(vmem_limit_bytes=VMEM_LIMIT),
        cost_estimate=cost(2 * rows * units * d, [left, rights], outs),
    )(ids, left, rights)


def segments(lengths, whole_rows):
    count = lengths.shape[1]
    order = jnp.arange(count, dtype=jnp.int32)
    item_ends = jnp.sum(
        jnp.where(order[None, :] <= order[:, None], lengths[0][None, :], 0), axis=1, dtype=jnp.int32
    )
    positions = jnp.arange(whole_rows, dtype=jnp.int32)
    segment = jnp.sum(
        (positions[:, None] >= item_ends[None, :]).astype(jnp.int32), axis=1, dtype=jnp.int32
    )
    is_valid = positions < jnp.sum(lengths[0], dtype=jnp.int32)
    segment = jnp.where(is_valid, segment, positions + count)
    return (segment, is_valid)


def frame_allowed(segment):
    positions = jnp.arange(segment.shape[0], dtype=jnp.int32)
    return (positions[None, :] <= positions[:, None]) & (segment[None, :] == segment[:, None])


def split_heads(rows):
    return rows.reshape(rows.shape[0], rows.shape[1] // HD, HD)


def frame_forward(qkv_rows, segment):
    queries, key_rows, value_rows = (split_heads(qkv_rows[t]) for t in range(3))
    raw_scores = jnp.einsum("qhe,khe->hqk", queries, key_rows, preferred_element_type=F32) * (
        1.0 / math.sqrt(HD)
    )
    scores = jnp.where(frame_allowed(segment)[None], raw_scores, -1e30)
    top_score = jnp.max(scores, axis=-1, keepdims=True)
    exp_scores = jnp.exp(scores - top_score)
    exp_total = jnp.sum(exp_scores, axis=-1, keepdims=True)
    attn_probs = (exp_scores / exp_total).astype(BF)
    mixed = jnp.einsum("hqk,khe->qhe", attn_probs, value_rows, preferred_element_type=F32)
    log_total = top_score[:, :, 0] + jnp.log(exp_total[:, :, 0])
    return (mixed.astype(BF).reshape(qkv_rows.shape[1], -1), log_total)


def frame_backward(qkv_rows, log_total, grad_mixed, segment):
    queries, key_rows, value_rows = (split_heads(qkv_rows[t]) for t in range(3))
    grad_heads = split_heads(grad_mixed)
    scale = 1.0 / math.sqrt(HD)
    raw_scores = jnp.einsum("qhe,khe->hqk", queries, key_rows, preferred_element_type=F32) * scale
    scores = jnp.where(frame_allowed(segment)[None], raw_scores, -1e30)
    attn_probs = jnp.exp(scores - log_total[:, :, None])
    value_grad = jnp.einsum(
        "hqk,qhe->khe", attn_probs.astype(BF), grad_heads, preferred_element_type=F32
    )
    grad_probs = jnp.einsum("qhe,khe->hqk", grad_heads, value_rows, preferred_element_type=F32)
    row_delta = jnp.sum(attn_probs * grad_probs, axis=-1, keepdims=True)
    grad_scores = (attn_probs * (grad_probs - row_delta)).astype(BF)
    query_grad = jnp.einsum("hqk,khe->qhe", grad_scores, key_rows, preferred_element_type=F32) * scale
    key_grad = jnp.einsum("hqk,qhe->khe", grad_scores, queries, preferred_element_type=F32) * scale
    rows = qkv_rows.shape[1]
    return [g.reshape(rows, -1).astype(BF) for g in (query_grad, key_grad, value_grad)]


def head_table(features):
    at = jnp.arange(features, dtype=jnp.int32)
    return ((at // HD)[:, None] == jnp.arange(128, dtype=jnp.int32)[None, :]).astype(BF)


def shards(frames, codes_embed, lengths, cotangent, *params):
    gain_a, w_qkv, w_out, gain_b, w_up, b_up, w_down, b_down = params[:8]
    t_gain_a, t_qkv, t_out, t_gain_b, t_up, t_bup, t_down, t_bdown = params[8:]
    dp, parts = lax.axis_size("dp"), lax.axis_size("mp")
    z = lax.axis_index("mp")
    ids = jnp.stack([my_place(), z]).astype(jnp.int32)
    local, d = frames.shape
    n_attn, n_ff = w_out.shape[0], w_down.shape[0]
    block = d // INNER
    segment, is_valid = segments(lengths, local * parts)
    valid = lax.dynamic_slice_in_dim(is_valid, z * local, local, 0).astype(F32)[:, None]

    stream = frames.astype(F32)
    gain_a32, gain_b32 = gain_a.astype(F32), gain_b.astype(F32)
    normed_a = normalize(stream, gain_a32).astype(BF)
    gathered_a = gather_rows(normed_a)

    attn_w = Gather(jnp.concatenate([own_cols(t_qkv), own_rows(t_out)[None]], axis=0))
    ff_w = Gather(jnp.stack([own_cols(t_up), own_rows(t_down)]))
    out_w = Gather(own_rows(w_out)[None])
    out_w.shards()
    out_w.plane_first()
    out_w.plane_last()
    out_w.cores()
    attn_w.shards()
    gathered_a = after(gathered_a, *out_w.held, *attn_w.held)

    qkv_rows = jnp.einsum("rd,tde->tre", gathered_a, w_qkv, preferred_element_type=F32).astype(BF)
    mixed_rows, log_total = frame_forward(qkv_rows, segment)
    by_rows = [
        lax.dynamic_slice_in_dim(mixed_rows, (z ^ r) * local, local, 0) for r in range(parts)
    ]
    mixed_own = [by_rows[0]] + [swap_mp(by_rows[r], r) for r in range(1, parts)]

    attn_w.plane_first(mixed_rows)
    middle, normed_b = frame_out(ids, mixed_own, frames, gain_b32[None], w_out, out_w.held)
    ff_w.shards(normed_b)
    gathered_b = gather_rows(normed_b)

    attn_w.plane_last(normed_b)
    ff_w.plane_first(normed_b)
    gathered_b = after(gathered_b, *attn_w.marks(), *ff_w.marks())

    hidden_pre = dot_nn(gathered_b, w_up) + b_up.astype(F32)
    hidden = activate(hidden_pre).astype(BF)
    part_b = dot_nn(hidden, w_down).astype(BF)
    branch_b = scatter_rows(part_b)

    attn_w.cores(part_b)
    ff_w.plane_last(part_b)
    f_result = middle + after(branch_b, *attn_w.held, *ff_w.marks()) + b_down.astype(F32)

    t_bias = jnp.concatenate(gather_all(t_bup)).astype(F32)[None]
    own_qkv = jnp.transpose(t_qkv, (0, 2, 1))
    table = head_table(n_attn * parts)
    tga, tgb = t_gain_a.astype(F32)[None], t_gain_b.astype(F32)[None]

    attn_bufs = attn_w.held
    t_stream, g_low, t_na, q, k, v, mixed, t_middle, t_nb, probs = token_attn(
        ids, f_result, codes_embed, cotangent, valid, tga, tgb, table, own_qkv, t_out, attn_bufs
    )
    ff_w.cores()
    output, t_gnb, t_left, t_gbup = token_ff(
        ids, t_nb, g_low, t_middle, valid, t_bias, t_bdown.astype(F32)[None], t_up, t_down, ff_w.held
    )
    rights = jnp.stack([d_order(g_low), d_order(t_nb)])
    rights_other = swap_dp(rights, 1)
    left_other = swap_dp(t_left, 1)
    m_low, a_left, grad_frame, t_da, t_db = token_back(
        ids, g_low, t_gnb, t_middle, t_stream, tga, tgb, q, k, v, mixed, probs, table, own_qkv, t_out, attn_bufs
    )
    t_dbd = jnp.sum(g_low.astype(F32), axis=0)

    ff_grad = pair_grad(ids, after(t_left, grad_frame), left_other, rights, rights_other, 4 * n_ff)
    ff_sum = scatter_plane(ff_grad)
    grad_low = grad_frame.astype(BF)
    gathered_down = gather_rows_p(grad_low)
    a_rights = jnp.stack([d_order(t_na), d_order(m_low)])
    a_rights_other = swap_dp(a_rights, 1)
    a_other = swap_dp(a_left, 1)
    gathered_down = after(gathered_down, ff_grad)
    grad_hidden = dot_nt(gathered_down, w_down)
    grad_pre = jax.vjp(activate, hidden_pre)[1](grad_hidden)[0].astype(BF)
    part_c = dot_nt(grad_pre, w_up).astype(BF)
    grad_nb = shards_total(*scatter_rows_p(part_c))

    attn_grad = pair_grad(ids, after(a_left, part_c), a_other, a_rights, a_rights_other, 3 * n_attn * parts)
    f_left = jnp.concatenate([hidden, grad_pre], axis=1)
    ff_same, ff_cross = frame_grad(
        ids, after(f_left, part_c), jnp.stack([d_order(gathered_down), d_order(gathered_b)]), n_ff
    )
    ff_cross = swap_dp(ff_cross, 1)
    grad_nb = after(grad_nb, attn_grad, ff_same)
    grad_middle, mid_low, f_db, pieces = frame_mid(
        ids, grad_nb, middle, grad_frame, gain_b32[None], w_out, out_w.held
    )
    gathered_mid = gather_rows_p(mid_low)
    grad_mixed = jnp.concatenate(
        by_xor_mp([pieces[0]] + [swap_mp(pieces[r], r) for r in range(1, parts)]), axis=0
    )
    grad_qkv = jnp.concatenate(frame_backward(qkv_rows, log_total, grad_mixed, segment), axis=1)
    w_all = jnp.concatenate([w_qkv[0], w_qkv[1], w_qkv[2]], axis=1)
    part_d32 = dot_nt(grad_qkv, w_all)
    part_d = after(part_d32.astype(BF), ff_sum, gathered_mid)
    attn_sum = scatter_plane(after(attn_grad, ff_sum))
    attn_same, attn_cross = frame_grad(
        ids,
        jnp.concatenate([grad_qkv, mixed_rows], axis=1),
        jnp.stack([d_order(gathered_a), d_order(gathered_mid)]),
        3 * n_attn,
    )
    attn_cross = swap_dp(attn_cross, 1)
    part_d = after(part_d, attn_same)
    f_ff_value = (ff_same.astype(F32) + ff_cross.astype(F32)).astype(BF)
    f_attn_value = (attn_same.astype(F32) + attn_cross.astype(F32)).astype(BF)
    na_parts = scatter_rows_p(part_d)
    ff_z = scatter_shards(ff_sum, n_ff, part_d)
    f_ff_parts = plane_parts(f_ff_value, part_d)
    f_attn_parts = plane_parts(f_attn_value, part_d)
    grad_na = shards_total(*na_parts)
    first = jax.vjp(normalize, stream, gain_a32)[1](grad_na)
    frames_grad = grad_middle + first[0]
    attn_z = scatter_shards(after(attn_sum, grad_na), n_attn)
    f_da = jnp.sum(part_d32 * gathered_a.astype(F32), axis=0) / gain_a32

    wide = lax.dynamic_update_slice_in_dim(
        jnp.zeros((parts, n_ff), F32), jnp.sum(grad_pre.astype(F32), axis=0)[None], z, 0
    )

    def by_owner(full):
        return jnp.transpose(full.reshape(dp, parts, -1), (1, 0, 2)).reshape(parts, -1)

    vec = jnp.concatenate(
        [
            jnp.stack([f_da, f_db[0], jnp.sum(grad_frame, axis=0), t_da[0], t_db[0], t_dbd]),
            by_owner(wide),
            by_owner(t_gbup[0]),
        ],
        axis=0,
    )
    vec = d_order(after(vec, part_d))
    vec = jnp.concatenate(by_xor([vec[:, i * block : (i + 1) * block] for i in range(INNER)]), axis=1)
    for bit in (4, 2, 1):
        half = vec.shape[1] // 2
        vec = vec[:, :half] + swap_dp(vec[:, half:], bit)
    vec = outer_sum(vec, 1)
    width = vec.shape[1]
    quarter = width // parts
    rows = by_xor_mp(
        [
            jnp.concatenate(
                [vec[:6, i * quarter : (i + 1) * quarter].reshape(-1), vec[6 + i], vec[6 + parts + i]]
            )
            for i in range(parts)
        ]
    )
    mine = rows[0] + sum(swap_mp(rows[r], r) for r in (1, 2, 3))
    vectors = [mine[i * quarter : (i + 1) * quarter] for i in range(6)]
    f_bup, t_bup_grad = mine[6 * quarter : 6 * quarter + width], mine[6 * quarter + width :]

    t_ff = shards_total(*ff_z, mine)
    f_ff = shards_total(*f_ff_parts, mine)

    def ff_split(total):
        return total[:, :n_ff].T, total[:, n_ff:]

    def attn_split(total):
        rows = total.reshape(block, 4, n_attn)
        return jnp.transpose(rows[:, :3], (1, 0, 2)), total[:, 3 * n_attn :].T

    t_down_grad, t_up_grad = ff_split(t_ff)
    f_down_grad, f_up_grad = ff_split(f_ff)
    f_qkv_grad, f_out_grad = attn_split(shards_total(*f_attn_parts, mine))
    t_qkv_grad, t_out_grad = attn_split(shards_total(*attn_z, t_ff))

    def owned(qkv_grad, out_grad, up_grad, down_grad):
        return (
            outer_sum(qkv_grad, 1),
            outer_sum(out_grad, 1),
            outer_sum(up_grad, 0),
            outer_sum(down_grad, 1),
        )

    f = owned(f_qkv_grad, f_out_grad, f_up_grad, f_down_grad)
    t = owned(t_qkv_grad, t_out_grad, t_up_grad, t_down_grad)
    return (
        output,
        frames_grad,
        vectors[0],
        f[0],
        f[1],
        vectors[1],
        f[2],
        f_bup,
        f[3],
        vectors[2],
        vectors[3],
        t[0],
        t[1],
        vectors[4],
        t[2],
        t_bup_grad,
        t[3],
        vectors[5],
    )


def solution(mesh):
    rows = P(("dp", "mp"), None)
    block = (
        P(),
        P(None, None, "mp"),
        P("mp", None),
        P(),
        P(None, "mp"),
        P("mp"),
        P("mp", None),
        P(),
    )
    vec = P(("dp", "mp"))
    block_out = (
        vec,
        P(None, "dp", "mp"),
        P("mp", "dp"),
        vec,
        P("dp", "mp"),
        vec,
        P("mp", "dp"),
        vec,
    )
    return jax.shard_map(
        shards,
        mesh=mesh,
        in_specs=(rows, rows, P("dp", None), rows) + block + block,
        out_specs=(rows, rows) + block_out + block_out,
        check_vma=False,
    )
```

```python
import functools
import math

import jax
import jax.numpy as jnp
from jax import lax
from jax.experimental import pallas as pl
from jax.experimental.pallas import tpu as pltpu
from jax.sharding import PartitionSpec as P

HD = 64
eps = 1e-05
BF = jnp.bfloat16
F32 = jnp.float32


def normalize(stream, gain_vec):
    return stream * lax.rsqrt(jnp.mean(stream * stream, axis=-1, keepdims=True) + eps) * gain_vec


def activate(values):
    return jax.nn.gelu(values, approximate=True)


def dot_nt(a, b):
    return lax.dot_general(a, b, (((1,), (1,)), ((), ())), preferred_element_type=F32)


def dot_nn(a, b):
    return lax.dot_general(a, b, (((1,), (0,)), ((), ())), preferred_element_type=F32)


def dot_tn(a, b):
    return lax.dot_general(a, b, (((0,), (0,)), ((), ())), preferred_element_type=F32)


def gather_rows(rows):
    return lax.all_gather(rows, "mp", axis=0, tiled=True)


def scatter_rows(partial):
    return lax.psum_scatter(
        partial.astype(BF), "mp", scatter_dimension=0, tiled=True
    ).astype(F32)


INNER = 8


def swap_dp(value, bit):
    size = lax.axis_size("dp")
    return lax.ppermute(value, "dp", [(i, i ^ bit) for i in range(size)])


def swap_mp(value, mask):
    size = lax.axis_size("mp")
    return lax.ppermute(value, "mp", [(i, i ^ mask) for i in range(size)])


def my_place():
    return lax.axis_index("dp") % INNER


BITS = [2, 4]
SIDES = [BITS, BITS[::-1]]


def after(value, *marks):
    return lax.optimization_barrier((value,) + tuple(marks))[0]


def all_after(values, *marks):
    return lax.optimization_barrier(tuple(values) + tuple(marks))[: len(values)]


class Gather:
    def __init__(self, piece):
        self.k = piece.shape[1]
        self.piece = piece

    def shards(self, *marks, then=()):
        piece = after(self.piece, *marks) if marks else self.piece
        near = swap_mp(piece, 1)
        far = swap_mp(piece, 2)
        inner = lax.ppermute(piece, "mp", [(1, 2), (2, 1)])
        outer = lax.ppermute(after(far, *then), "mp", [(2, 3), (1, 0)])
        self.held = (near, far, inner, outer)

    def plane_first(self, *marks):
        near, far, inner, outer = all_after(self.held, *marks)
        z = lax.axis_index("mp")
        last = jnp.where((z == 1) | (z == 2), inner, outer)
        half = near.shape[2] // 2
        self.held = []
        for h, side in enumerate(SIDES):
            lanes = slice(h * half, (h + 1) * half)
            whole = jnp.concatenate([near[..., lanes], far[..., lanes], last[..., lanes]], axis=1)
            self.held.append((whole, swap_dp(whole, side[0])))

    def marks(self):
        return [got for _, got in self.held]

    def plane_last(self, *marks):
        held = []
        for (whole, got), side in zip(self.held, SIDES):
            whole, got = all_after((whole, got), *marks)
            low = jnp.concatenate([whole, got], axis=1)
            held.append((low, swap_dp(low, side[1])))
        self.held = held

    def cores(self, *marks):
        held = []
        for low, high in self.held:
            low, high = all_after((low, high), *marks)
            held += [low, high, swap_dp(low, 1), swap_dp(high, 1)]
        self.held = held


def buffer_rows(k):
    out = []
    for h, side in enumerate(SIDES):
        first, last = side[0] // 2, side[1] // 2
        for core in range(2):
            for high in range(2):
                for i in range(2):
                    place = 2 * (i * first + high * last) + core
                    for r in range(3):
                        out.append((h, 4 * h + 2 * core + high, (3 * i + r) * k, place, r + 1))
    return out


def own_rows(shard_rows):
    k = shard_rows.shape[0] // INNER
    return lax.dynamic_slice_in_dim(shard_rows, my_place() * k, k, 0)


def own_cols(shard_cols):
    k = shard_cols.shape[-1] // INNER
    piece = lax.dynamic_slice_in_dim(shard_cols, my_place() * k, k, shard_cols.ndim - 1)
    return jnp.swapaxes(piece, -1, -2)


def by_xor(slots):
    me = my_place()
    for bit in [1] + BITS:
        on = (me & bit) != 0
        slots = [jnp.where(on, slots[i ^ bit], slots[i]) for i in range(len(slots))]
    return slots


def by_xor_mp(slots):
    z = lax.axis_index("mp")
    for bit in (1, 2):
        on = (z & bit) != 0
        slots = [jnp.where(on, slots[i ^ bit], slots[i]) for i in range(len(slots))]
    return slots


def gather_all(value):
    return by_xor_mp([value] + [swap_mp(value, r) for r in (1, 2, 3)])


def gather_rows_p(rows):
    return jnp.concatenate(gather_all(rows), axis=0)


def scatter_rows_p(partial):
    low = partial.astype(BF)
    local = low.shape[0] // 4
    z = lax.axis_index("mp")
    cut = lambda at: lax.dynamic_slice_in_dim(low, at * local, local, 0)
    return cut(z), [swap_mp(cut(z ^ r), r) for r in (1, 2, 3)]


def scatter_plane(value):
    size = lax.axis_size("dp")
    groups = [
        [o + 2 * i + c for i in range(4)] for o in range(0, size, INNER) for c in range(2)
    ]
    return lax.psum_scatter(value, "dp", scatter_dimension=0, axis_index_groups=groups, tiled=True)


def plane_parts(value, *marks):
    if marks:
        value = after(value, *marks)
    block = value.shape[0] // 4
    at = my_place() // 2
    cut = lambda i: lax.dynamic_slice_in_dim(value, i * block, block, 0)
    return cut(at), [swap_dp(cut(at ^ m), 2 * m) for m in (1, 2, 3)]


def scatter_shards(value, n, *marks):
    z = lax.axis_index("mp")
    if marks:
        value = after(value, *marks)
    count = value.shape[1] // (4 * n)

    def cut(at):
        return jnp.concatenate(
            [lax.dynamic_slice_in_dim(value, (4 * i + at) * n, n, 1) for i in range(count)], axis=1
        )

    return cut(z), [swap_mp(cut(z ^ r), r) for r in (1, 2, 3)]


def shards_total(own, sent, *marks):
    sent = all_after(sent, *marks)
    return own.astype(F32) + sent[0].astype(F32) + sent[1].astype(F32) + sent[2].astype(F32)


def d_order(rows):
    outer = lax.axis_size("dp") // INNER
    if outer == 1:
        return rows
    view = rows.reshape(rows.shape[0], outer, INNER, -1)
    return jnp.transpose(view, (0, 2, 1, 3)).reshape(rows.shape)


def outer_sum(value, axis):
    size = lax.axis_size("dp")
    if size == INNER:
        return value
    groups = [[o * INNER + i for o in range(size // INNER)] for i in range(INNER)]
    return lax.psum_scatter(
        value, "dp", scatter_dimension=axis, axis_index_groups=groups, tiled=True
    )


def rsq(x):
    return lax.rsqrt(jnp.mean(x * x, axis=-1, keepdims=True) + eps)


def norm_back(grad, x, gain):
    r = rsq(x)
    xr = x * r
    gg = grad * gain
    return r * (gg - xr * jnp.mean(gg * xr, axis=-1, keepdims=True)), grad * xr


def split_dot(x, table):
    hi = x.astype(BF)
    lo = (x - hi.astype(F32)).astype(BF)
    return dot_nn(hi, table) + dot_nn(lo, table)


PAIRS = [(p, s) for p in range(3) for s in range(p + 1)]


def weight_copies(ids, k, bufs, dst, sem, first):
    half, n = dst.shape[2] // 2, dst.shape[1] // 4
    copies = []
    for i, (h, buf, row, place, hop) in enumerate(buffer_rows(k)):
        at = pl.multiple_of((ids[1] ^ hop) * n + (ids[0] ^ place) * k, k)
        copies.append(
            pltpu.make_async_copy(
                bufs[buf].at[:, pl.ds(row, k)],
                dst.at[:, pl.ds(at, k), pl.ds(h * half, half)],
                sem.at[first + i],
            )
        )
    return copies


COPIES = 48


def attn_weight_copies(ids, own_qkv, own_out, bufs, w, sem):
    n = own_out.shape[0]
    own = pl.ds(pl.multiple_of(ids[1] * n, n), n)
    copies = [
        pltpu.make_async_copy(own_qkv, w.at[pl.ds(0, 3), own], sem.at[0]),
        pltpu.make_async_copy(own_out, w.at[3, own], sem.at[1]),
    ]
    return copies + weight_copies(ids, n // INNER, bufs, w, sem, 2)


def place_pick(p, frames):
    col = lax.broadcasted_iota(jnp.int32, (frames, 3 * frames), 1)
    row = lax.broadcasted_iota(jnp.int32, (frames, 3 * frames), 0)
    return (col == 3 * row + p).astype(BF)


def place_put(p, frames):
    row = lax.broadcasted_iota(jnp.int32, (3 * frames, frames), 0)
    col = lax.broadcasted_iota(jnp.int32, (3 * frames, frames), 1)
    return (row == 3 * col + p).astype(BF)


def frame_out_copies(ids, own, bufs, w, sem):
    n, d = own.shape
    k, half = n // INNER, d // 2
    copies = [pltpu.make_async_copy(own, w.at[0], sem.at[0])]
    for h, buf, row, place, hop in buffer_rows(k):
        at = pl.multiple_of((ids[0] ^ place) * k, k)
        copies.append(
            pltpu.make_async_copy(
                bufs[buf].at[0, pl.ds(row, k)],
                w.at[hop, pl.ds(at, k), pl.ds(h * half, half)],
                sem.at[len(copies)],
            )
        )
    return copies


FRAME_OUT_COPIES = 1 + 48


def frame_out_kernel(ids, m0, m1, m2, m3, frames, gain, own, *rest):
    bufs, (mid_o, nb_o, w, sem) = rest[:8], rest[8:]
    copies = frame_out_copies(ids, own, bufs, w, sem)
    for c in copies:
        c.start()
    for c in copies:
        c.wait()
    mid = frames[...].astype(F32)
    for r, m in enumerate((m0, m1, m2, m3)):
        mid = mid + dot_nn(m[...], w[r])
    mid_o[...] = mid
    nb_o[...] = (mid * rsq(mid) * gain[...]).astype(BF)


def frame_mid_kernel(ids, gnb, mid, grad_out, gain, own, *rest):
    bufs, (gm_o, low_o, dg_o, gx_o, w, sem) = rest[:8], rest[8:]
    copies = frame_out_copies(ids, own, bufs, w, sem)
    for c in copies:
        c.start()
    dx, dg = norm_back(gnb[...], mid[...], gain[...])
    grad = grad_out[...] + dx
    gm_o[...] = grad
    low_o[...] = grad.astype(BF)
    dg_o[...] = jnp.sum(dg, axis=0, keepdims=True)
    for c in copies:
        c.wait()
    for r in range(4):
        gx_o[r] = dot_nt(low_o[...], w[r]).astype(BF)


def token_attn_kernel(ids, fo, emb, cot, valid, ga, gb, table, own_qkv, own_out, *rest):
    bufs, (s_o, g_o, na_o, q_o, k_o, v_o, mix_o, mid_o, nb_o, pr_o, w, sem) = rest[:8], rest[8:]
    copies = attn_weight_copies(ids, own_qkv, own_out, bufs, w, sem)
    for c in copies:
        c.start()
    frames = fo.shape[0]
    places = [pl.ds(p * frames, frames) for p in range(3)]
    for p in range(3):
        pick = place_pick(p, frames)
        g = dot_nn(pick, cot[...])
        g_o[places[p]] = jnp.where(valid[...] > 0.0, g, 0.0).astype(BF)
        s = fo[...] + dot_nn(pick, emb[...])
        s_o[places[p]] = s
        na_o[places[p]] = (s * rsq(s) * ga[...]).astype(BF)
    for c in copies:
        c.wait()
    for t, out in enumerate((q_o, k_o, v_o)):
        out[...] = dot_nt(na_o[...], w[t]).astype(BF)
    scale = 1.0 / math.sqrt(HD)
    for p in range(3):
        scores = [
            split_dot(q_o[places[p]].astype(F32) * k_o[places[s]].astype(F32), table[...]) * scale
            for s in range(p + 1)
        ]
        top = scores[0]
        for x in scores[1:]:
            top = jnp.maximum(top, x)
        ex = [jnp.exp(x - top) for x in scores]
        total = ex[0]
        for x in ex[1:]:
            total = total + x
        mixed = None
        for s in range(p + 1):
            prob = ex[s] / total
            pr_o[PAIRS.index((p, s))] = prob
            term = dot_nt(prob.astype(BF), table[...]) * v_o[places[s]].astype(F32)
            mixed = term if mixed is None else mixed + term
        mix_o[places[p]] = mixed.astype(BF)
    for p in places:
        mid = s_o[p] + dot_nn(mix_o[p], w[3])
        mid_o[p] = mid
        nb_o[p] = (mid * rsq(mid) * gb[...]).astype(BF)


def token_back_kernel(ids, g, gnb, mid, s_in, ga, gb, q, k, v, mix, pr, table, own_qkv, own_out, *rest):
    bufs, (ml_o, left_o, gf_o, da_o, db_o, w, gm, gx, sem) = rest[:8], rest[8:]
    copies = attn_weight_copies(ids, own_qkv, own_out, bufs, w, sem)
    for c in copies:
        c.start()
    frames, feats = gf_o.shape[0], q.shape[1]
    places = [pl.ds(p * frames, frames) for p in range(3)]
    lanes = [pl.ds(t * feats, feats) for t in range(4)]
    total = None
    for p in places:
        dx, dg = norm_back(gnb[p], mid[p], gb[...])
        grad = g[p].astype(F32) + dx
        gm[p] = grad
        ml_o[p] = grad.astype(BF)
        row = jnp.sum(dg, axis=0, keepdims=True)
        total = row if total is None else total + row
    db_o[...] = total
    left_o[:, lanes[3]] = mix[...]
    for c in copies:
        c.wait()
    gx[...] = dot_nt(ml_o[...], w[3]).astype(BF)
    scale = 1.0 / math.sqrt(HD)
    kg, vg = {}, {}
    for p in range(3):
        gp = [
            split_dot(gx[places[p]].astype(F32) * v[places[s]].astype(F32), table[...])
            for s in range(p + 1)
        ]
        probs = [pr[PAIRS.index((p, s))] for s in range(p + 1)]
        delta = probs[0] * gp[0]
        for s in range(1, p + 1):
            delta = delta + probs[s] * gp[s]
        query = None
        for s in range(p + 1):
            wide = dot_nt((probs[s] * (gp[s] - delta)).astype(BF), table[...])
            term = wide * k[places[s]].astype(F32)
            query = term if query is None else query + term
            key = wide * q[places[p]].astype(F32) * scale
            value = dot_nt(probs[s].astype(BF), table[...]) * gx[places[p]].astype(F32)
            if p == s:
                kg[s], vg[s] = key, value
            else:
                kg[s], vg[s] = kg[s] + key, vg[s] + value
        left_o[places[p], lanes[0]] = (query * scale).astype(BF)
    for s in range(3):
        left_o[places[s], lanes[1]] = kg[s].astype(BF)
        left_o[places[s], lanes[2]] = vg[s].astype(BF)
    gna = dot_nn(left_o[:, lanes[0]], w[0]) + dot_nn(left_o[:, lanes[1]], w[1]) + dot_nn(left_o[:, lanes[2]], w[2])
    total = out = None
    for i, p in enumerate(places):
        dx, dg = norm_back(gna[i * frames : (i + 1) * frames], s_in[p], ga[...])
        grad = gm[p] + dx
        row = jnp.sum(dg, axis=0, keepdims=True)
        total = row if total is None else total + row
        out = grad if out is None else out + grad
    da_o[...] = total
    gf_o[...] = out


GELU_S = math.sqrt(2.0 / math.pi)


def gelu_both(u):
    u2 = u * u
    t = jnp.tanh(GELU_S * (u + 0.044715 * (u2 * u)))
    h = 0.5 * (1.0 + t)
    return u * h, h + 0.5 * u * (1.0 - t * t) * (GELU_S * (1.0 + 3.0 * 0.044715 * u2))


def token_ff_kernel(step, ids, nb, g, mid, valid, bias, bdown, own_up, own_down, *rest):
    bufs, (out_o, gnb_o, left_o, gb_o, wuo, wdo, w, acc, sem) = rest[:8], rest[8:]
    n, frames = own_down.shape[0], valid.shape[0]
    own = [
        pltpu.make_async_copy(own_up, wuo, sem.at[0]),
        pltpu.make_async_copy(own_down, wdo, sem.at[1]),
    ]
    copies = weight_copies(ids, n // INNER, bufs, w, sem, 2)
    z = ids[1]
    for c in own + copies:
        c.start()
    acc[...] = jnp.zeros_like(acc)
    gnb_o[...] = jnp.zeros_like(gnb_o)

    def middle(at, size, pre, back):
        cols = pl.ds(at, size)
        h, dh = gelu_both(pre + bias[:, cols])
        h = h.astype(BF)
        gp = (dh * back).astype(BF)
        left_o[:, cols] = h
        left_o[:, pl.ds(pl.multiple_of(4 * n + at, 128), size)] = gp
        gb_o[:, cols] = jnp.sum(gp.astype(F32), axis=0, keepdims=True)
        return h, gp

    for c in own:
        c.wait()
    own_step = n // 2

    def own_block(j, carry):
        cols = pl.ds(pl.multiple_of(j * own_step, own_step), own_step)
        pre = dot_nn(nb[...], wuo[:, cols])
        back = dot_nt(g[...], wdo[cols, :])
        h, gp = middle(pl.multiple_of(z * n + j * own_step, own_step), own_step, pre, back)
        acc[...] += dot_nn(h, wdo[cols, :])
        gnb_o[...] += dot_nt(gp, wuo[:, cols])
        return carry

    lax.fori_loop(0, n // own_step, own_block, 0)
    for c in copies:
        c.wait()

    def block(j, carry):
        at = pl.multiple_of(j * step + jnp.where(j * step >= z * n, n, 0), step)
        rows = pl.ds(at, step)
        pre = dot_nt(nb[...], w[0, rows, :])
        back = dot_nt(g[...], w[1, rows, :])
        h, gp = middle(at, step, pre, back)
        acc[...] += dot_nn(h, w[1, rows, :])
        gnb_o[...] += dot_nn(gp, w[0, rows, :])
        return carry

    lax.fori_loop(0, 3 * n // step, block, 0)
    out = None
    for p in range(3):
        rows = pl.ds(p * frames, frames)
        val = jnp.where(valid[...] > 0.0, acc[rows] + mid[rows] + bdown[...], 0.0).astype(BF)
        term = dot_nn(place_put(p, frames), val)
        out = term if out is None else out + term
    out_o[...] = out.astype(BF)


def lay_right(dst, row, col, right, core, block):
    for i in range(INNER // 2):
        at = pl.multiple_of((2 * i + core) * block, block)
        dst[pl.ds(row + i * block, block), pl.ds(col, right.shape[1])] = right[pl.ds(at, block), :]


def pair_grad_kernel(new, ids, lm, lt, rm, rt, out, tmp, am):
    @pl.when(new(pl.program_id(0)))
    def _():
        for i, src in enumerate((rm, rt)):
            tmp[...] = jnp.transpose(src[0])
            lay_right(am, 0, i * src.shape[1], tmp, ids[0] & 1, src.shape[2] // INNER)

    out[...] = dot_nn(am[...], jnp.concatenate([lm[...], lt[...]], axis=0)).astype(BF)


def frame_grad_kernel(second, ids, left, right0, right1, same, cross, tmp, am):
    d = right0.shape[1]
    for first, right in ((0, right0), (second, right1)):

        @pl.when(pl.program_id(0) == first)
        def _(right=right):
            tmp[...] = jnp.transpose(right[...])
            for i in range(2):
                lay_right(am, i * (d // 2), 0, tmp, (ids[0] & 1) ^ i, d // INNER)

    total = dot_nn(am[...], left[...])
    same[...] = total[: d // 2].astype(BF)
    cross[...] = total[d // 2 :].astype(BF)


VMEM_LIMIT = 60 * 1024 * 1024


def arr(shape, dtype):
    return jax.ShapeDtypeStruct(shape, dtype)


def cost(flops, ins, outs):
    size = sum(a.size * a.dtype.itemsize for a in ins) + sum(
        math.prod(o.shape) * o.dtype.itemsize for o in outs
    )
    return pl.CostEstimate(flops=flops, bytes_accessed=size, transcendentals=0)


def call(kernel, outs, ins, scratch, any_from, flops, smem=0):
    def space(i):
        return pltpu.SMEM if i < smem else pltpu.VMEM if i < any_from else pl.ANY

    return pl.pallas_call(
        kernel,
        out_shape=outs,
        in_specs=[pl.BlockSpec(memory_space=space(i)) for i in range(len(ins))],
        out_specs=[pl.BlockSpec(memory_space=pltpu.VMEM)] * len(outs),
        scratch_shapes=scratch,
        compiler_params=pltpu.CompilerParams(vmem_limit_bytes=VMEM_LIMIT),
        cost_estimate=cost(flops, ins, outs),
    )(*ins)


def frame_out(ids, mixed, frames, gain, own, bufs):
    rows, d = frames.shape
    ins = [ids, *mixed, frames, gain, own, *bufs]
    scratch = [pltpu.VMEM((4, *own.shape), BF), pltpu.SemaphoreType.DMA((FRAME_OUT_COPIES,))]
    outs = [arr((rows, d), F32), arr((rows, d), BF)]
    return call(frame_out_kernel, outs, ins, scratch, 7, 8 * rows * own.size, smem=1)


def frame_mid(ids, gnb, mid, grad_out, gain, own, bufs):
    rows, d = mid.shape
    ins = [ids, gnb, mid, grad_out, gain, own, *bufs]
    scratch = [pltpu.VMEM((4, *own.shape), BF), pltpu.SemaphoreType.DMA((FRAME_OUT_COPIES,))]
    outs = [arr((rows, d), F32), arr((rows, d), BF), arr((1, d), F32), arr((4, rows, own.shape[0]), BF)]
    return call(frame_mid_kernel, outs, ins, scratch, 5, 8 * rows * own.size, smem=1)


def token_attn(ids, fo, emb, cot, valid, ga, gb, table, own_qkv, own_out, bufs):
    frames, d = fo.shape
    rows, feats = 3 * frames, table.shape[0]
    outs = (
        [arr((rows, d), F32), arr((rows, d), BF), arr((rows, d), BF)]
        + [arr((rows, feats), BF)] * 4
        + [arr((rows, d), F32), arr((rows, d), BF), arr((len(PAIRS), frames, table.shape[1]), F32)]
    )
    return call(
        token_attn_kernel,
        outs,
        [ids, fo, emb, cot, valid, ga, gb, table, own_qkv, own_out, *bufs],
        [pltpu.VMEM((4, feats, d), BF), pltpu.SemaphoreType.DMA((2 + COPIES,))],
        8,
        8 * rows * feats * d,
        smem=1,
    )


def token_back(ids, g, gnb, mid, s, ga, gb, q, k, v, mix, pr, table, own_qkv, own_out, bufs):
    rows, d = s.shape
    frames, feats = rows // 3, table.shape[0]
    outs = [
        arr((rows, d), BF),
        arr((rows, 4 * feats), BF),
        arr((frames, d), F32),
        arr((1, d), F32),
        arr((1, d), F32),
    ]
    return call(
        token_back_kernel,
        outs,
        [ids, g, gnb, mid, s, ga, gb, q, k, v, mix, pr, table, own_qkv, own_out, *bufs],
        [
            pltpu.VMEM((4, feats, d), BF),
            pltpu.VMEM((rows, d), F32),
            pltpu.VMEM((rows, feats), BF),
            pltpu.SemaphoreType.DMA((2 + COPIES,)),
        ],
        13,
        8 * rows * feats * d,
        smem=1,
    )


def token_ff(ids, nb, g, mid, valid, bias, bdown, own_up, own_down, bufs):
    rows, d = nb.shape
    n = own_down.shape[0]
    outs = [
        arr((rows, d), BF),
        arr((rows, d), F32),
        arr((rows, 8 * n), BF),
        arr((1, 4 * n), F32),
    ]
    return call(
        functools.partial(token_ff_kernel, 512),
        outs,
        [ids, nb, g, mid, valid, bias, bdown, own_up, own_down, *bufs],
        [
            pltpu.VMEM((d, n), BF),
            pltpu.VMEM((n, d), BF),
            pltpu.VMEM((2, 4 * n, d), BF),
            pltpu.VMEM((rows, d), F32),
            pltpu.SemaphoreType.DMA((2 + COPIES,)),
        ],
        7,
        32 * rows * n * d,
        smem=1,
    )


def smem_spec():
    return pl.BlockSpec(memory_space=pltpu.SMEM)


def pair_grad(ids, left, left_other, rights, rights_other, split):
    rows, units = left.shape
    d = rights.shape[2]
    step = d
    at = split // step
    pick = lambda j: jnp.where(j < at, 0, 1)
    outs = [arr((d // 2, units), BF)]
    [out] = pl.pallas_call(
        functools.partial(pair_grad_kernel, lambda j: (j == 0) | (j == at)),
        grid=(units // step,),
        in_specs=[smem_spec()]
        + [pl.BlockSpec((rows, step), lambda j: (0, j))] * 2
        + [pl.BlockSpec((1, rows, d), lambda j: (pick(j), 0, 0))] * 2,
        out_specs=[pl.BlockSpec((d // 2, step), lambda j: (0, j))],
        out_shape=outs,
        scratch_shapes=[pltpu.VMEM((d, rows), BF), pltpu.VMEM((d // 2, 2 * rows), BF)],
        compiler_params=pltpu.CompilerParams(vmem_limit_bytes=VMEM_LIMIT),
        cost_estimate=cost(2 * rows * units * d, [left, left_other, rights, rights_other], outs),
    )(ids, left, left_other, rights, rights_other)
    return out


def frame_grad(ids, left, rights, split):
    rows, units = left.shape
    d = rights[0].shape[1]
    step = units // 4
    outs = [arr((d // 2, units), BF)] * 2
    ins = [left, *rights]
    return pl.pallas_call(
        functools.partial(frame_grad_kernel, split // step),
        grid=(4,),
        in_specs=[smem_spec(), pl.BlockSpec((rows, step), lambda j: (0, j))]
        + [pl.BlockSpec((rows, d), lambda j: (0, 0))] * 2,
        out_specs=[pl.BlockSpec((d // 2, step), lambda j: (0, j))] * 2,
        out_shape=outs,
        scratch_shapes=[pltpu.VMEM((d, rows), BF)] * 2,
        compiler_params=pltpu.CompilerParams(vmem_limit_bytes=VMEM_LIMIT),
        cost_estimate=cost(2 * rows * units * d, ins, outs),
    )(ids, *ins)


def segments(lengths, whole_rows):
    count = lengths.shape[1]
    order = jnp.arange(count, dtype=jnp.int32)
    item_ends = jnp.sum(
        jnp.where(order[None, :] <= order[:, None], lengths[0][None, :], 0), axis=1, dtype=jnp.int32
    )
    positions = jnp.arange(whole_rows, dtype=jnp.int32)
    segment = jnp.sum(
        (positions[:, None] >= item_ends[None, :]).astype(jnp.int32), axis=1, dtype=jnp.int32
    )
    is_valid = positions < jnp.sum(lengths[0], dtype=jnp.int32)
    segment = jnp.where(is_valid, segment, positions + count)
    return (segment, is_valid)


def frame_allowed(segment):
    positions = jnp.arange(segment.shape[0], dtype=jnp.int32)
    return (positions[None, :] <= positions[:, None]) & (segment[None, :] == segment[:, None])


def split_heads(rows):
    return rows.reshape(rows.shape[0], rows.shape[1] // HD, HD)


def frame_forward(qkv_rows, segment):
    queries, key_rows, value_rows = (split_heads(qkv_rows[t]) for t in range(3))
    raw_scores = jnp.einsum("qhe,khe->hqk", queries, key_rows, preferred_element_type=F32) * (
        1.0 / math.sqrt(HD)
    )
    scores = jnp.where(frame_allowed(segment)[None], raw_scores, -1e30)
    top_score = jnp.max(scores, axis=-1, keepdims=True)
    exp_scores = jnp.exp(scores - top_score)
    exp_total = jnp.sum(exp_scores, axis=-1, keepdims=True)
    attn_probs = (exp_scores / exp_total).astype(BF)
    mixed = jnp.einsum("hqk,khe->qhe", attn_probs, value_rows, preferred_element_type=F32)
    log_total = top_score[:, :, 0] + jnp.log(exp_total[:, :, 0])
    return (mixed.astype(BF).reshape(qkv_rows.shape[1], -1), log_total)


def frame_backward(qkv_rows, log_total, grad_mixed, segment):
    queries, key_rows, value_rows = (split_heads(qkv_rows[t]) for t in range(3))
    grad_heads = split_heads(grad_mixed)
    scale = 1.0 / math.sqrt(HD)
    raw_scores = jnp.einsum("qhe,khe->hqk", queries, key_rows, preferred_element_type=F32) * scale
    scores = jnp.where(frame_allowed(segment)[None], raw_scores, -1e30)
    attn_probs = jnp.exp(scores - log_total[:, :, None])
    value_grad = jnp.einsum(
        "hqk,qhe->khe", attn_probs.astype(BF), grad_heads, preferred_element_type=F32
    )
    grad_probs = jnp.einsum("qhe,khe->hqk", grad_heads, value_rows, preferred_element_type=F32)
    row_delta = jnp.sum(attn_probs * grad_probs, axis=-1, keepdims=True)
    grad_scores = (attn_probs * (grad_probs - row_delta)).astype(BF)
    query_grad = jnp.einsum("hqk,khe->qhe", grad_scores, key_rows, preferred_element_type=F32) * scale
    key_grad = jnp.einsum("hqk,qhe->khe", grad_scores, queries, preferred_element_type=F32) * scale
    rows = qkv_rows.shape[1]
    return [g.reshape(rows, -1).astype(BF) for g in (query_grad, key_grad, value_grad)]


def head_table(features):
    at = jnp.arange(features, dtype=jnp.int32)
    return ((at // HD)[:, None] == jnp.arange(128, dtype=jnp.int32)[None, :]).astype(BF)


def shards(frames, codes_embed, lengths, cotangent, *params):
    gain_a, w_qkv, w_out, gain_b, w_up, b_up, w_down, b_down = params[:8]
    t_gain_a, t_qkv, t_out, t_gain_b, t_up, t_bup, t_down, t_bdown = params[8:]
    dp, parts = lax.axis_size("dp"), lax.axis_size("mp")
    z = lax.axis_index("mp")
    ids = jnp.stack([my_place(), z]).astype(jnp.int32)
    local, d = frames.shape
    n_attn, n_ff = w_out.shape[0], w_down.shape[0]
    block = d // INNER
    segment, is_valid = segments(lengths, local * parts)
    valid = lax.dynamic_slice_in_dim(is_valid, z * local, local, 0).astype(F32)[:, None]

    stream = frames.astype(F32)
    gain_a32, gain_b32 = gain_a.astype(F32), gain_b.astype(F32)
    normed_a = normalize(stream, gain_a32).astype(BF)
    gathered_a = gather_rows(normed_a)

    attn_w = Gather(jnp.concatenate([own_cols(t_qkv), own_rows(t_out)[None]], axis=0))
    ff_w = Gather(jnp.stack([own_cols(t_up), own_rows(t_down)]))
    out_w = Gather(own_rows(w_out)[None])
    out_w.shards()
    out_w.plane_first()
    out_w.plane_last()
    out_w.cores()
    attn_w.shards()
    gathered_a = after(gathered_a, *out_w.held, *attn_w.held)

    qkv_rows = jnp.einsum("rd,tde->tre", gathered_a, w_qkv, preferred_element_type=F32).astype(BF)
    mixed_rows, log_total = frame_forward(qkv_rows, segment)
    by_rows = [
        lax.dynamic_slice_in_dim(mixed_rows, (z ^ r) * local, local, 0) for r in range(parts)
    ]
    mixed_own = [by_rows[0]] + [swap_mp(by_rows[r], r) for r in range(1, parts)]

    attn_w.plane_first(mixed_rows)
    middle, normed_b = frame_out(ids, mixed_own, frames, gain_b32[None], w_out, out_w.held)
    ff_w.shards(normed_b)
    gathered_b = gather_rows(normed_b)

    attn_w.plane_last(normed_b)
    ff_w.plane_first(normed_b)
    gathered_b = after(gathered_b, *attn_w.marks(), *ff_w.marks())

    hidden_pre = dot_nn(gathered_b, w_up) + b_up.astype(F32)
    hidden = activate(hidden_pre).astype(BF)
    part_b = dot_nn(hidden, w_down).astype(BF)
    branch_b = scatter_rows(part_b)

    attn_w.cores(part_b)
    ff_w.plane_last(part_b)
    f_result = middle + after(branch_b, *attn_w.held, *ff_w.marks()) + b_down.astype(F32)

    t_bias = jnp.concatenate(gather_all(t_bup)).astype(F32)[None]
    own_qkv = jnp.transpose(t_qkv, (0, 2, 1))
    table = head_table(n_attn * parts)
    tga, tgb = t_gain_a.astype(F32)[None], t_gain_b.astype(F32)[None]

    attn_bufs = attn_w.held
    t_stream, g_low, t_na, q, k, v, mixed, t_middle, t_nb, probs = token_attn(
        ids, f_result, codes_embed, cotangent, valid, tga, tgb, table, own_qkv, t_out, attn_bufs
    )
    ff_w.cores()
    output, t_gnb, t_left, t_gbup = token_ff(
        ids, t_nb, g_low, t_middle, valid, t_bias, t_bdown.astype(F32)[None], t_up, t_down, ff_w.held
    )
    rights = jnp.stack([d_order(g_low), d_order(t_nb)])
    rights_other = swap_dp(rights, 1)
    left_other = swap_dp(t_left, 1)
    m_low, a_left, grad_frame, t_da, t_db = token_back(
        ids, g_low, t_gnb, t_middle, t_stream, tga, tgb, q, k, v, mixed, probs, table, own_qkv, t_out, attn_bufs
    )
    t_dbd = jnp.sum(g_low.astype(F32), axis=0)

    ff_grad = pair_grad(ids, after(t_left, grad_frame), left_other, rights, rights_other, 4 * n_ff)
    ff_sum = scatter_plane(ff_grad)
    grad_low = grad_frame.astype(BF)
    gathered_down = gather_rows_p(grad_low)
    a_rights = jnp.stack([d_order(t_na), d_order(m_low)])
    a_rights_other = swap_dp(a_rights, 1)
    a_other = swap_dp(a_left, 1)
    gathered_down = after(gathered_down, ff_grad)
    grad_hidden = dot_nt(gathered_down, w_down)
    grad_pre = jax.vjp(activate, hidden_pre)[1](grad_hidden)[0].astype(BF)
    part_c = dot_nt(grad_pre, w_up).astype(BF)
    grad_nb = shards_total(*scatter_rows_p(part_c))

    attn_grad = pair_grad(ids, after(a_left, part_c), a_other, a_rights, a_rights_other, 3 * n_attn * parts)
    f_left = jnp.concatenate([hidden, grad_pre], axis=1)
    ff_same, ff_cross = frame_grad(
        ids, after(f_left, part_c), [d_order(gathered_down), d_order(gathered_b)], n_ff
    )
    ff_cross = swap_dp(ff_cross, 1)
    grad_nb = after(grad_nb, attn_grad, ff_same)
    grad_middle, mid_low, f_db, pieces = frame_mid(
        ids, grad_nb, middle, grad_frame, gain_b32[None], w_out, out_w.held
    )
    gathered_mid = gather_rows_p(mid_low)
    grad_mixed = jnp.concatenate(
        by_xor_mp([pieces[0]] + [swap_mp(pieces[r], r) for r in range(1, parts)]), axis=0
    )
    grad_qkv = jnp.concatenate(frame_backward(qkv_rows, log_total, grad_mixed, segment), axis=1)
    w_all = jnp.concatenate([w_qkv[0], w_qkv[1], w_qkv[2]], axis=1)
    part_d32 = dot_nt(grad_qkv, w_all)
    part_d = after(part_d32.astype(BF), ff_sum, gathered_mid)
    attn_sum = scatter_plane(after(attn_grad, grad_mixed))
    attn_same, attn_cross = frame_grad(
        ids,
        jnp.concatenate([grad_qkv, mixed_rows], axis=1),
        [d_order(gathered_a), d_order(gathered_mid)],
        3 * n_attn,
    )
    attn_cross = swap_dp(attn_cross, 1)
    part_d = after(part_d, attn_same)
    f_ff_value = (ff_same.astype(F32) + ff_cross.astype(F32)).astype(BF)
    f_attn_value = (attn_same.astype(F32) + attn_cross.astype(F32)).astype(BF)
    na_parts = scatter_rows_p(part_d)
    ff_z = scatter_shards(ff_sum, n_ff, part_d)
    f_ff_parts = plane_parts(f_ff_value, part_d)
    f_attn_parts = plane_parts(f_attn_value, part_d)
    grad_na = shards_total(*na_parts)
    first = jax.vjp(normalize, stream, gain_a32)[1](grad_na)
    frames_grad = grad_middle + first[0]
    attn_z = scatter_shards(after(attn_sum, grad_na), n_attn)
    f_da = jnp.sum(part_d32 * gathered_a.astype(F32), axis=0) / gain_a32

    wide = lax.dynamic_update_slice_in_dim(
        jnp.zeros((parts, n_ff), F32), jnp.sum(grad_pre.astype(F32), axis=0)[None], z, 0
    )

    def by_owner(full):
        return jnp.transpose(full.reshape(dp, parts, -1), (1, 0, 2)).reshape(parts, -1)

    vec = jnp.concatenate(
        [
            jnp.stack([f_da, f_db[0], jnp.sum(grad_frame, axis=0), t_da[0], t_db[0], t_dbd]),
            by_owner(wide),
            by_owner(t_gbup[0]),
        ],
        axis=0,
    )
    vec = d_order(after(vec, part_d))
    vec = jnp.concatenate(by_xor([vec[:, i * block : (i + 1) * block] for i in range(INNER)]), axis=1)
    for bit in (4, 2, 1):
        half = vec.shape[1] // 2
        vec = vec[:, :half] + swap_dp(vec[:, half:], bit)
    vec = outer_sum(vec, 1)
    width = vec.shape[1]
    quarter = width // parts
    rows = by_xor_mp(
        [
            jnp.concatenate(
                [vec[:6, i * quarter : (i + 1) * quarter].reshape(-1), vec[6 + i], vec[6 + parts + i]]
            )
            for i in range(parts)
        ]
    )
    mine = rows[0] + sum(swap_mp(rows[r], r) for r in (1, 2, 3))
    vectors = [mine[i * quarter : (i + 1) * quarter] for i in range(6)]
    f_bup, t_bup_grad = mine[6 * quarter : 6 * quarter + width], mine[6 * quarter + width :]

    f_ff = shards_total(*f_ff_parts, mine)
    f_attn = shards_total(*f_attn_parts, mine)
    t_attn = shards_total(*attn_z, f_ff, f_attn)
    t_ff = shards_total(*ff_z, t_attn)

    def ff_split(total):
        return total[:, :n_ff].T, total[:, n_ff:]

    def attn_split(total):
        rows = total.reshape(block, 4, n_attn)
        return jnp.transpose(rows[:, :3], (1, 0, 2)), total[:, 3 * n_attn :].T

    t_down_grad, t_up_grad = ff_split(t_ff)
    f_down_grad, f_up_grad = ff_split(f_ff)
    f_qkv_grad, f_out_grad = attn_split(f_attn)
    t_qkv_grad, t_out_grad = attn_split(t_attn)

    def owned(qkv_grad, out_grad, up_grad, down_grad):
        return (
            outer_sum(qkv_grad, 1),
            outer_sum(out_grad, 1),
            outer_sum(up_grad, 0),
            outer_sum(down_grad, 1),
        )

    f = owned(f_qkv_grad, f_out_grad, f_up_grad, f_down_grad)
    t = owned(t_qkv_grad, t_out_grad, t_up_grad, t_down_grad)
    return (
        output,
        frames_grad,
        vectors[0],
        f[0],
        f[1],
        vectors[1],
        f[2],
        f_bup,
        f[3],
        vectors[2],
        vectors[3],
        t[0],
        t[1],
        vectors[4],
        t[2],
        t_bup_grad,
        t[3],
        vectors[5],
    )


def solution(mesh):
    rows = P(("dp", "mp"), None)
    block = (
        P(),
        P(None, None, "mp"),
        P("mp", None),
        P(),
        P(None, "mp"),
        P("mp"),
        P("mp", None),
        P(),
    )
    vec = P(("dp", "mp"))
    block_out = (
        vec,
        P(None, "dp", "mp"),
        P("mp", "dp"),
        vec,
        P("dp", "mp"),
        vec,
        P("mp", "dp"),
        vec,
    )
    return jax.shard_map(
        shards,
        mesh=mesh,
        in_specs=(rows, rows, P("dp", None), rows) + block + block,
        out_specs=(rows, rows) + block_out + block_out,
        check_vma=False,
    )
```

```python
import functools
import math

import jax
import jax.numpy as jnp
from jax import lax
from jax.experimental import pallas as pl
from jax.experimental.pallas import tpu as pltpu
from jax.sharding import PartitionSpec as P

HD = 64
eps = 1e-05
BF = jnp.bfloat16
F32 = jnp.float32


def normalize(stream, gain_vec):
    return stream * lax.rsqrt(jnp.mean(stream * stream, axis=-1, keepdims=True) + eps) * gain_vec


def activate(values):
    return jax.nn.gelu(values, approximate=True)


def dot_nt(a, b):
    return lax.dot_general(a, b, (((1,), (1,)), ((), ())), preferred_element_type=F32)


def dot_nn(a, b):
    return lax.dot_general(a, b, (((1,), (0,)), ((), ())), preferred_element_type=F32)


def dot_tn(a, b):
    return lax.dot_general(a, b, (((0,), (0,)), ((), ())), preferred_element_type=F32)


def gather_rows(rows):
    return lax.all_gather(rows, "mp", axis=0, tiled=True)


def scatter_rows(partial):
    return lax.psum_scatter(
        partial.astype(BF), "mp", scatter_dimension=0, tiled=True
    ).astype(F32)


INNER = 8


def swap_dp(value, bit):
    size = lax.axis_size("dp")
    return lax.ppermute(value, "dp", [(i, i ^ bit) for i in range(size)])


def swap_mp(value, mask):
    size = lax.axis_size("mp")
    return lax.ppermute(value, "mp", [(i, i ^ mask) for i in range(size)])


def my_place():
    return lax.axis_index("dp") % INNER


BITS = [2, 4]
SIDES = [BITS, BITS[::-1]]


def after(value, *marks):
    return lax.optimization_barrier((value,) + tuple(marks))[0]


def all_after(values, *marks):
    return lax.optimization_barrier(tuple(values) + tuple(marks))[: len(values)]


class Gather:
    def __init__(self, piece):
        self.k = piece.shape[1]
        self.piece = piece

    def shards(self, *marks, then=()):
        piece = after(self.piece, *marks) if marks else self.piece
        near = swap_mp(piece, 1)
        far = swap_mp(piece, 2)
        inner = lax.ppermute(piece, "mp", [(1, 2), (2, 1)])
        outer = lax.ppermute(after(far, *then), "mp", [(2, 3), (1, 0)])
        self.held = (near, far, inner, outer)

    def shards_straight(self):
        self.held = tuple(swap_mp(self.piece, r) for r in (1, 2, 3))

    def plane_first(self, *marks):
        near, far, *hops = all_after(self.held, *marks)
        z = lax.axis_index("mp")
        last = hops[0] if len(hops) == 1 else jnp.where((z == 1) | (z == 2), *hops)
        half = near.shape[2] // 2
        self.held = []
        for h, side in enumerate(SIDES):
            lanes = slice(h * half, (h + 1) * half)
            whole = jnp.concatenate([near[..., lanes], far[..., lanes], last[..., lanes]], axis=1)
            self.held.append((whole, swap_dp(whole, side[0])))

    def marks(self):
        return [got for _, got in self.held]

    def plane_last(self, *marks):
        held = []
        for (whole, got), side in zip(self.held, SIDES):
            whole, got = all_after((whole, got), *marks)
            low = jnp.concatenate([whole, got], axis=1)
            held.append((low, swap_dp(low, side[1])))
        self.held = held

    def cores(self, *marks):
        held = []
        for low, high in self.held:
            low, high = all_after((low, high), *marks)
            held += [low, high, swap_dp(low, 1), swap_dp(high, 1)]
        self.held = held


def buffer_rows(k):
    out = []
    for h, side in enumerate(SIDES):
        first, last = side[0] // 2, side[1] // 2
        for core in range(2):
            for high in range(2):
                for i in range(2):
                    place = 2 * (i * first + high * last) + core
                    for r in range(3):
                        out.append((h, 4 * h + 2 * core + high, (3 * i + r) * k, place, r + 1))
    return out


def own_rows(shard_rows):
    k = shard_rows.shape[0] // INNER
    return lax.dynamic_slice_in_dim(shard_rows, my_place() * k, k, 0)


def own_cols(shard_cols):
    k = shard_cols.shape[-1] // INNER
    piece = lax.dynamic_slice_in_dim(shard_cols, my_place() * k, k, shard_cols.ndim - 1)
    return jnp.swapaxes(piece, -1, -2)


def by_xor(slots):
    me = my_place()
    for bit in [1] + BITS:
        on = (me & bit) != 0
        slots = [jnp.where(on, slots[i ^ bit], slots[i]) for i in range(len(slots))]
    return slots


def by_xor_mp(slots):
    z = lax.axis_index("mp")
    for bit in (1, 2):
        on = (z & bit) != 0
        slots = [jnp.where(on, slots[i ^ bit], slots[i]) for i in range(len(slots))]
    return slots


def gather_all(value):
    return by_xor_mp([value] + [swap_mp(value, r) for r in (1, 2, 3)])


def gather_rows_p(rows):
    return jnp.concatenate(gather_all(rows), axis=0)


def scatter_rows_p(partial):
    low = partial.astype(BF)
    local = low.shape[0] // 4
    z = lax.axis_index("mp")
    cut = lambda at: lax.dynamic_slice_in_dim(low, at * local, local, 0)
    return cut(z), [swap_mp(cut(z ^ r), r) for r in (1, 2, 3)]


def scatter_plane(value):
    size = lax.axis_size("dp")
    groups = [
        [o + 2 * i + c for i in range(4)] for o in range(0, size, INNER) for c in range(2)
    ]
    return lax.psum_scatter(value, "dp", scatter_dimension=0, axis_index_groups=groups, tiled=True)


def plane_parts(value, *marks):
    if marks:
        value = after(value, *marks)
    block = value.shape[0] // 4
    at = my_place() // 2
    cut = lambda i: lax.dynamic_slice_in_dim(value, i * block, block, 0)
    return cut(at), [swap_dp(cut(at ^ m), 2 * m) for m in (1, 2, 3)]


def scatter_shards(value, n, *marks):
    z = lax.axis_index("mp")
    if marks:
        value = after(value, *marks)
    count = value.shape[1] // (4 * n)

    def cut(at):
        return jnp.concatenate(
            [lax.dynamic_slice_in_dim(value, (4 * i + at) * n, n, 1) for i in range(count)], axis=1
        )

    return cut(z), [swap_mp(cut(z ^ r), r) for r in (1, 2, 3)]


def shards_total(own, sent, *marks):
    sent = all_after(sent, *marks)
    return own.astype(F32) + sent[0].astype(F32) + sent[1].astype(F32) + sent[2].astype(F32)


def d_order(rows):
    outer = lax.axis_size("dp") // INNER
    if outer == 1:
        return rows
    view = rows.reshape(rows.shape[0], outer, INNER, -1)
    return jnp.transpose(view, (0, 2, 1, 3)).reshape(rows.shape)


def outer_sum(value, axis):
    size = lax.axis_size("dp")
    if size == INNER:
        return value
    groups = [[o * INNER + i for o in range(size // INNER)] for i in range(INNER)]
    return lax.psum_scatter(
        value, "dp", scatter_dimension=axis, axis_index_groups=groups, tiled=True
    )


def rsq(x):
    return lax.rsqrt(jnp.mean(x * x, axis=-1, keepdims=True) + eps)


def norm_back(grad, x, gain):
    r = rsq(x)
    xr = x * r
    gg = grad * gain
    return r * (gg - xr * jnp.mean(gg * xr, axis=-1, keepdims=True)), grad * xr


def split_dot(x, table):
    hi = x.astype(BF)
    lo = (x - hi.astype(F32)).astype(BF)
    return dot_nn(hi, table) + dot_nn(lo, table)


PAIRS = [(p, s) for p in range(3) for s in range(p + 1)]


def weight_copies(ids, k, bufs, dst, sem, first):
    half, n = dst.shape[2] // 2, dst.shape[1] // 4
    copies = []
    for i, (h, buf, row, place, hop) in enumerate(buffer_rows(k)):
        at = pl.multiple_of((ids[1] ^ hop) * n + (ids[0] ^ place) * k, k)
        copies.append(
            pltpu.make_async_copy(
                bufs[buf].at[:, pl.ds(row, k)],
                dst.at[:, pl.ds(at, k), pl.ds(h * half, half)],
                sem.at[first + i],
            )
        )
    return copies


COPIES = 48


def attn_weight_copies(ids, own_qkv, own_out, bufs, w, sem):
    n = own_out.shape[0]
    own = pl.ds(pl.multiple_of(ids[1] * n, n), n)
    copies = [
        pltpu.make_async_copy(own_qkv, w.at[pl.ds(0, 3), own], sem.at[0]),
        pltpu.make_async_copy(own_out, w.at[3, own], sem.at[1]),
    ]
    return copies + weight_copies(ids, n // INNER, bufs, w, sem, 2)


def place_pick(p, frames):
    col = lax.broadcasted_iota(jnp.int32, (frames, 3 * frames), 1)
    row = lax.broadcasted_iota(jnp.int32, (frames, 3 * frames), 0)
    return (col == 3 * row + p).astype(BF)


def place_put(p, frames):
    row = lax.broadcasted_iota(jnp.int32, (3 * frames, frames), 0)
    col = lax.broadcasted_iota(jnp.int32, (3 * frames, frames), 1)
    return (row == 3 * col + p).astype(BF)


def frame_out_copies(ids, own, bufs, w, sem):
    n, d = own.shape
    k, half = n // INNER, d // 2
    copies = [pltpu.make_async_copy(own, w.at[0], sem.at[0])]
    for h, buf, row, place, hop in buffer_rows(k):
        at = pl.multiple_of((ids[0] ^ place) * k, k)
        copies.append(
            pltpu.make_async_copy(
                bufs[buf].at[0, pl.ds(row, k)],
                w.at[hop, pl.ds(at, k), pl.ds(h * half, half)],
                sem.at[len(copies)],
            )
        )
    return copies


FRAME_OUT_COPIES = 1 + 48


def frame_out_kernel(ids, m0, m1, m2, m3, frames, gain, own, *rest):
    bufs, (mid_o, nb_o, w, sem) = rest[:8], rest[8:]
    copies = frame_out_copies(ids, own, bufs, w, sem)
    for c in copies:
        c.start()
    for c in copies:
        c.wait()
    mid = frames[...].astype(F32)
    for r, m in enumerate((m0, m1, m2, m3)):
        mid = mid + dot_nn(m[...], w[r])
    mid_o[...] = mid
    nb_o[...] = (mid * rsq(mid) * gain[...]).astype(BF)


def frame_mid_kernel(ids, gnb, mid, grad_out, gain, own, *rest):
    bufs, (gm_o, low_o, dg_o, gx_o, w, sem) = rest[:8], rest[8:]
    copies = frame_out_copies(ids, own, bufs, w, sem)
    for c in copies:
        c.start()
    dx, dg = norm_back(gnb[...], mid[...], gain[...])
    grad = grad_out[...] + dx
    gm_o[...] = grad
    low_o[...] = grad.astype(BF)
    dg_o[...] = jnp.sum(dg, axis=0, keepdims=True)
    for c in copies:
        c.wait()
    for r in range(4):
        gx_o[r] = dot_nt(low_o[...], w[r]).astype(BF)


def token_attn_kernel(ids, fo, emb, cot, valid, ga, gb, table, own_qkv, own_out, *rest):
    bufs, (s_o, g_o, na_o, q_o, k_o, v_o, mix_o, mid_o, nb_o, pr_o, w, sem) = rest[:8], rest[8:]
    copies = attn_weight_copies(ids, own_qkv, own_out, bufs, w, sem)
    for c in copies:
        c.start()
    frames = fo.shape[0]
    places = [pl.ds(p * frames, frames) for p in range(3)]
    for p in range(3):
        pick = place_pick(p, frames)
        g = dot_nn(pick, cot[...])
        g_o[places[p]] = jnp.where(valid[...] > 0.0, g, 0.0).astype(BF)
        s = fo[...] + dot_nn(pick, emb[...])
        s_o[places[p]] = s
        na_o[places[p]] = (s * rsq(s) * ga[...]).astype(BF)
    for c in copies:
        c.wait()
    for t, out in enumerate((q_o, k_o, v_o)):
        out[...] = dot_nt(na_o[...], w[t]).astype(BF)
    scale = 1.0 / math.sqrt(HD)
    for p in range(3):
        scores = [
            split_dot(q_o[places[p]].astype(F32) * k_o[places[s]].astype(F32), table[...]) * scale
            for s in range(p + 1)
        ]
        top = scores[0]
        for x in scores[1:]:
            top = jnp.maximum(top, x)
        ex = [jnp.exp(x - top) for x in scores]
        total = ex[0]
        for x in ex[1:]:
            total = total + x
        mixed = None
        for s in range(p + 1):
            prob = ex[s] / total
            pr_o[PAIRS.index((p, s))] = prob
            term = dot_nt(prob.astype(BF), table[...]) * v_o[places[s]].astype(F32)
            mixed = term if mixed is None else mixed + term
        mix_o[places[p]] = mixed.astype(BF)
    for p in places:
        mid = s_o[p] + dot_nn(mix_o[p], w[3])
        mid_o[p] = mid
        nb_o[p] = (mid * rsq(mid) * gb[...]).astype(BF)


def token_back_kernel(ids, g, gnb, mid, s_in, ga, gb, q, k, v, mix, pr, table, own_qkv, own_out, *rest):
    bufs, (ml_o, left_o, gf_o, da_o, db_o, w, gm, gx, sem) = rest[:8], rest[8:]
    copies = attn_weight_copies(ids, own_qkv, own_out, bufs, w, sem)
    for c in copies:
        c.start()
    frames, feats = gf_o.shape[0], q.shape[1]
    places = [pl.ds(p * frames, frames) for p in range(3)]
    lanes = [pl.ds(t * feats, feats) for t in range(4)]
    total = None
    for p in places:
        dx, dg = norm_back(gnb[p], mid[p], gb[...])
        grad = g[p].astype(F32) + dx
        gm[p] = grad
        ml_o[p] = grad.astype(BF)
        row = jnp.sum(dg, axis=0, keepdims=True)
        total = row if total is None else total + row
    db_o[...] = total
    left_o[:, lanes[3]] = mix[...]
    for c in copies:
        c.wait()
    gx[...] = dot_nt(ml_o[...], w[3]).astype(BF)
    scale = 1.0 / math.sqrt(HD)
    kg, vg = {}, {}
    for p in range(3):
        gp = [
            split_dot(gx[places[p]].astype(F32) * v[places[s]].astype(F32), table[...])
            for s in range(p + 1)
        ]
        probs = [pr[PAIRS.index((p, s))] for s in range(p + 1)]
        delta = probs[0] * gp[0]
        for s in range(1, p + 1):
            delta = delta + probs[s] * gp[s]
        query = None
        for s in range(p + 1):
            wide = dot_nt((probs[s] * (gp[s] - delta)).astype(BF), table[...])
            term = wide * k[places[s]].astype(F32)
            query = term if query is None else query + term
            key = wide * q[places[p]].astype(F32) * scale
            value = dot_nt(probs[s].astype(BF), table[...]) * gx[places[p]].astype(F32)
            if p == s:
                kg[s], vg[s] = key, value
            else:
                kg[s], vg[s] = kg[s] + key, vg[s] + value
        left_o[places[p], lanes[0]] = (query * scale).astype(BF)
    for s in range(3):
        left_o[places[s], lanes[1]] = kg[s].astype(BF)
        left_o[places[s], lanes[2]] = vg[s].astype(BF)
    gna = dot_nn(left_o[:, lanes[0]], w[0]) + dot_nn(left_o[:, lanes[1]], w[1]) + dot_nn(left_o[:, lanes[2]], w[2])
    total = out = None
    for i, p in enumerate(places):
        dx, dg = norm_back(gna[i * frames : (i + 1) * frames], s_in[p], ga[...])
        grad = gm[p] + dx
        row = jnp.sum(dg, axis=0, keepdims=True)
        total = row if total is None else total + row
        out = grad if out is None else out + grad
    da_o[...] = total
    gf_o[...] = out


GELU_S = math.sqrt(2.0 / math.pi)


def gelu_both(u):
    u2 = u * u
    t = jnp.tanh(GELU_S * (u + 0.044715 * (u2 * u)))
    h = 0.5 * (1.0 + t)
    return u * h, h + 0.5 * u * (1.0 - t * t) * (GELU_S * (1.0 + 3.0 * 0.044715 * u2))


def token_ff_kernel(step, ids, nb, g, mid, valid, bias, bdown, own_up, own_down, *rest):
    bufs, (out_o, gnb_o, left_o, gb_o, wuo, wdo, w, acc, sem) = rest[:8], rest[8:]
    n, frames = own_down.shape[0], valid.shape[0]
    own = [
        pltpu.make_async_copy(own_up, wuo, sem.at[0]),
        pltpu.make_async_copy(own_down, wdo, sem.at[1]),
    ]
    copies = weight_copies(ids, n // INNER, bufs, w, sem, 2)
    z = ids[1]
    for c in own + copies:
        c.start()
    acc[...] = jnp.zeros_like(acc)
    gnb_o[...] = jnp.zeros_like(gnb_o)

    def middle(at, size, pre, back):
        cols = pl.ds(at, size)
        h, dh = gelu_both(pre + bias[:, cols])
        h = h.astype(BF)
        gp = (dh * back).astype(BF)
        left_o[:, cols] = h
        left_o[:, pl.ds(pl.multiple_of(4 * n + at, 128), size)] = gp
        gb_o[:, cols] = jnp.sum(gp.astype(F32), axis=0, keepdims=True)
        return h, gp

    for c in own:
        c.wait()
    own_step = n // 2

    def own_block(j, carry):
        cols = pl.ds(pl.multiple_of(j * own_step, own_step), own_step)
        pre = dot_nn(nb[...], wuo[:, cols])
        back = dot_nt(g[...], wdo[cols, :])
        h, gp = middle(pl.multiple_of(z * n + j * own_step, own_step), own_step, pre, back)
        acc[...] += dot_nn(h, wdo[cols, :])
        gnb_o[...] += dot_nt(gp, wuo[:, cols])
        return carry

    lax.fori_loop(0, n // own_step, own_block, 0)
    for c in copies:
        c.wait()

    def block(j, carry):
        at = pl.multiple_of(j * step + jnp.where(j * step >= z * n, n, 0), step)
        rows = pl.ds(at, step)
        pre = dot_nt(nb[...], w[0, rows, :])
        back = dot_nt(g[...], w[1, rows, :])
        h, gp = middle(at, step, pre, back)
        acc[...] += dot_nn(h, w[1, rows, :])
        gnb_o[...] += dot_nn(gp, w[0, rows, :])
        return carry

    lax.fori_loop(0, 3 * n // step, block, 0)
    out = None
    for p in range(3):
        rows = pl.ds(p * frames, frames)
        val = jnp.where(valid[...] > 0.0, acc[rows] + mid[rows] + bdown[...], 0.0).astype(BF)
        term = dot_nn(place_put(p, frames), val)
        out = term if out is None else out + term
    out_o[...] = out.astype(BF)


def lay_right(dst, row, col, right, core, block):
    for i in range(INNER // 2):
        at = pl.multiple_of((2 * i + core) * block, block)
        dst[pl.ds(row + i * block, block), pl.ds(col, right.shape[1])] = right[pl.ds(at, block), :]


def pair_grad_kernel(new, ids, lm, lt, rm, rt, out, tmp, am):
    @pl.when(new(pl.program_id(0)))
    def _():
        for i, src in enumerate((rm, rt)):
            tmp[...] = jnp.transpose(src[0])
            lay_right(am, 0, i * src.shape[1], tmp, ids[0] & 1, src.shape[2] // INNER)

    out[...] = dot_nn(am[...], jnp.concatenate([lm[...], lt[...]], axis=0)).astype(BF)


def frame_grad_kernel(second, ids, left, right0, right1, same, cross, tmp, am):
    d = right0.shape[1]
    for first, right in ((0, right0), (second, right1)):

        @pl.when(pl.program_id(0) == first)
        def _(right=right):
            tmp[...] = jnp.transpose(right[...])
            for i in range(2):
                lay_right(am, i * (d // 2), 0, tmp, (ids[0] & 1) ^ i, d // INNER)

    total = dot_nn(am[...], left[...])
    same[...] = total[: d // 2].astype(BF)
    cross[...] = total[d // 2 :].astype(BF)


VMEM_LIMIT = 60 * 1024 * 1024


def arr(shape, dtype):
    return jax.ShapeDtypeStruct(shape, dtype)


def cost(flops, ins, outs):
    size = sum(a.size * a.dtype.itemsize for a in ins) + sum(
        math.prod(o.shape) * o.dtype.itemsize for o in outs
    )
    return pl.CostEstimate(flops=flops, bytes_accessed=size, transcendentals=0)


def call(kernel, outs, ins, scratch, any_from, flops, smem=0):
    def space(i):
        return pltpu.SMEM if i < smem else pltpu.VMEM if i < any_from else pl.ANY

    return pl.pallas_call(
        kernel,
        out_shape=outs,
        in_specs=[pl.BlockSpec(memory_space=space(i)) for i in range(len(ins))],
        out_specs=[pl.BlockSpec(memory_space=pltpu.VMEM)] * len(outs),
        scratch_shapes=scratch,
        compiler_params=pltpu.CompilerParams(vmem_limit_bytes=VMEM_LIMIT),
        cost_estimate=cost(flops, ins, outs),
    )(*ins)


def frame_out(ids, mixed, frames, gain, own, bufs):
    rows, d = frames.shape
    ins = [ids, *mixed, frames, gain, own, *bufs]
    scratch = [pltpu.VMEM((4, *own.shape), BF), pltpu.SemaphoreType.DMA((FRAME_OUT_COPIES,))]
    outs = [arr((rows, d), F32), arr((rows, d), BF)]
    return call(frame_out_kernel, outs, ins, scratch, 7, 8 * rows * own.size, smem=1)


def frame_mid(ids, gnb, mid, grad_out, gain, own, bufs):
    rows, d = mid.shape
    ins = [ids, gnb, mid, grad_out, gain, own, *bufs]
    scratch = [pltpu.VMEM((4, *own.shape), BF), pltpu.SemaphoreType.DMA((FRAME_OUT_COPIES,))]
    outs = [arr((rows, d), F32), arr((rows, d), BF), arr((1, d), F32), arr((4, rows, own.shape[0]), BF)]
    return call(frame_mid_kernel, outs, ins, scratch, 5, 8 * rows * own.size, smem=1)


def token_attn(ids, fo, emb, cot, valid, ga, gb, table, own_qkv, own_out, bufs):
    frames, d = fo.shape
    rows, feats = 3 * frames, table.shape[0]
    outs = (
        [arr((rows, d), F32), arr((rows, d), BF), arr((rows, d), BF)]
        + [arr((rows, feats), BF)] * 4
        + [arr((rows, d), F32), arr((rows, d), BF), arr((len(PAIRS), frames, table.shape[1]), F32)]
    )
    return call(
        token_attn_kernel,
        outs,
        [ids, fo, emb, cot, valid, ga, gb, table, own_qkv, own_out, *bufs],
        [pltpu.VMEM((4, feats, d), BF), pltpu.SemaphoreType.DMA((2 + COPIES,))],
        8,
        8 * rows * feats * d,
        smem=1,
    )


def token_back(ids, g, gnb, mid, s, ga, gb, q, k, v, mix, pr, table, own_qkv, own_out, bufs):
    rows, d = s.shape
    frames, feats = rows // 3, table.shape[0]
    outs = [
        arr((rows, d), BF),
        arr((rows, 4 * feats), BF),
        arr((frames, d), F32),
        arr((1, d), F32),
        arr((1, d), F32),
    ]
    return call(
        token_back_kernel,
        outs,
        [ids, g, gnb, mid, s, ga, gb, q, k, v, mix, pr, table, own_qkv, own_out, *bufs],
        [
            pltpu.VMEM((4, feats, d), BF),
            pltpu.VMEM((rows, d), F32),
            pltpu.VMEM((rows, feats), BF),
            pltpu.SemaphoreType.DMA((2 + COPIES,)),
        ],
        13,
        8 * rows * feats * d,
        smem=1,
    )


def token_ff(ids, nb, g, mid, valid, bias, bdown, own_up, own_down, bufs):
    rows, d = nb.shape
    n = own_down.shape[0]
    outs = [
        arr((rows, d), BF),
        arr((rows, d), F32),
        arr((rows, 8 * n), BF),
        arr((1, 4 * n), F32),
    ]
    return call(
        functools.partial(token_ff_kernel, 512),
        outs,
        [ids, nb, g, mid, valid, bias, bdown, own_up, own_down, *bufs],
        [
            pltpu.VMEM((d, n), BF),
            pltpu.VMEM((n, d), BF),
            pltpu.VMEM((2, 4 * n, d), BF),
            pltpu.VMEM((rows, d), F32),
            pltpu.SemaphoreType.DMA((2 + COPIES,)),
        ],
        7,
        32 * rows * n * d,
        smem=1,
    )


def smem_spec():
    return pl.BlockSpec(memory_space=pltpu.SMEM)


def pair_grad(ids, left, left_other, rights, rights_other, split):
    rows, units = left.shape
    d = rights.shape[2]
    step = d
    at = split // step
    pick = lambda j: jnp.where(j < at, 0, 1)
    outs = [arr((d // 2, units), BF)]
    [out] = pl.pallas_call(
        functools.partial(pair_grad_kernel, lambda j: (j == 0) | (j == at)),
        grid=(units // step,),
        in_specs=[smem_spec()]
        + [pl.BlockSpec((rows, step), lambda j: (0, j))] * 2
        + [pl.BlockSpec((1, rows, d), lambda j: (pick(j), 0, 0))] * 2,
        out_specs=[pl.BlockSpec((d // 2, step), lambda j: (0, j))],
        out_shape=outs,
        scratch_shapes=[pltpu.VMEM((d, rows), BF), pltpu.VMEM((d // 2, 2 * rows), BF)],
        compiler_params=pltpu.CompilerParams(vmem_limit_bytes=VMEM_LIMIT),
        cost_estimate=cost(2 * rows * units * d, [left, left_other, rights, rights_other], outs),
    )(ids, left, left_other, rights, rights_other)
    return out


def frame_grad(ids, left, rights, split):
    rows, units = left.shape
    d = rights[0].shape[1]
    step = units // 4
    outs = [arr((d // 2, units), BF)] * 2
    ins = [left, *rights]
    return pl.pallas_call(
        functools.partial(frame_grad_kernel, split // step),
        grid=(4,),
        in_specs=[smem_spec(), pl.BlockSpec((rows, step), lambda j: (0, j))]
        + [pl.BlockSpec((rows, d), lambda j: (0, 0))] * 2,
        out_specs=[pl.BlockSpec((d // 2, step), lambda j: (0, j))] * 2,
        out_shape=outs,
        scratch_shapes=[pltpu.VMEM((d, rows), BF)] * 2,
        compiler_params=pltpu.CompilerParams(vmem_limit_bytes=VMEM_LIMIT),
        cost_estimate=cost(2 * rows * units * d, ins, outs),
    )(ids, *ins)


def segments(lengths, whole_rows):
    count = lengths.shape[1]
    order = jnp.arange(count, dtype=jnp.int32)
    item_ends = jnp.sum(
        jnp.where(order[None, :] <= order[:, None], lengths[0][None, :], 0), axis=1, dtype=jnp.int32
    )
    positions = jnp.arange(whole_rows, dtype=jnp.int32)
    segment = jnp.sum(
        (positions[:, None] >= item_ends[None, :]).astype(jnp.int32), axis=1, dtype=jnp.int32
    )
    is_valid = positions < jnp.sum(lengths[0], dtype=jnp.int32)
    segment = jnp.where(is_valid, segment, positions + count)
    return (segment, is_valid)


def frame_allowed(segment):
    positions = jnp.arange(segment.shape[0], dtype=jnp.int32)
    return (positions[None, :] <= positions[:, None]) & (segment[None, :] == segment[:, None])


def split_heads(rows):
    return rows.reshape(rows.shape[0], rows.shape[1] // HD, HD)


def frame_forward(qkv_rows, segment):
    queries, key_rows, value_rows = (split_heads(qkv_rows[t]) for t in range(3))
    raw_scores = jnp.einsum("qhe,khe->hqk", queries, key_rows, preferred_element_type=F32) * (
        1.0 / math.sqrt(HD)
    )
    scores = jnp.where(frame_allowed(segment)[None], raw_scores, -1e30)
    top_score = jnp.max(scores, axis=-1, keepdims=True)
    exp_scores = jnp.exp(scores - top_score)
    exp_total = jnp.sum(exp_scores, axis=-1, keepdims=True)
    attn_probs = (exp_scores / exp_total).astype(BF)
    mixed = jnp.einsum("hqk,khe->qhe", attn_probs, value_rows, preferred_element_type=F32)
    log_total = top_score[:, :, 0] + jnp.log(exp_total[:, :, 0])
    return (mixed.astype(BF).reshape(qkv_rows.shape[1], -1), log_total)


def frame_backward(qkv_rows, log_total, grad_mixed, segment):
    queries, key_rows, value_rows = (split_heads(qkv_rows[t]) for t in range(3))
    grad_heads = split_heads(grad_mixed)
    scale = 1.0 / math.sqrt(HD)
    raw_scores = jnp.einsum("qhe,khe->hqk", queries, key_rows, preferred_element_type=F32) * scale
    scores = jnp.where(frame_allowed(segment)[None], raw_scores, -1e30)
    attn_probs = jnp.exp(scores - log_total[:, :, None])
    value_grad = jnp.einsum(
        "hqk,qhe->khe", attn_probs.astype(BF), grad_heads, preferred_element_type=F32
    )
    grad_probs = jnp.einsum("qhe,khe->hqk", grad_heads, value_rows, preferred_element_type=F32)
    row_delta = jnp.sum(attn_probs * grad_probs, axis=-1, keepdims=True)
    grad_scores = (attn_probs * (grad_probs - row_delta)).astype(BF)
    query_grad = jnp.einsum("hqk,khe->qhe", grad_scores, key_rows, preferred_element_type=F32) * scale
    key_grad = jnp.einsum("hqk,qhe->khe", grad_scores, queries, preferred_element_type=F32) * scale
    rows = qkv_rows.shape[1]
    return [g.reshape(rows, -1).astype(BF) for g in (query_grad, key_grad, value_grad)]


def head_table(features):
    at = jnp.arange(features, dtype=jnp.int32)
    return ((at // HD)[:, None] == jnp.arange(128, dtype=jnp.int32)[None, :]).astype(BF)


def shards(frames, codes_embed, lengths, cotangent, *params):
    gain_a, w_qkv, w_out, gain_b, w_up, b_up, w_down, b_down = params[:8]
    t_gain_a, t_qkv, t_out, t_gain_b, t_up, t_bup, t_down, t_bdown = params[8:]
    dp, parts = lax.axis_size("dp"), lax.axis_size("mp")
    z = lax.axis_index("mp")
    ids = jnp.stack([my_place(), z]).astype(jnp.int32)
    local, d = frames.shape
    n_attn, n_ff = w_out.shape[0], w_down.shape[0]
    block = d // INNER
    segment, is_valid = segments(lengths, local * parts)
    valid = lax.dynamic_slice_in_dim(is_valid, z * local, local, 0).astype(F32)[:, None]

    stream = frames.astype(F32)
    gain_a32, gain_b32 = gain_a.astype(F32), gain_b.astype(F32)
    normed_a = normalize(stream, gain_a32).astype(BF)
    gathered_a = gather_rows(normed_a)

    attn_w = Gather(jnp.concatenate([own_cols(t_qkv), own_rows(t_out)[None]], axis=0))
    ff_w = Gather(jnp.stack([own_cols(t_up), own_rows(t_down)]))
    out_w = Gather(own_rows(w_out)[None])
    out_w.shards_straight()
    out_w.plane_first()
    out_w.plane_last()
    out_w.cores()
    attn_w.shards()
    gathered_a = after(gathered_a, *out_w.held, *attn_w.held)

    qkv_rows = jnp.einsum("rd,tde->tre", gathered_a, w_qkv, preferred_element_type=F32).astype(BF)
    mixed_rows, log_total = frame_forward(qkv_rows, segment)
    by_rows = [
        lax.dynamic_slice_in_dim(mixed_rows, (z ^ r) * local, local, 0) for r in range(parts)
    ]
    mixed_own = [by_rows[0]] + [swap_mp(by_rows[r], r) for r in range(1, parts)]

    attn_w.plane_first(mixed_rows)
    middle, normed_b = frame_out(ids, mixed_own, frames, gain_b32[None], w_out, out_w.held)
    ff_w.shards(normed_b)
    gathered_b = gather_rows(normed_b)

    attn_w.plane_last(normed_b)
    ff_w.plane_first(normed_b)
    gathered_b = after(gathered_b, *attn_w.marks(), *ff_w.marks())

    hidden_pre = dot_nn(gathered_b, w_up) + b_up.astype(F32)
    hidden = activate(hidden_pre).astype(BF)
    part_b = dot_nn(hidden, w_down).astype(BF)
    branch_b = scatter_rows(part_b)

    attn_w.cores(part_b)
    ff_w.plane_last(part_b)
    f_result = middle + after(branch_b, *attn_w.held, *ff_w.marks()) + b_down.astype(F32)

    t_bias = jnp.concatenate(gather_all(t_bup)).astype(F32)[None]
    own_qkv = jnp.transpose(t_qkv, (0, 2, 1))
    table = head_table(n_attn * parts)
    tga, tgb = t_gain_a.astype(F32)[None], t_gain_b.astype(F32)[None]

    attn_bufs = attn_w.held
    t_stream, g_low, t_na, q, k, v, mixed, t_middle, t_nb, probs = token_attn(
        ids, f_result, codes_embed, cotangent, valid, tga, tgb, table, own_qkv, t_out, attn_bufs
    )
    ff_w.cores()
    output, t_gnb, t_left, t_gbup = token_ff(
        ids, t_nb, g_low, t_middle, valid, t_bias, t_bdown.astype(F32)[None], t_up, t_down, ff_w.held
    )
    rights = jnp.stack([d_order(g_low), d_order(t_nb)])
    rights_other = swap_dp(rights, 1)
    left_other = swap_dp(t_left, 1)
    m_low, a_left, grad_frame, t_da, t_db = token_back(
        ids, g_low, t_gnb, t_middle, t_stream, tga, tgb, q, k, v, mixed, probs, table, own_qkv, t_out, attn_bufs
    )
    t_dbd = jnp.sum(g_low.astype(F32), axis=0)

    ff_grad = pair_grad(ids, after(t_left, grad_frame), left_other, rights, rights_other, 4 * n_ff)
    ff_sum = scatter_plane(ff_grad)
    grad_low = grad_frame.astype(BF)
    gathered_down = gather_rows_p(grad_low)
    a_rights = jnp.stack([d_order(t_na), d_order(m_low)])
    a_rights_other = swap_dp(a_rights, 1)
    a_other = swap_dp(a_left, 1)
    gathered_down = after(gathered_down, ff_grad)
    grad_hidden = dot_nt(gathered_down, w_down)
    grad_pre = jax.vjp(activate, hidden_pre)[1](grad_hidden)[0].astype(BF)
    part_c = dot_nt(grad_pre, w_up).astype(BF)
    grad_nb = shards_total(*scatter_rows_p(part_c))

    attn_grad = pair_grad(ids, after(a_left, part_c), a_other, a_rights, a_rights_other, 3 * n_attn * parts)
    f_left = jnp.concatenate([hidden, grad_pre], axis=1)
    ff_same, ff_cross = frame_grad(
        ids, after(f_left, part_c), [d_order(gathered_down), d_order(gathered_b)], n_ff
    )
    ff_cross = swap_dp(ff_cross, 1)
    grad_nb = after(grad_nb, attn_grad, ff_same)
    grad_middle, mid_low, f_db, pieces = frame_mid(
        ids, grad_nb, middle, grad_frame, gain_b32[None], w_out, out_w.held
    )
    gathered_mid = gather_rows_p(mid_low)
    grad_mixed = jnp.concatenate(
        by_xor_mp([pieces[0]] + [swap_mp(pieces[r], r) for r in range(1, parts)]), axis=0
    )
    grad_qkv = jnp.concatenate(frame_backward(qkv_rows, log_total, grad_mixed, segment), axis=1)
    w_all = jnp.concatenate([w_qkv[0], w_qkv[1], w_qkv[2]], axis=1)
    part_d32 = dot_nt(grad_qkv, w_all)
    part_d = after(part_d32.astype(BF), ff_sum, gathered_mid)
    attn_sum = scatter_plane(after(attn_grad, grad_mixed))
    attn_same, attn_cross = frame_grad(
        ids,
        jnp.concatenate([grad_qkv, mixed_rows], axis=1),
        [d_order(gathered_a), d_order(gathered_mid)],
        3 * n_attn,
    )
    attn_cross = swap_dp(attn_cross, 1)
    part_d = after(part_d, attn_same)
    f_ff_value = (ff_same.astype(F32) + ff_cross.astype(F32)).astype(BF)
    f_attn_value = (attn_same.astype(F32) + attn_cross.astype(F32)).astype(BF)
    na_parts = scatter_rows_p(part_d)
    ff_z = scatter_shards(ff_sum, n_ff, part_d)
    f_ff_parts = plane_parts(f_ff_value, part_d)
    f_attn_parts = plane_parts(f_attn_value, part_d)
    grad_na = shards_total(*na_parts)
    first = jax.vjp(normalize, stream, gain_a32)[1](grad_na)
    frames_grad = grad_middle + first[0]
    attn_z = scatter_shards(after(attn_sum, grad_na), n_attn)
    f_da = jnp.sum(part_d32 * gathered_a.astype(F32), axis=0) / gain_a32

    wide = lax.dynamic_update_slice_in_dim(
        jnp.zeros((parts, n_ff), F32), jnp.sum(grad_pre.astype(F32), axis=0)[None], z, 0
    )

    def by_owner(full):
        return jnp.transpose(full.reshape(dp, parts, -1), (1, 0, 2)).reshape(parts, -1)

    vec = jnp.concatenate(
        [
            jnp.stack([f_da, f_db[0], jnp.sum(grad_frame, axis=0), t_da[0], t_db[0], t_dbd]),
            by_owner(wide),
            by_owner(t_gbup[0]),
        ],
        axis=0,
    )
    vec = d_order(after(vec, part_d))
    vec = jnp.concatenate(by_xor([vec[:, i * block : (i + 1) * block] for i in range(INNER)]), axis=1)
    for bit in (4, 2, 1):
        half = vec.shape[1] // 2
        vec = vec[:, :half] + swap_dp(vec[:, half:], bit)
    vec = outer_sum(vec, 1)
    width = vec.shape[1]
    quarter = width // parts
    rows = by_xor_mp(
        [
            jnp.concatenate(
                [vec[:6, i * quarter : (i + 1) * quarter].reshape(-1), vec[6 + i], vec[6 + parts + i]]
            )
            for i in range(parts)
        ]
    )
    mine = rows[0] + sum(swap_mp(rows[r], r) for r in (1, 2, 3))
    vectors = [mine[i * quarter : (i + 1) * quarter] for i in range(6)]
    f_bup, t_bup_grad = mine[6 * quarter : 6 * quarter + width], mine[6 * quarter + width :]

    f_ff = shards_total(*f_ff_parts, mine)
    f_attn = shards_total(*f_attn_parts, mine)
    t_attn = shards_total(*attn_z, f_ff, f_attn)
    t_ff = shards_total(*ff_z, t_attn)

    def ff_split(total):
        return total[:, :n_ff].T, total[:, n_ff:]

    def attn_split(total):
        rows = total.reshape(block, 4, n_attn)
        return jnp.transpose(rows[:, :3], (1, 0, 2)), total[:, 3 * n_attn :].T

    t_down_grad, t_up_grad = ff_split(t_ff)
    f_down_grad, f_up_grad = ff_split(f_ff)
    f_qkv_grad, f_out_grad = attn_split(f_attn)
    t_qkv_grad, t_out_grad = attn_split(t_attn)

    def owned(qkv_grad, out_grad, up_grad, down_grad):
        return (
            outer_sum(qkv_grad, 1),
            outer_sum(out_grad, 1),
            outer_sum(up_grad, 0),
            outer_sum(down_grad, 1),
        )

    f = owned(f_qkv_grad, f_out_grad, f_up_grad, f_down_grad)
    t = owned(t_qkv_grad, t_out_grad, t_up_grad, t_down_grad)
    return (
        output,
        frames_grad,
        vectors[0],
        f[0],
        f[1],
        vectors[1],
        f[2],
        f_bup,
        f[3],
        vectors[2],
        vectors[3],
        t[0],
        t[1],
        vectors[4],
        t[2],
        t_bup_grad,
        t[3],
        vectors[5],
    )


def solution(mesh):
    rows = P(("dp", "mp"), None)
    block = (
        P(),
        P(None, None, "mp"),
        P("mp", None),
        P(),
        P(None, "mp"),
        P("mp"),
        P("mp", None),
        P(),
    )
    vec = P(("dp", "mp"))
    block_out = (
        vec,
        P(None, "dp", "mp"),
        P("mp", "dp"),
        vec,
        P("dp", "mp"),
        vec,
        P("mp", "dp"),
        vec,
    )
    return jax.shard_map(
        shards,
        mesh=mesh,
        in_specs=(rows, rows, P("dp", None), rows) + block + block,
        out_specs=(rows, rows) + block_out + block_out,
        check_vma=False,
    )
```
